32 devices in a mesh: layer: 2 (over x), gx: 4 (over z), gy: 4 (over y, core).
Axes of the slice: x: 2, y: 2, z: 4, core: 2. Of those that a mesh axis runs over, the one named last changes fastest.
Arguments:
- pressure: float32 [16, 256, 1024], P('layer', 'gx', 'gy'), may hold values from -6 to 6
- source: float32 [16, 256, 1024], P('layer', 'gx', 'gy'), may hold values from -6 to 6
- perm_x: float32 [16, 256, 1024], P('layer', 'gx', 'gy'), may hold values from 0.05 to 0.5
- perm_y: float32 [16, 256, 1024], P('layer', 'gx', 'gy'), may hold values from 0.05 to 0.5
- line_inverse: float32 [2, 8, 8, 256, 1024], P('layer', None, None, 'gx', 'gy'), may hold values from -0.98 to 1.2
- robin_below: float32 [2, 256, 1024], P('layer', 'gx', 'gy'), may hold values from -6 to 6
- tile_count: int32 [2, 16], P('layer', ('gx', 'gy')), may hold values from 1 to 48, 256 in all within a row
- perf_owner: int32 [2, 768, 1], P('layer', ('gx', 'gy')), may hold values from 0 to 15; in each aligned block of 48 rows (0 to 47, 48 to 95, ..., all dimensions but the last counted through in order) at most 3 rows name the same one
- perf_well: int32 [2, 768], P('layer', ('gx', 'gy')), may hold values from 0 to 7
- perf_column: int32 [2, 768], P('layer', ('gx', 'gy')), may hold values from 0 to 16383
- perf_index: float32 [2, 768, 8], P('layer', ('gx', 'gy')), may hold values from 0.2 to 2
- well_rate: float32 [2, 128], P('layer', ('gx', 'gy')), may hold values from -8 to 8
Outputs:
- pressure_out: float32 [16, 256, 1024], P('layer', 'gx', 'gy')
- perf_flow: float32 [2, 768, 8], P('layer', ('gx', 'gy'))
The draws below stay inside these ranges and needn't reach their ends.
Inputs may be any that keep to these rules, and one draw needn't show every extreme that they name: `tile_count`: live slots of a tile are its first ones; some tile of every group has all 48 live. `perf_owner`: among the 48 slots of one tile at most 3 name one owner.
All inputs are finite; a program needn't handle non-finite values.
Results may differ from the reference program's by a relative error of at most 0.00018.
Values sent between devices are 32-bit elements; how exact they have to be, the bound alone decides.
A program may use at most 64 MiB of HBM per device.

```python
import math
import jax
import jax.numpy as jnp
import numpy as np
from jax import lax

LZ = 8
CX = 64
CY = 256
ITERS = 2
SLOTS = 48
WO = 8
GROUPS = 2
TILES = 16
CAP = 3
NZ = 16
NX = 256
NY = 1024
N_GY = 4


def draw_line_inverse(key, part):
    keys = jax.random.split(key, 9)
    shape = (GROUPS, LZ, LZ, NX, NY)
    layer_sheet = (GROUPS, NX, NY)
    spread = jax.random.uniform(keys[0], shape, jnp.float32, -0.25, 0.25)
    diag_vals = jnp.exp(jax.random.uniform(keys[1], (GROUPS, LZ, NX, NY), jnp.float32, jnp.log(0.3), jnp.log(1.2)))
    eye_mask = (jnp.arange(LZ)[:, None] == jnp.arange(LZ)[None, :]).astype(jnp.float32)[None, :, :, None, None]
    matrix = spread * (1.0 - eye_mask) + eye_mask * diag_vals[:, :, None, :, :]
    slow_low = 0.2 ** (1.0 / max(GROUPS - 1, 1))
    slow_share = 0.5
    corners = []
    for which in range(2):
        gradual_indicator = jax.random.bernoulli(keys[2 + 3 * which], slow_share, layer_sheet)
        subset_part = jax.random.split(keys[3 + 3 * which], 3)
        gradual_amplitude = jax.random.uniform(subset_part[0], layer_sheet, jnp.float32, slow_low, 0.98)
        rapid_amplitude = jax.random.uniform(subset_part[1], layer_sheet, jnp.float32, 0.15, 0.45)
        spike_indicator = jax.random.bernoulli(subset_part[2], 0.15, layer_sheet)
        sign_flag = jax.random.bernoulli(keys[4 + 3 * which], 0.8, layer_sheet)
        amplitude_level = jnp.where(gradual_indicator, gradual_amplitude, rapid_amplitude) * jnp.where(spike_indicator, 0.5, 1.0)
        corners.append(amplitude_level * jnp.where(sign_flag, 1.0, -1.0))
    matrix = matrix.at[:, LZ - 1, 0].set(corners[0])
    matrix = matrix.at[:, 0, LZ - 1].set(corners[1])
    return matrix.astype(jnp.float32)


def plant(values, rng, smallest, top_value):
    extent = values.shape
    spot = [jax.random.randint(jax.random.fold_in(rng, axis), (), 0, extent[axis]) for axis in range(len(extent))]
    values = values.at[tuple(spot)].set(smallest)
    longest = extent.index(max(extent))
    spot[longest] = (spot[longest] + 1) % extent[longest]
    return values.at[tuple(spot)].set(top_value)


def levels(own_key, dims, shards, smallest, high):
    def one(position, blocks):
        steps = jax.random.uniform(jax.random.fold_in(jax.random.fold_in(own_key, 6), position), (blocks,), jnp.float32, smallest / len(shards), high / len(shards))
        return jnp.repeat(jnp.exp(steps), dims[position] // blocks).reshape((-1,) + (1,) * (len(dims) - position - 1))

    factor_of = one(*shards[0])
    for cut in shards[1:]:
        factor_of = factor_of * one(*cut)
    return factor_of


def length_profile(count, total, most, slope):
    portions = [(1 << 20) // math.isqrt(standing ** slope) + 1 for standing in range(2, count + 1)]
    rest, given = total - most - (count - 1), [1] * (count - 1)
    while rest > 0:
        free = [i for i in range(count - 1) if given[i] < most]
        mass, budget = sum([portions[i] for i in free]), rest
        for i in free:
            addition = min(most - given[i], max(1, budget * portions[i] // mass), rest)
            given[i] = given[i] + addition
            rest = rest - addition
    return np.array([most] + given)


def ragged_sizes(key, count, total, reach, slope):
    if count == 2:
        one = jax.random.randint(key, (), max(1, total - reach), min(reach, total - 1) + 1)
        return jnp.stack([one, total - one])
    sizes = jnp.asarray(length_profile(count, total, reach, slope), jnp.int32)
    twos = (count - 1) // 2
    giver, taker = sizes[1:1 + 2 * twos:2], sizes[2:2 + 2 * twos:2]
    room = jnp.minimum(giver - 1, reach - taker)
    moved = jax.random.randint(jax.random.fold_in(key, 1), (twos,), 0, 1 << 20) % (room + 1)
    sizes = sizes.at[1:1 + 2 * twos:2].set(giver - moved).at[2:2 + 2 * twos:2].set(taker + moved)
    return sizes[jax.random.permutation(jax.random.fold_in(key, 2), count)]


def assign_block(rng, own, number, rows, amount, top, bound, lean):
    order = jax.random.permutation(rng, amount)
    heavy_load, usual = portions_of(amount, rows * top, bound, lean, True), portions_of(amount, rows * top, bound, lean, False)
    places = jnp.arange(amount)

    def named(sizes, offset_by):
        used = int((sizes > 0).sum())
        fixed = max(1, used // 4)
        moved = fixed + (places - fixed + offset_by * (used - fixed)) % max(1, amount - fixed)
        return jnp.zeros((amount,), jnp.int32).at[order[jnp.where(places < fixed, places, moved)]].set(jnp.asarray(sizes, jnp.int32))

    sizes = jnp.where(number % 4 == 0, named(heavy_load, number // 4), named(usual, number - number // 4 - 1))
    mixed = jax.random.permutation(jax.random.fold_in(own, 3), amount)
    giver, sink = mixed[0:amount // 2 * 2:2], mixed[1:amount // 2 * 2:2]
    slack = jnp.minimum(sizes[giver] - 1, bound - sizes[sink]) // 2
    slack = jnp.where((giver == order[0]) | (sink == order[0]) | (sizes[sink] == 0), 0, jnp.maximum(slack, 0))
    moved = jax.random.randint(jax.random.fold_in(own, 4), (amount // 2,), 0, 1 << 20) % (slack + 1)
    sizes = sizes.at[giver].add(-moved).at[sink].add(moved)
    labels = jnp.searchsorted(jnp.cumsum(sizes), jnp.arange(rows * top), side="right").astype(jnp.int32)
    grid = labels.reshape(top, rows).T
    grid = grid[jax.random.permutation(jax.random.fold_in(own, 1), rows)]
    offset_by = jax.random.randint(jax.random.fold_in(own, 2), (rows, 1), 0, top)
    return jnp.take_along_axis(grid, (jnp.arange(top)[None, :] + offset_by) % top, axis=1)


def portions_of(count, total, most, skew, full):
    loads = [(1 << 20) // math.isqrt(standing ** skew) + 1 for standing in range(1, count + 1)]
    largest = most if full else min(most, max(-(-total // count), total * loads[0] // sum(loads)))
    least = 1 if total - largest >= count - 1 else 0
    given, spare = [largest] + [least] * (count - 1), total - largest - least * (count - 1)
    while spare > 0:
        movable = [i for i in range(1, count) if given[i] < largest] or [i for i in range(1, count) if given[i] < most]
        pool, remaining = sum([loads[i] for i in movable]), spare
        for i in movable:
            addition = min(most - given[i], max(1, remaining * loads[i] // pool), spare)
            given[i] = given[i] + addition
            spare = spare - addition
    return np.array(given)


def centred(stream_key, shape, width, limit, shards=(), kind=jnp.bfloat16):
    entries = width * jax.random.normal(stream_key, shape, jnp.float32)
    if shards:
        entries = entries * levels(stream_key, shape, shards, -0.22, 0.18)
    return jnp.clip(entries, -limit, limit).astype(kind)


def setup_inputs(seed: int = 0) -> dict:
    key_list = jax.random.split(jax.random.key(seed), 13)
    pressure = centred(key_list[0], (NZ, NX, NY), 1.0, 6.0, ((0, 2), (1, 4), (2, 4)), jnp.float32)
    source = centred(key_list[1], (NZ, NX, NY), 1.0, 6.0, ((0, 2), (1, 4), (2, 4)), jnp.float32)
    perm_x = jnp.clip(jnp.exp(math.log(0.5) - 2.3025851 * jax.random.uniform(key_list[2], (NZ, NX, NY), jnp.float32) ** levels(key_list[2], (NZ, NX, NY), ((0, 2), (1, 4), (2, 4)), -0.2, 0.2)), 0.05, 0.5)
    perm_y = jnp.clip(jnp.exp(math.log(0.5) - 2.3025851 * jax.random.uniform(key_list[3], (NZ, NX, NY), jnp.float32) ** levels(key_list[3], (NZ, NX, NY), ((0, 2), (1, 4), (2, 4)), -0.2, 0.2)), 0.05, 0.5)
    line_inverse = draw_line_inverse(jax.random.fold_in(key_list[12], 71), 0)
    robin_below = centred(key_list[5], (GROUPS, NX, NY), 1.0, 6.0, ((0, 2), (1, 4), (2, 4)), jnp.float32)
    tile_count = jax.vmap(lambda own: ragged_sizes(own, TILES, TILES * SLOTS // 3, SLOTS, 2))(jax.random.split(key_list[6], GROUPS)).reshape((GROUPS, TILES)).astype(jnp.int32)
    perf_owner_keys = jax.random.split(jax.random.fold_in(key_list[7], 1), GROUPS * (TILES * SLOTS) // SLOTS)
    perf_owner_turns = jax.random.permutation(jax.random.fold_in(key_list[7], 3), GROUPS * (TILES * SLOTS) // SLOTS)
    perf_owner = jax.vmap(lambda own, number: assign_block(jax.random.fold_in(key_list[7], 2), own, number, SLOTS, TILES, 1, CAP, 2))(perf_owner_keys, perf_owner_turns).reshape((GROUPS, TILES * SLOTS, 1))
    perf_well = plant(jax.random.randint(key_list[8], (GROUPS, TILES * SLOTS), 0, WO), jax.random.fold_in(key_list[8], 1), 0, WO - 1).astype(jnp.int32)
    perf_column = plant(jax.random.randint(key_list[9], (GROUPS, TILES * SLOTS), 0, CX * CY), jax.random.fold_in(key_list[9], 1), 0, (CX * CY) - 1).astype(jnp.int32)
    perf_index = jnp.clip(jnp.exp(math.log(2.0) - 2.3025851 * jax.random.uniform(key_list[10], (GROUPS, TILES * SLOTS, LZ), jnp.float32) ** levels(key_list[10], (GROUPS, TILES * SLOTS, LZ), ((0, 2), (1, 16)), -0.2, 0.2)), 0.2, 2.0)
    well_rate = centred(key_list[11], (GROUPS, TILES * WO), 2.0, 8.0, ((0, 2), (1, 16)), jnp.float32)
    return {"pressure": pressure, "source": source, "perm_x": perm_x, "perm_y": perm_y, "line_inverse": line_inverse, "robin_below": robin_below, "tile_count": tile_count, "perf_owner": perf_owner, "perf_well": perf_well, "perf_column": perf_column, "perf_index": perf_index, "well_rate": well_rate}


HIGHEST_PRECISION = lax.Precision.HIGHEST


def neighbours(padded_field, rock_x, rock_y, perm_x, perm_y):
    east_term = 0.5 * (perm_x + rock_x[:, 2:, 1:-1]) * padded_field[:, 2:, 1:-1]
    west_term = 0.5 * (perm_x + rock_x[:, :-2, 1:-1]) * padded_field[:, :-2, 1:-1]
    north_term = 0.5 * (perm_y + rock_y[:, 1:-1, 2:]) * padded_field[:, 1:-1, 2:]
    south_term = 0.5 * (perm_y + rock_y[:, 1:-1, :-2]) * padded_field[:, 1:-1, :-2]
    return (east_term + west_term) + (north_term + south_term)


def reference(pressure, source, perm_x, perm_y, line_inverse, robin_below, tile_count, perf_owner, perf_well, perf_column, perf_index, well_rate):
    group_total = GROUPS
    tile_total = TILES
    border = ((0, 0), (1, 1), (1, 1))
    rock_x = jnp.pad(perm_x, border)
    rock_y = jnp.pad(perm_y, border)
    live_slot = (jnp.arange(SLOTS).astype(jnp.int32)[None, None, :] < tile_count[:, :, None]).astype(jnp.float32)[..., None]
    tile_ids = jnp.arange(tile_total).astype(jnp.int32)
    column = perf_column.reshape(group_total, tile_total, SLOTS)
    cell_x = (tile_ids // N_GY)[None, :, None] * CX + column // CY
    cell_y = (tile_ids % N_GY)[None, :, None] * CY + column % CY
    full_shape = (group_total, tile_total, SLOTS, LZ)
    layer_ids = jnp.broadcast_to((jnp.arange(group_total)[:, None, None, None] * LZ + jnp.arange(LZ)[None, None, None, :]).astype(jnp.int32), full_shape)
    cell_x4 = jnp.broadcast_to(cell_x[..., None], full_shape)
    cell_y4 = jnp.broadcast_to(cell_y[..., None], full_shape)
    index_rows = perf_index.reshape(full_shape)
    well_ids = perf_owner.reshape(group_total, tile_total, SLOTS) * WO + perf_well.reshape(group_total, tile_total, SLOTS)
    group_ids = jnp.broadcast_to(jnp.arange(group_total).astype(jnp.int32)[:, None, None], well_ids.shape)
    field_now = pressure
    lower_data = robin_below
    slot_flow = jnp.zeros(full_shape, jnp.float32)
    for sweep_step in range(ITERS):
        lateral = neighbours(jnp.pad(field_now, border), rock_x, rock_y, perm_x, perm_y)
        at_slots = field_now[layer_ids, cell_x4, cell_y4]
        index_sum = jnp.zeros((group_total, tile_total * WO), jnp.float32).at[group_ids, well_ids].add(jnp.sum(index_rows * live_slot, axis=-1))
        weighted_sum = jnp.zeros((group_total, tile_total * WO), jnp.float32).at[group_ids, well_ids].add(jnp.sum(index_rows * at_slots * live_slot, axis=-1))
        bottom_hole = (well_rate + weighted_sum) / (index_sum + 1.0)
        slot_flow = index_rows * (bottom_hole[group_ids, well_ids][..., None] - at_slots) * live_slot
        well_term = jnp.zeros_like(field_now).at[layer_ids, cell_x4, cell_y4].add(slot_flow)
        rhs = (source + lateral) + well_term
        blocks = rhs.reshape(group_total, LZ, NX, NY)
        solved = jnp.einsum('gijxy,gjxy->gixy', line_inverse, blocks, precision=HIGHEST_PRECISION)
        upper_trace = jnp.zeros((NX, NY), jnp.float32)
        upper_list = [upper_trace]
        for group_id in range(group_total - 1):
            carried = (solved[group_id, LZ - 1] + line_inverse[group_id, LZ - 1, LZ - 1] * lower_data[group_id]) - lower_data[group_id]
            upper_trace = line_inverse[group_id, LZ - 1, 0] * upper_trace + carried
            upper_list.append(upper_trace)
        upper_all = jnp.stack(upper_list)
        lower_trace = jnp.zeros((NX, NY), jnp.float32)
        lower_list = [lower_trace for group_id in range(group_total)]
        for group_id in range(group_total - 1, 0, -1):
            carried = (solved[group_id, 0] + line_inverse[group_id, 0, 0] * upper_all[group_id]) - upper_all[group_id]
            lower_trace = line_inverse[group_id, 0, LZ - 1] * lower_trace + carried
            lower_list[group_id - 1] = lower_trace
        lower_data = jnp.stack(lower_list)
        updated = solved + line_inverse[:, :, 0] * upper_all[:, None] + line_inverse[:, :, LZ - 1] * lower_data[:, None]
        field_now = updated.reshape(NZ, NX, NY)
    return field_now, slot_flow.reshape(group_total, tile_total * SLOTS, LZ)
```

```python
import functools

import jax
import jax.numpy as jnp
from jax import lax
from jax.experimental import pallas as pl
from jax.experimental.pallas import tpu as pltpu
from jax.sharding import PartitionSpec as P

ITERS = 2
LIMIT = 24 << 20
MESH = pl.DeviceIdType.MESH
F32 = jnp.float32
BF16 = jnp.bfloat16
ROWS = 8
LANES = 128


def pieces(value):
    high = value.astype(BF16)
    rest = value - high.astype(F32)
    middle = rest.astype(BF16)
    low = (rest - middle.astype(F32)).astype(BF16)
    return jnp.concatenate([high, middle, low], axis=0)


def as_column(row):
    n = row.shape[1]
    eye = lax.broadcasted_iota(jnp.int32, (n, n), 0) == lax.broadcasted_iota(jnp.int32, (n, n), 1)
    return jnp.sum(jnp.where(eye, jnp.broadcast_to(row, (n, n)), 0.0), axis=1, keepdims=True)


def as_row(column):
    n = column.shape[0]
    eye = lax.broadcasted_iota(jnp.int32, (n, n), 0) == lax.broadcasted_iota(jnp.int32, (n, n), 1)
    return jnp.sum(jnp.where(eye, jnp.broadcast_to(column, (n, n)), 0.0), axis=0, keepdims=True)


def one_hots(column_row, width_x, width_y):
    slots = column_row.shape[1]
    column_col = as_column(column_row.astype(F32)).astype(jnp.int32)
    lane_x = lax.broadcasted_iota(jnp.int32, (slots, width_x), 1)
    in_x = (column_col >= lane_x * width_y) & (column_col < lane_x * width_y + width_y)
    x_of = jnp.sum(jnp.where(in_x, lane_x.astype(F32), 0.0), axis=1, keepdims=True).astype(jnp.int32)
    in_y = lax.broadcasted_iota(jnp.int32, (slots, width_y), 1) == column_col - x_of * width_y
    hot_x = jnp.where(in_x, 1.0, 0.0).astype(BF16)
    row_x = lax.broadcasted_iota(jnp.int32, (width_x, slots), 0)
    hot_xt = jnp.where(
        (column_row >= row_x * width_y) & (column_row < row_x * width_y + width_y), 1.0, 0.0
    ).astype(BF16)
    return in_y, jnp.concatenate([hot_x] * 3, axis=1), jnp.concatenate([hot_xt] * 3, axis=1)


def keep(field_in, flow_in, field_out, flow_out, sem):
    copies = [
        pltpu.make_async_copy(field_in, field_out, sem.at[0]),
        pltpu.make_async_copy(flow_in, flow_out, sem.at[1]),
    ]
    for copy in copies:
        copy.start()
    for copy in copies:
        copy.wait()


def kernel(
    dims,
    pressure,
    source,
    perm_x,
    perm_y,
    inverse,
    robin,
    count_in,
    owner_in,
    well_in,
    column_in,
    index_in,
    rate_in,
    field_out,
    flow_out,
    field,
    src,
    kx,
    ky,
    inv,
    lower,
    count_v,
    owner_v,
    well_v,
    column_v,
    index_v,
    rate_v,
    upper,
    rhs,
    solved,
    flow_v,
    halo_mult_x,
    halo_mult_y,
    well_send0,
    well_recv0,
    well_send1,
    well_recv1,
    row_send,
    row_recv,
    col_send,
    col_recv,
    coef_recv,
    down_send,
    down_recv,
    up_send,
    up_recv,
    own_down,
    spot_recv,
    delta_send,
    delta_recv,
    load_sem,
    store_sem,
    well_ssem,
    well_rsem,
    halo_ssem,
    halo_rsem,
    coef_ssem,
    coef_rsem,
    down_ssem,
    down_rsem,
    up_ssem,
    up_rsem,
    spot_ssem,
    spot_rsem,
    delta_ssem,
    delta_rsem,
):
    groups, n_gx, n_gy = dims
    tiles = n_gx * n_gy
    depth, width_x, width_y = field.shape
    slots = well_v.shape[1]
    own_wells = rate_v.shape[1]
    wells = tiles * own_wells
    me_l, me_x, me_y = lax.axis_index("layer"), lax.axis_index("gx"), lax.axis_index("gy")
    me = me_x * n_gy + me_y

    loads = [
        pltpu.make_async_copy(a, b, load_sem.at[i])
        for i, (a, b) in enumerate(
            [
                (pressure, field),
                (column_in, column_v),
                (well_in, well_v),
                (owner_in, owner_v),
                (index_in, index_v),
                (count_in, count_v),
                (rate_in, rate_v),
                (perm_x, kx),
                (perm_y, ky),
                (source, src),
                (robin, lower),
                (inverse, inv),
            ]
        )
    ]
    for load in loads:
        load.start()

    def peer(step):
        other = lax.rem(me + step, tiles)
        return {"gx": lax.div(other, n_gy), "gy": lax.rem(other, n_gy)}

    barrier = pltpu.get_barrier_semaphore()
    for step in range(1, tiles):
        pl.semaphore_signal(barrier, inc=1, device_id=peer(step), device_id_type=MESH)
    for step in range(1, groups):
        pl.semaphore_signal(
            barrier, inc=1, device_id={"layer": lax.rem(me_l + step, groups)}, device_id_type=MESH
        )

    for load in loads[1:7]:
        load.wait()
    live = lax.broadcasted_iota(jnp.int32, (slots, 1), 0) < count_v[...]
    in_y, hot_x3, hot_xt3 = one_hots(column_v[...], width_x, width_y)
    well_col = as_column(well_v[...].astype(F32)).astype(jnp.int32)
    owner_col = as_column(owner_v[...].astype(F32)).astype(jnp.int32)
    well_id = owner_col * own_wells + well_col
    member = jnp.where(
        (lax.broadcasted_iota(jnp.int32, (slots, wells), 1) == well_id) & live, 1.0, 0.0
    )
    layer_lane = lax.broadcasted_iota(jnp.int32, (slots, depth), 1)
    index = jnp.zeros((slots, depth), F32)
    for l in range(depth):
        index = jnp.where(layer_lane == l, as_column(index_v[l : l + 1, :]), index)
    rate_col = as_column(rate_v[...])
    rate_spot = (
        lax.broadcasted_iota(jnp.int32, (own_wells, wells), 1)
        == lax.broadcasted_iota(jnp.int32, (own_wells, wells), 0) + me * own_wells
    )
    rate_row = jnp.sum(jnp.where(rate_spot, rate_col, 0.0), axis=0, keepdims=True)

    def gathered(ref):
        at = jnp.zeros((slots, depth), F32)
        for l in range(depth):
            picked = jnp.dot(hot_x3, pieces(ref[l]), preferred_element_type=F32)
            one = jnp.sum(jnp.where(in_y, picked, 0.0), axis=1, keepdims=True)
            at = jnp.where(layer_lane == l, one, at)
        return at

    def well_row(at):
        share = jnp.sum(index * at, axis=1, keepdims=True)
        return jnp.sum(share * member, axis=0, keepdims=True) + rate_row

    def well_copy(it, step):
        send, recv = ((well_send0, well_recv0), (well_send1, well_recv1))[it]
        return pltpu.make_async_remote_copy(
            src_ref=send,
            dst_ref=recv.at[step],
            send_sem=well_ssem.at[it, step],
            recv_sem=well_rsem.at[it, step],
            device_id=peer(step),
            device_id_type=MESH,
        )

    sides = (
        ("gx", me_x, -1, me_x > 0),
        ("gx", me_x, 1, me_x < n_gx - 1),
        ("gy", me_y, -1, me_y > 0),
        ("gy", me_y, 1, me_y < n_gy - 1),
    )

    def halo_copy(it, side):
        axis, mine, way, _ = sides[side]
        send, recv = (row_send, row_recv) if side < 2 else (col_send, col_recv)
        width = slice(0, 2 if it == 0 else 1)
        if side < 2:
            source_ref = send.at[it, side, width]
            target_ref = recv.at[it, 1 - side, width]
        else:
            source_ref = send.at[it, side - 2]
            target_ref = recv.at[it, 3 - side]
        return pltpu.make_async_remote_copy(
            src_ref=source_ref,
            dst_ref=target_ref,
            send_sem=halo_ssem.at[it, side],
            recv_sem=halo_rsem.at[it, side ^ 1],
            device_id={axis: mine + way},
            device_id_type=MESH,
        )

    def halo_landing(it, side):
        axis, mine, way, _ = sides[side]
        if side < 2:
            width = slice(0, 2 if it == 0 else 1)
            ref, other = row_recv.at[it, side, width], row_send.at[it, 1 - side, width]
        else:
            ref, other = col_recv.at[it, side - 2], col_send.at[it, 3 - side]
        return pltpu.make_async_remote_copy(
            src_ref=other,
            dst_ref=ref,
            send_sem=halo_ssem.at[it, side],
            recv_sem=halo_rsem.at[it, side],
            device_id={axis: mine + way},
            device_id_type=MESH,
        )

    lane128 = lax.broadcasted_iota(jnp.int32, (width_x, 128), 1)

    def packed_columns(arrays, lane):
        out = jnp.zeros((width_x, 128), F32)
        at = 0
        for ref in arrays:
            for l in range(depth):
                out = jnp.where(lane128 == at, ref[l, :, lane : lane + 1], out)
                at += 1
        return out

    def stage_halos(it):
        for l in range(depth):
            row_send[it, 0, 0, l : l + 1, :] = field[l, 0:1, :]
            row_send[it, 1, 0, l : l + 1, :] = field[l, width_x - 1 : width_x, :]
            if it == 0:
                row_send[it, 0, 1, l : l + 1, :] = kx[l, 0:1, :]
                row_send[it, 1, 1, l : l + 1, :] = kx[l, width_x - 1 : width_x, :]
        arrays = (field, ky) if it == 0 else (field,)
        col_send[it, 0] = packed_columns(arrays, 0)
        col_send[it, 1] = packed_columns(arrays, width_y - 1)
        for side in range(4):

            @pl.when(jnp.logical_not(sides[side][3]))
            def _():
                if side < 2:
                    row_recv[it, side] = jnp.zeros(row_recv.shape[2:], F32)
                else:
                    col_recv[it, side - 2] = jnp.zeros(col_recv.shape[2:], F32)

    def start_halos(it):
        for side in range(4):
            @pl.when(sides[side][3])
            def _():
                halo_copy(it, side).start()

    def wait_halos(it):
        for side in range(4):
            @pl.when(sides[side][3])
            def _():
                halo_landing(it, side).wait_recv()

    last_x = lax.broadcasted_iota(jnp.int32, (width_x, width_y), 0) == width_x - 1
    first_x = lax.broadcasted_iota(jnp.int32, (width_x, width_y), 0) == 0
    last_y = lax.broadcasted_iota(jnp.int32, (width_x, width_y), 1) == width_y - 1
    first_y = lax.broadcasted_iota(jnp.int32, (width_x, width_y), 1) == 0

    def face_coefficients():
        for l in range(depth):
            mult = kx[l]
            kx[l] = 0.5 * (mult + pltpu.roll(mult, width_x - 1, 0))
            mult = ky[l]
            ky[l] = 0.5 * (mult + pltpu.roll(mult, width_y - 1, 1))

    def edge_coefficients():
        for l in range(depth):
            one = slice(l, l + 1)
            halo_mult_x[one, :] = 0.5 * (row_send[0, 0, 1, one, :] + row_recv[0, 0, 1, one, :])
            kx[l, width_x - 1 : width_x, :] = 0.5 * (
                row_send[0, 1, 1, one, :] + row_recv[0, 1, 1, one, :]
            )
            lane = slice(depth + l, depth + l + 1)
            ky[l, :, width_y - 1 : width_y] = 0.5 * (
                col_send[0, 1, :, lane] + col_recv[0, 1, :, lane]
            )
        halo_mult_y[...] = 0.5 * (col_send[0, 0] + col_recv[0, 0])

    def lateral_sum():
        for l in range(depth):
            now = field[l]
            face_x, face_y = kx[l], ky[l]
            east = jnp.where(last_x, 0.0, face_x * pltpu.roll(now, width_x - 1, 0))
            west = jnp.where(first_x, 0.0, pltpu.roll(face_x * now, 1, 0))
            north = jnp.where(last_y, 0.0, face_y * pltpu.roll(now, width_y - 1, 1))
            south = jnp.where(first_y, 0.0, pltpu.roll(face_y * now, 1, 1))
            rhs[l] = src[l] + ((east + west) + (north + south))

    def lateral_edges(it):
        end_x, end_y = slice(width_x - 1, width_x), slice(width_y - 1, width_y)
        for l in range(depth):
            one = slice(l, l + 1)
            lane = slice(depth + l, depth + l + 1)
            rhs[l, 0:1, :] += halo_mult_x[one, :] * row_recv[it, 0, 0, one, :]
            rhs[l, end_x, :] += kx[l, end_x, :] * row_recv[it, 1, 0, one, :]
            rhs[l, :, 0:1] += halo_mult_y[:, lane] * col_recv[it, 0, :, one]
            rhs[l, :, end_y] += ky[l, :, end_y] * col_recv[it, 1, :, one]

    def layer_copy(ref, target, ssem, rsem, other):
        return pltpu.make_async_remote_copy(
            src_ref=ref,
            dst_ref=target,
            send_sem=ssem,
            recv_sem=rsem,
            device_id={"layer": other},
            device_id_type=MESH,
        )

    last = depth - 1
    coef_at = ((0, 0), (0, last), (last, 0))[: 1 if groups == 2 else 3]

    def coef_copy(which, sender, other):
        i, j = coef_at[which]
        return layer_copy(
            inv.at[i, j],
            coef_recv.at[sender, which],
            coef_ssem.at[other, which],
            coef_rsem.at[sender, which],
            other,
        )

    def coef_sent(which, sender, other):
        if which == 0:
            return other < sender
        if which == 1:
            return other < sender < groups - 1
        return 0 < sender < groups - 1

    def spot_copy(step):
        return layer_copy(
            column_v, spot_recv.at[step], spot_ssem.at[step], spot_rsem.at[step],
            lax.rem(me_l + step, groups),
        )

    def delta_copy(it, step):
        return layer_copy(
            delta_send.at[it], delta_recv.at[it, step], delta_ssem.at[it, step],
            delta_rsem.at[it, step], lax.rem(me_l + step, groups),
        )

    def down_copy(it, sender, other):
        return layer_copy(
            down_send.at[it], down_recv.at[it, sender], down_ssem.at[it, other],
            down_rsem.at[it, sender], other,
        )

    def up_copy(it, sender, other):
        return layer_copy(
            up_send.at[it], up_recv.at[it, sender], up_ssem.at[it, other],
            up_rsem.at[it, sender], other,
        )

    def layer_sends(act, which):
        for g in range(groups):

            @pl.when(me_l == g)
            def _():
                for other in range(groups):
                    if other == g:
                        continue
                    if which == "coef":
                        for c in range(len(coef_at)):
                            if coef_sent(c, g, other):
                                getattr(coef_copy(c, g, other), act)()
                    else:
                        it = which
                        if g < groups - 1:
                            getattr(down_copy(it, g, other), act)()
                        if other < g:
                            getattr(up_copy(it, g, other), act)()

    def chunk_loop(body):
        def step(c, carry):
            body(pl.ds(pl.multiple_of(c * ROWS, ROWS), ROWS))
            return carry

        lax.fori_loop(0, width_x // ROWS, step, 0)

    def dot_layer(i, rows, terms):
        total = inv[i, 0, rows, :] * terms[0]
        for j in range(1, depth):
            total = total + inv[i, j, rows, :] * terms[j]
        return total

    def solve_faces(it):
        def body(rows):
            terms = [rhs[j, rows, :] for j in range(depth)]
            bottom = dot_layer(last, rows, terms)
            top = dot_layer(0, rows, terms)
            below = lower[rows, :]
            nothing = jnp.zeros_like(below)
            down_send[it, rows, :] = inv[last, 0, rows, :] * nothing + (
                (bottom + inv[last, last, rows, :] * below) - below
            )
            up_send[it, rows, :] = inv[0, last, rows, :] * nothing + top

        chunk_loop(body)

    def solve_all():
        def body(rows):
            terms = [rhs[j, rows, :] for j in range(depth)]
            for i in range(depth):
                value = dot_layer(i, rows, terms)
                solved[i, rows, :] = value
                if i == last:
                    below = lower[rows, :]
                    own_down[rows, :] = inv[last, 0, rows, :] * jnp.zeros_like(below) + (
                        (value + inv[last, last, rows, :] * below) - below
                    )

        chunk_loop(body)

    def sweeps(it):
        for g in range(groups):

            @pl.when(me_l == g)
            def _():
                for k in range(groups):
                    if k == g:
                        continue
                    if k < groups - 1:
                        down_copy(it, k, k).wait_recv()
                    if k > g:
                        up_copy(it, k, k).wait_recv()
                    if it == 0:
                        for c in range(len(coef_at)):
                            if coef_sent(c, k, g):
                                coef_copy(c, k, k).wait_recv()
                    step = (g - k) % groups
                    delta_copy(it, step).wait_recv()
                    other_y, _, other_xt3 = spots[step]
                    for row, wanted, ref in ((0, k < groups - 1, down_recv), (1, k > g, up_recv)):
                        if wanted:
                            spread = as_column(delta_recv[it, step, row : row + 1, :])
                            spread = pieces(jnp.where(other_y, spread, 0.0))
                            ref[it, k] = ref[it, k] + jnp.dot(
                                other_xt3, spread, preferred_element_type=F32
                            )

                def body(rows):
                    def coef(which, k):
                        i, j = coef_at[which]
                        return inv[i, j, rows, :] if k == g else coef_recv[k, which, rows, :]

                    above = [jnp.zeros((ROWS, width_y), F32)]
                    for k in range(groups - 1):
                        value = own_down[rows, :] if k == g else down_recv[it, k, rows, :]
                        if k > 0:
                            value = coef(2, k) * above[k] + value
                        above.append(value)
                    below = jnp.zeros((ROWS, width_y), F32)
                    for k in range(groups - 1, g, -1):
                        value = (up_recv[it, k, rows, :] + coef(0, k) * above[k]) - above[k]
                        if k < groups - 1:
                            value = coef(1, k) * below + value
                        below = value
                    upper[rows, :] = above[g]
                    lower[rows, :] = below

                chunk_loop(body)

    def update():
        def body(rows):
            above, below = upper[rows, :], lower[rows, :]
            for i in range(depth):
                field[i, rows, :] = (
                    solved[i, rows, :]
                    + inv[i, 0, rows, :] * above
                    + inv[i, last, rows, :] * below
                )

        chunk_loop(body)

    index_total = None
    spots = [None] * groups
    for it in range(ITERS):
        if it == 0:
            loads[0].wait()
        at = gathered(field)
        if it == 0:
            index_row = jnp.sum(
                jnp.sum(index, axis=1, keepdims=True) * member, axis=0, keepdims=True
            )
            well_send0[...] = jnp.concatenate([well_row(at), index_row], axis=1)
            loads[7].wait()
            loads[8].wait()
            stage_halos(it)
            pl.semaphore_wait(barrier, tiles - 1 + groups - 1)
        else:
            well_send1[...] = well_row(at)
        for step in range(1, tiles):
            well_copy(it, step).start()
        if it > 0:
            stage_halos(it)
        start_halos(it)
        if it == 0:
            for step in range(1, groups):
                spot_copy(step).start()
            for load in loads[9:]:
                load.wait()
            layer_sends("start", "coef")
        if it == 0:
            face_coefficients()
        lateral_sum()
        wait_halos(it)
        if it == 0:
            edge_coefficients()
        lateral_edges(it)
        solve_faces(it)
        layer_sends("start", it)
        if it == 0:
            for step in range(1, groups):
                spot_copy(step).wait_recv()
                spots[step] = one_hots(spot_recv[step], width_x, width_y)
            face_last, face_first = gathered(inv.at[last]), gathered(inv.at[0])
        total = (well_send0, well_send1)[it][...]
        for step in range(1, tiles):
            well_copy(it, step).wait_recv()
        for step in range(1, tiles):
            total = total + (well_recv0, well_recv1)[it][step]
        if it == 0:
            index_total = total[:, wells:] + 1.0
            total = total[:, :wells]
        bottom_hole = total / index_total
        hole = jnp.sum(member * bottom_hole, axis=1, keepdims=True)
        flow = jnp.where(live, index * (hole - at), 0.0)
        for row, face in enumerate((face_last, face_first)):
            delta_send[it, row : row + 1, :] = as_row(
                jnp.sum(face * flow, axis=1, keepdims=True)
            )
        for step in range(1, groups):
            delta_copy(it, step).start()
        if it == ITERS - 1:
            for l in range(depth):
                flow_v[l : l + 1, :] = as_row(flow[:, l : l + 1])
            flow_store = pltpu.make_async_copy(flow_v, flow_out, store_sem.at[0])
            flow_store.start()
        for l in range(depth):
            spread = jnp.where(in_y, flow[:, l : l + 1], 0.0)
            rhs[l] = rhs[l] + jnp.dot(hot_xt3, pieces(spread), preferred_element_type=F32)
        solve_all()
        sweeps(it)
        update()
    field_store = pltpu.make_async_copy(field, field_out, store_sem.at[1])
    field_store.start()
    for it in range(ITERS):
        for step in range(1, tiles):
            well_copy(it, step).wait_send()
        for side in range(4):

            @pl.when(sides[side][3])
            def _():
                halo_copy(it, side).wait_send()

        layer_sends("wait_send", it)
        for step in range(1, groups):
            delta_copy(it, step).wait_send()
    for step in range(1, groups):
        spot_copy(step).wait_send()
    layer_sends("wait_send", "coef")
    flow_store.wait()
    field_store.wait()


def split(value, count):
    out = []
    for _ in range(count - 1):
        part = value.astype(BF16).astype(F32)
        out.append(part)
        value = value - part
    out.append(value)
    return out


def fused(
    dims,
    pressure,
    source,
    perm_x,
    perm_y,
    inverse,
    robin,
    count_in,
    owner_in,
    well_in,
    column_in,
    index_in,
    rate_in,
    field,
    flow_out,
    src,
    kx,
    ky,
    inv,
    lower,
    column_s,
    count_v,
    owner_v,
    well_v,
    column_v,
    index_v,
    rate_v,
    slabs,
    lower_at,
    rhs,
    solved,
    spread,
    left,
    own,
    par,
    lines,
    at_send,
    at_recv,
    coef_x,
    coef_y,
    well_send0,
    well_recv0,
    well_send1,
    well_recv1,
    row_send,
    row_recv,
    col_send,
    col_recv,
    gain_x,
    gain_y,
    gain_xr,
    gain_yr,
    edge_send,
    edge_recv,
    x_send,
    x_recv,
    kappa,
    smem_sem,
    slab_sem,
    load_sem,
    rest_sem,
    well_ssem,
    well_rsem,
    halo_ssem,
    halo_rsem,
    gain_ssem,
    gain_rsem,
    edge_ssem,
    edge_rsem,
    x_ssem,
    x_rsem,
    misc_ssem,
    misc_rsem,
):
    groups, n_gx, n_gy, depth = dims
    tiles = n_gx * n_gy
    width_x, width_y = lower.shape
    slots = well_v.shape[1]
    own_wells = rate_v.shape[1]
    wells = tiles * own_wells
    me_l, me_x, me_y = lax.axis_index("layer"), lax.axis_index("gx"), lax.axis_index("gy")
    me = me_x * n_gy + me_y
    upper_group = me_l == 0
    phi = (1 - me_l) * (depth - 1)
    halves = width_y // LANES

    def sheet(i):
        return slice(i * width_x, (i + 1) * width_x)

    def dyn_sheet(i):
        return pl.ds(pl.multiple_of(i * width_x, width_x), width_x)

    def peer(dl, step):
        return {"layer": me_l ^ dl, "gx": me_x ^ (step // n_gy), "gy": me_y ^ (step % n_gy)}

    peers = [
        (dl, step)
        for step in reversed(range(tiles))
        for dl in reversed(range(groups))
        if (dl, step) != (0, 0)
    ]
    partner = {"layer": 1 - me_l}

    block = depth * width_x
    to_smem = pltpu.make_async_copy(column_in, column_s, smem_sem)
    to_smem.start()
    loads = [
        pltpu.make_async_copy(a, b, load_sem.at[i])
        for i, (a, b) in enumerate(
            [
                (column_in, column_v),
                (well_in, well_v),
                (owner_in, owner_v),
                (index_in, index_v),
                (count_in, count_v),
                (rate_in, rate_v),
                (pressure, field),
                (perm_x, kx),
                (perm_y, ky),
                (source, src),
                (robin, lower),
            ]
        )
    ]
    tiled = [
        pltpu.make_async_copy(pressure.at[:, n * LANES : (n + 1) * LANES], slabs.at[n], slab_sem)
        for n in range(halves)
    ]
    barrier = pltpu.get_barrier_semaphore()
    for load in loads[:6] + tiled:
        load.start()
    for dl, step in peers:
        pl.semaphore_signal(barrier, inc=1, device_id=peer(dl, step), device_id_type=MESH)
    face_block = pl.ds(pl.multiple_of(phi * block, block), block)
    other_blocks = pl.ds(pl.multiple_of(me_l * block, block), (depth - 1) * block)

    def line_loads(rows, sem):
        return [
            pltpu.make_async_copy(
                inverse.at[rows, n * LANES : (n + 1) * LANES], inv.at[n, rows, :], sem
            )
            for n in range(halves)
        ]

    def lines_loaded(rows, sem):
        return pltpu.make_async_copy(inv.at[:, rows, :], inv.at[:, rows, :], sem)

    for load in loads[6:] + line_loads(face_block, rest_sem.at[0]):
        load.start()

    lane = lax.broadcasted_iota(jnp.int32, (8, LANES), 1)
    sub = lax.broadcasted_iota(jnp.int32, (8, LANES), 0)

    own[...] = jnp.zeros(own.shape, F32)
    for load in loads[:6]:
        load.wait()
    live = lax.broadcasted_iota(jnp.int32, (depth, slots), 1) < count_v[...]
    own[0:depth, 0:slots] = jnp.where(live, index_v[...], 0.0)
    own[2 * depth : 2 * depth + 1, 0:slots] = column_v[...].astype(F32)
    own[2 * depth + 1 : 2 * depth + 2, 0:slots] = (owner_v[...] * own_wells + well_v[...]).astype(F32)
    index = own[0:depth, :]
    well_id = own[2 * depth + 1 : 2 * depth + 2, :]
    member = jnp.where(
        lax.broadcasted_iota(jnp.int32, (LANES, wells), 1).astype(F32) == as_column(well_id), 1.0, 0.0
    ).astype(BF16)
    rate_col = as_column(rate_v[...])
    rate_spot = (
        lax.broadcasted_iota(jnp.int32, (own_wells, wells), 1)
        == lax.broadcasted_iota(jnp.int32, (own_wells, wells), 0) + me * own_wells
    )
    rate_row = jnp.sum(jnp.where(rate_spot, rate_col, 0.0), axis=0, keepdims=True)

    def gather(jobs, span):
        shift = width_y.bit_length() - 1

        def step(c, accs):
            for k in range(span):
                s = c * span + k
                column = column_s[0, s]
                if width_y == 1 << shift:
                    x, y = lax.shift_right_logical(column, shift), column & (width_y - 1)
                else:
                    x, y = lax.div(column, width_y), lax.rem(column, width_y)
                tile = lax.shift_right_logical(y, LANES.bit_length() - 1)
                turn = (s + LANES - (y & (LANES - 1))) & (LANES - 1)
                found = []
                for ref, first, stride, count in jobs:
                    if count == 1:
                        value = ref[tile, pl.ds(first + x, 1), :]
                    else:
                        value = ref[tile, pl.ds(first + x, count, stride=stride), :]
                    found.append(pltpu.roll(value, turn, 1))
                accs = tuple(
                    jnp.where(lane[: value.shape[0]] == s, value, acc) for acc, value in zip(accs, found)
                )
            return accs

        accs = tuple(jnp.zeros((count, LANES), F32) for _, _, _, count in jobs)
        if span == slots:
            return step(0, accs)
        return lax.fori_loop(0, slots // span, step, accs)

    wide = lax.broadcasted_iota(jnp.int32, (16, LANES), 0)

    def binned(rows):
        at, out = 0, jnp.zeros((16, LANES), F32)
        for row in rows:
            for part in split(row, 3):
                out = jnp.where(wide == at, part, out)
                at += 1
        total = jnp.dot(out.astype(BF16), member, preferred_element_type=F32)
        return [jnp.sum(total[3 * k : 3 * k + 3, :], axis=0, keepdims=True) for k in range(len(rows))]

    def remote(a, b, ssem, rsem, device):
        return pltpu.make_async_remote_copy(
            src_ref=a, dst_ref=b, send_sem=ssem, recv_sem=rsem, device_id=device, device_id_type=MESH
        )

    def well_copy(it, dl, step):
        send, recv = ((well_send0, well_recv0), (well_send1, well_recv1))[it]
        return remote(
            send, recv.at[dl * tiles + step - 1], well_ssem.at[it], well_rsem.at[it], peer(dl, step)
        )

    def all_wells(it):
        recv = (well_recv0, well_recv1)[it]
        return remote(recv, recv, well_ssem.at[it], well_rsem.at[it], partner)

    sides = (
        ("gx", me_x, -1, me_x > 0),
        ("gx", me_x, 1, me_x < n_gx - 1),
        ("gy", me_y, -1, me_y > 0),
        ("gy", me_y, 1, me_y < n_gy - 1),
    )

    def across(side, flip=False):
        axis, mine, way, _ = sides[side]
        out = {axis: mine + way}
        if flip:
            out["layer"] = 1 - me_l
        return out

    def halo_copy(it, side, landing=False):
        other = side ^ 1
        at, to = (other, side) if landing else (side, other)
        width = slice(0, 2 if it == 0 else 1)
        if side < 2:
            a, b = row_send.at[it, at, width], row_recv.at[it, to, width]
        else:
            a, b = col_send.at[it, at - 2], col_recv.at[it, to - 2]
        return remote(a, b, halo_ssem.at[it, at], halo_rsem.at[it, to], across(side))

    def gain_copy(side, landing=False):
        other = side ^ 1
        at, to = (other, side) if landing else (side, other)
        if side < 2:
            a, b = gain_x.at[at], gain_xr.at[to]
        else:
            a, b = gain_y.at[at - 2], gain_yr.at[to - 2]
        return remote(a, b, gain_ssem.at[at], gain_rsem.at[to], across(side))

    def edge_copy(side, landing=False):
        other = side ^ 1
        at, to = (other, side) if landing else (side, other)
        return remote(
            edge_send.at[1, at], edge_recv.at[1, to], edge_ssem.at[at], edge_rsem.at[to],
            across(side, True),
        )

    def edge_pack():
        return remote(edge_send.at[0], edge_recv.at[0], edge_ssem.at[4], edge_rsem.at[4], partner)

    def x_copy(it):
        return remote(x_send.at[it], x_recv.at[it], x_ssem.at[it], x_rsem.at[it], partner)

    slot_copy = remote(own, par, misc_ssem.at[0], misc_rsem.at[0], partner)
    at_copy = remote(at_send, at_recv, misc_ssem.at[1], misc_rsem.at[1], partner)
    kappa_copy = remote(inv.at[:, 0:width_x, :], kappa, misc_ssem.at[2], misc_rsem.at[2], partner)

    lane_x = lax.broadcasted_iota(jnp.int32, (width_x, LANES), 1)

    def packed_columns(blocks, y):
        out = jnp.zeros((width_x, LANES), F32)
        for at, (ref, rows) in enumerate(blocks):
            tile = y - y % LANES
            value = ref[rows, tile : tile + LANES]
            out = jnp.where(lane_x == at, pltpu.roll(value, (at - y) % LANES, 1), out)
        return out

    def each(ref):
        return [(ref, sheet(l)) for l in range(depth)]

    ends_x, ends_y = (0, width_x - 1), (0, width_y - 1)

    def stage_halos(it):
        for side, x in enumerate(ends_x):
            for l in range(depth):
                row = l * width_x + x
                row_send[it, side, 0, l : l + 1, :] = field[row : row + 1, :]
                if it == 0:
                    row_send[it, side, 1, l : l + 1, :] = kx[row : row + 1, :]
        blocks = each(field) + (each(ky) if it == 0 else [])
        for side, y in enumerate(ends_y):
            col_send[it, side] = packed_columns(blocks, y)

    def clear_halos(it):
        for side in range(4):

            @pl.when(jnp.logical_not(sides[side][3]))
            def _():
                if side < 2:
                    row_recv[it, side] = jnp.zeros(row_recv.shape[2:], F32)
                else:
                    col_recv[it, side - 2] = jnp.zeros(col_recv.shape[2:], F32)
                if it == 1:
                    edge_recv[it, side] = jnp.zeros(edge_recv.shape[2:], F32)

    def on_sides(body):
        for side in range(4):
            pl.when(sides[side][3])(functools.partial(body, side))

    first_x = lax.broadcasted_iota(jnp.int32, (width_x, width_y), 0) == width_x - 1
    first_y = lax.broadcasted_iota(jnp.int32, (width_x, width_y), 1) == width_y - 1

    def face_coefficients():
        for l in range(depth):
            mult = kx[sheet(l), :]
            kx[sheet(l), :] = jnp.where(first_x, 0.0, 0.5 * (mult + pltpu.roll(mult, width_x - 1, 0)))
            mult = ky[sheet(l), :]
            ky[sheet(l), :] = jnp.where(first_y, 0.0, 0.5 * (mult + pltpu.roll(mult, width_y - 1, 1)))

    def lateral_sum():
        for l in range(depth):
            now = field[sheet(l), :]
            face_x, face_y = kx[sheet(l), :], ky[sheet(l), :]
            east = face_x * pltpu.roll(now, width_x - 1, 0)
            west = pltpu.roll(face_x * now, 1, 0)
            north = face_y * pltpu.roll(now, width_y - 1, 1)
            south = pltpu.roll(face_y * now, 1, 1)
            rhs[sheet(l), :] = src[sheet(l), :] + ((east + west) + (north + south))

    def lateral_edges(it):
        for l in range(depth):
            one = slice(l, l + 1)
            for side, x in enumerate(ends_x):
                row = slice(l * width_x + x, l * width_x + x + 1)
                rhs[row, :] += coef_x[side, one, :] * row_recv[it, side, 0, one, :]
        for side, y in enumerate(ends_y):
            tile = y - y % LANES
            terms = coef_y[side] * col_recv[it, side]
            for l in range(depth):
                term = pltpu.roll(terms, (y - l) % LANES, 1)
                rhs[sheet(l), tile : tile + LANES] += jnp.where(lane_x == y - tile, term, 0.0)

    def edge_coefficients():
        for side in range(2):
            coef_x[side] = 0.5 * (row_send[0, side, 1] + row_recv[0, side, 1])
            coef_y[side] = pltpu.roll(
                0.5 * (col_send[0, side] + col_recv[0, side]), LANES - depth, 1
            )

    def chunk_loop(body):
        def step(c, carry):
            body(pl.multiple_of(c * ROWS, ROWS))
            return carry

        lax.fori_loop(0, width_x // ROWS, step, 0)

    def whole(ref, rows):
        return jnp.concatenate([ref[n, rows, :] for n in range(halves)], axis=1)

    def rows_of(i, at):
        return pl.ds(pl.multiple_of(i * width_x + at, ROWS), ROWS)

    def own_face(at):
        below = lower[pl.ds(at, ROWS), :]
        corner = whole(inv, rows_of(phi * depth + phi, at))
        return jnp.where(upper_group, corner * below - below, 0.0)

    def interior_face(it):
        def body(at):
            total = own_face(at)
            for j in range(depth):
                total = total + whole(inv, rows_of(phi * depth + j, at)) * rhs[rows_of(j, at), :]
            x_send[it, pl.ds(at, ROWS), :] = total

        chunk_loop(body)

    def solve_all():
        def body(at):
            terms = [rhs[rows_of(j, at), :] for j in range(depth)]
            for i in range(depth):
                total = whole(inv, rows_of(i * depth, at)) * terms[0]
                for j in range(1, depth):
                    total = total + whole(inv, rows_of(i * depth + j, at)) * terms[j]
                for n in range(halves):
                    solved[n, rows_of(i, at), :] = total[:, n * LANES : (n + 1) * LANES]

        chunk_loop(body)

    def robin_data(it):
        for side, x in enumerate(ends_x):
            x_recv[it, x : x + 1, :] += edge_recv[it, side]
        for side, y in enumerate(ends_y):
            x_recv[it, :, y : y + 1] += as_column(edge_recv[it, 2 + side, :, 0:width_x])

        def body(at):
            rows = pl.ds(at, ROWS)
            mine = whole(solved, rows_of(phi, at)) + own_face(at)
            data = x_recv[it, rows, :] + jnp.where(upper_group, whole(kappa, rows) * mine - mine, 0.0)
            lower[rows, :] = data
            for n in range(halves):
                lower_at[n, rows, :] = data[:, n * LANES : (n + 1) * LANES]

        chunk_loop(body)

    def update():
        def body(at):
            rows = pl.ds(at, ROWS)
            data = lower[rows, :] + spread[rows_of(depth, at), :]
            lower[rows, :] = data
            for i in range(depth):
                field[rows_of(i, at), :] = (
                    whole(solved, rows_of(i, at))
                    + spread[rows_of(i, at), :]
                    + whole(inv, rows_of(i * depth + phi, at)) * data
                )

        chunk_loop(body)

    def start(copy):
        copy.start()

    to_smem.wait()
    pltpu.make_async_copy(slabs, slabs, slab_sem).wait()
    for load in line_loads(other_blocks, rest_sem.at[1]):
        load.start()
    at_own = gather([(slabs, 0, width_x, depth)], slots)[0]
    own[depth : 2 * depth, :] = at_own
    share, sums = binned(
        [jnp.sum(index * at_own, axis=0, keepdims=True), jnp.sum(index, axis=0, keepdims=True)]
    )
    well_send0[...] = jnp.concatenate([share + rate_row, sums], axis=1)
    clear_halos(0)
    clear_halos(1)
    for load in loads[6:9]:
        load.wait()
    stage_halos(0)
    for load in loads[9:]:
        load.wait()
    lines_loaded(face_block, rest_sem.at[0]).wait()
    face_coefficients()
    lateral_sum()
    interior_face(0)
    pl.semaphore_wait(barrier, len(peers))
    for dl, step in peers:
        well_copy(0, dl, step).start()
    on_sides(lambda side: halo_copy(0, side).start())
    x_copy(0).start()
    lines_loaded(other_blocks, rest_sem.at[1]).wait()
    own[3 * depth : 4 * depth, :] = gather([(inv, phi * block, width_x, depth)], slots)[0]
    slot_copy.start()

    @pl.when(me_l == 1)
    def _():
        kappa_copy.start()
        kappa[...] = jnp.zeros(kappa.shape, F32)

    for j, value in enumerate(gather([(inv, j * width_x, block, depth) for j in range(depth)], 16)):
        lines[j] = value

    for side, x in enumerate(ends_x):
        for j in range(depth):
            gain_x[side, j : j + 1, :] = whole(inv, pl.ds((phi * depth + j) * width_x + x, 1))
    for side, y in enumerate(ends_y):
        n = y // LANES
        face = packed_columns(
            [(inv.at[n], dyn_sheet(phi * depth + j)) for j in range(depth)], y - n * LANES
        )
        gain_y[side] = jnp.where(lane_x < depth, face, 0.0)
    on_sides(lambda side: halo_copy(0, side, True).wait_recv())
    edge_coefficients()
    for side in range(2):
        gain_x[side] = gain_x[side] * coef_x[side]
        edge_send[0, side] = jnp.sum(gain_x[side] * row_recv[0, side, 0], axis=0, keepdims=True)
    for side in range(2):
        gain = gain_y[side] * coef_y[side]
        gain_y[side] = gain
        edge_send[0, 2 + side, :, 0:width_x] = as_row(
            jnp.sum(gain * col_recv[0, side], axis=1, keepdims=True)
        )
    edge_pack().start()
    on_sides(lambda side: gain_copy(side).start())
    lateral_edges(0)
    solve_all()

    half = LANES // 2
    slot_copy.wait_recv()
    both = own[0 : 3 * depth, :] + pltpu.roll(par[0 : 3 * depth, :], half, 1)
    index2, at2 = both[0:depth], both[depth : 2 * depth]
    column_row, wells_row = both[2 * depth : 2 * depth + 1], both[2 * depth + 1 : 2 * depth + 2]
    wells_at = jnp.broadcast_to(wells_row, (8, LANES)).astype(jnp.int32)
    column_col = as_column(column_row)
    same = jnp.where(column_col == column_row, 1.0, 0.0).astype(BF16)

    def x_of(column):
        return jnp.floor((column + 0.5) * (1.0 / width_y))

    y_col = column_col - x_of(column_col) * width_y
    hot_y = jnp.where(
        lax.broadcasted_iota(jnp.int32, (LANES, width_y), 1).astype(F32) == y_col, 1.0, 0.0
    ).astype(BF16)
    hot_y = jnp.concatenate([hot_y, hot_y], axis=0)
    in_x = lax.broadcasted_iota(jnp.int32, (width_x, LANES), 0).astype(F32) == x_of(column_row)
    lower_half = lane < half
    face_par = pltpu.roll(par[3 * depth : 4 * depth, :], half, 1)

    def well_totals(it):
        send, recv = ((well_send0, well_recv0), (well_send1, well_recv1))[it]
        all_wells(it).wait_recv()
        mine, other = send[...], recv[tiles - 1]
        for step in range(1, tiles):
            mine, other = mine + recv[step - 1], other + recv[tiles + step - 1]
        return mine, other

    def flows(mine, other, at_slots):
        def at_wells(row):
            return jnp.take_along_axis(
                jnp.broadcast_to(row, (8, LANES)), wells_at, axis=1, mode="promise_in_bounds"
            )

        hole = jnp.where(lower_half, at_wells(mine), at_wells(other))
        return index2 * (hole - at_slots)

    def responses(flow, kappa_gain):
        change = jnp.zeros((depth, LANES), F32)
        for j in range(depth):
            change = change + lines[j] * flow[j : j + 1, :]
        out = jnp.sum(jnp.where(sub == phi, change, 0.0), axis=0, keepdims=True)
        theirs = jnp.sum(face_par * flow, axis=0, keepdims=True)
        return change, kappa_gain * out + theirs

    def spread_out(change, data):
        for i in range(depth + 1):
            row = change[i : i + 1, :] if i < depth else data
            left[sheet(i), :] = jnp.concatenate(
                [jnp.where(in_x, part, 0.0).astype(BF16) for part in split(row, 2)], axis=1
            )
        spread[...] = jnp.dot(left[...], hot_y, preferred_element_type=F32)

    @pl.when(upper_group)
    def _():
        kappa_copy.wait_recv()

    solved_at, kappa_at = gather([(solved, 0, width_x, depth), (kappa, 0, 1, 1)], slots)
    kappa_gain = jnp.where(upper_group & lower_half[0:1], kappa_at - 1.0, 0.0)
    mine, other = well_totals(0)
    index_mine, index_other = mine[:, wells:] + 1.0, other[:, wells:] + 1.0
    flow = flows(mine[:, :wells] / index_mine, other[:, :wells] / index_other, at2)
    change, data = responses(flow, kappa_gain)
    spread_out(change, data)
    x_copy(0).wait_recv()
    edge_pack().wait_recv()
    robin_data(0)
    data_at = gather([(lower_at, 0, 1, 1)], slots)[0]
    stack = jnp.concatenate([change, jnp.broadcast_to(data, (8, LANES))], axis=0)
    pile = jnp.concatenate(split(stack, 3), axis=0).astype(BF16)
    summed = jnp.dot(pile, same, preferred_element_type=F32)
    summed = (summed[0:16] + summed[16:32]) + summed[32:48]
    at_own = (solved_at + summed[0:8]) + lines[phi] * (data_at + summed[8:9])
    at_send[...] = at_own
    (share,) = binned([jnp.sum(index * at_own, axis=0, keepdims=True)])
    well_send1[...] = share + rate_row
    for dl, step in peers:
        well_copy(1, dl, step).start()
    at_copy.start()
    update()

    lateral_sum()
    interior_face(1)
    x_copy(1).start()
    stage_halos(1)
    on_sides(lambda side: halo_copy(1, side).start())
    on_sides(lambda side: gain_copy(side, True).wait_recv())
    for side in range(4):

        @pl.when(sides[side][3])
        def _():
            if side < 2:
                edge_send[1, side] = jnp.sum(
                    gain_xr[side] * row_send[1, side, 0], axis=0, keepdims=True
                )
            else:
                edge_send[1, side, :, 0:width_x] = as_row(
                    jnp.sum(gain_yr[side - 2] * col_send[1, side - 2], axis=1, keepdims=True)
                )
            edge_copy(side).start()

    on_sides(lambda side: halo_copy(1, side, True).wait_recv())
    lateral_edges(1)
    solve_all()
    at_copy.wait_recv()
    at2 = jnp.where(lower_half, at_own, pltpu.roll(at_recv[...], half, 1))
    mine, other = well_totals(1)
    flow = flows(mine / index_mine, other / index_other, at2)
    flow_out[...] = flow[:, 0:slots]
    spread_out(*responses(flow, kappa_gain))
    x_copy(1).wait_recv()
    on_sides(lambda side: edge_copy(side, True).wait_recv())
    robin_data(1)
    update()

    for it in range(ITERS):
        all_wells(it).wait_send()
        on_sides(lambda side: halo_copy(it, side).wait_send())
        x_copy(it).wait_send()
    on_sides(lambda side: gain_copy(side).wait_send())
    on_sides(lambda side: edge_copy(side).wait_send())
    edge_pack().wait_send()
    slot_copy.wait_send()
    at_copy.wait_send()

    @pl.when(me_l == 1)
    def _():
        kappa_copy.wait_send()


def fused_shards(arrays, dims):
    (
        pressure, source, perm_x, perm_y, line_inverse, robin_below,
        tile_count, perf_owner, perf_well, perf_column, perf_index, well_rate,
    ) = arrays
    groups, n_gx, n_gy = dims
    depth, width_x, width_y = pressure.shape
    tiles = n_gx * n_gy
    slots = perf_well.shape[1]
    own_wells = well_rate.shape[1]
    wells = tiles * own_wells
    sheet = (width_x, width_y)
    stack = (depth * width_x, width_y)
    halves = width_y // LANES
    HBM = pl.BlockSpec(memory_space=pltpu.HBM)
    VMEM = pl.BlockSpec(memory_space=pltpu.VMEM)
    anywhere = pl.BlockSpec(memory_space=pl.ANY)
    dma = pltpu.SemaphoreType.DMA
    i32 = jnp.int32

    def vmem(*shape):
        return pltpu.VMEM(shape, F32)

    call = pl.pallas_call(
        functools.partial(fused, (groups, n_gx, n_gy, depth)),
        out_shape=(jax.ShapeDtypeStruct(stack, F32), jax.ShapeDtypeStruct((depth, slots), F32)),
        in_specs=[HBM] * 12,
        out_specs=(VMEM, VMEM),
        scratch_shapes=[
            vmem(*stack),
            vmem(*stack),
            vmem(*stack),
            vmem(halves, depth * depth * width_x, LANES),
            vmem(*sheet),
            pltpu.SMEM((1, slots), i32),
            pltpu.VMEM((1, 1), i32),
            pltpu.VMEM((1, slots), i32),
            pltpu.VMEM((1, slots), i32),
            pltpu.VMEM((1, slots), i32),
            vmem(depth, slots),
            vmem(1, own_wells),
            vmem(halves, depth * width_x, LANES),
            vmem(halves, width_x, LANES),
            vmem(*stack),
            vmem(halves, depth * width_x, LANES),
            vmem((depth + 1) * width_x, width_y),
            pltpu.VMEM(((depth + 1) * width_x, 2 * LANES), BF16),
            vmem(4 * depth, LANES),
            vmem(4 * depth, LANES),
            vmem(depth, depth, LANES),
            vmem(depth, LANES),
            vmem(depth, LANES),
            vmem(2, depth, width_y),
            vmem(2, width_x, LANES),
            vmem(1, 2 * wells),
            vmem(groups * tiles - 1, 1, 2 * wells),
            vmem(1, wells),
            vmem(groups * tiles - 1, 1, wells),
            vmem(ITERS, 2, 2, depth, width_y),
            vmem(ITERS, 2, 2, depth, width_y),
            vmem(ITERS, 2, width_x, LANES),
            vmem(ITERS, 2, width_x, LANES),
            vmem(2, depth, width_y),
            vmem(2, width_x, LANES),
            vmem(2, depth, width_y),
            vmem(2, width_x, LANES),
            vmem(ITERS, 4, 1, width_y),
            vmem(ITERS, 4, 1, width_y),
            vmem(ITERS, *sheet),
            vmem(ITERS, *sheet),
            vmem(halves, width_x, LANES),
            dma,
            dma,
            dma((11,)),
            dma((2,)),
            dma((ITERS,)),
            dma((ITERS,)),
            dma((ITERS, 4)),
            dma((ITERS, 4)),
            dma((4,)),
            dma((4,)),
            dma((5,)),
            dma((5,)),
            dma((ITERS,)),
            dma((ITERS,)),
            dma((3,)),
            dma((3,)),
        ],
        compiler_params=pltpu.CompilerParams(
            collective_id=0, has_side_effects=True, vmem_limit_bytes=LIMIT
        ),
        name="window",
    )
    operands = (
        pressure.reshape(stack),
        source.reshape(stack),
        perm_x.reshape(stack),
        perm_y.reshape(stack),
        line_inverse.reshape(depth * depth * width_x, width_y),
        robin_below[0],
        tile_count,
        perf_owner[:, :, 0],
        perf_well,
        perf_column,
        perf_index[0].T,
        well_rate,
    )
    field, flow = call(
        *[x if x.size == 1 else pltpu.with_memory_space_constraint(x, pltpu.HBM) for x in operands]
    )
    field, flow = pl.pallas_call(
        keep,
        out_shape=(
            jax.ShapeDtypeStruct(field.shape, F32),
            jax.ShapeDtypeStruct(flow.shape, F32),
        ),
        in_specs=[anywhere] * 2,
        out_specs=(HBM, HBM),
        scratch_shapes=[dma((2,))],
        compiler_params=pltpu.CompilerParams(vmem_limit_bytes=1 << 20),
        name="keep",
    )(field, flow)
    return field.reshape(pressure.shape), flow.T[None]


def shards(
    pressure,
    source,
    perm_x,
    perm_y,
    line_inverse,
    robin_below,
    tile_count,
    perf_owner,
    perf_well,
    perf_column,
    perf_index,
    well_rate,
):
    depth, width_x, width_y = pressure.shape
    groups, n_gx, n_gy = (lax.axis_size(a) for a in ("layer", "gx", "gy"))
    tiles = n_gx * n_gy
    slots = perf_well.shape[1]
    own_wells = well_rate.shape[1]
    wells = tiles * own_wells
    powers = all(n == 1 << (n.bit_length() - 1) for n in (n_gx, n_gy))
    if (
        groups == 2
        and depth == 8
        and wells == LANES
        and slots <= LANES // 2
        and slots % 16 == 0
        and width_x <= LANES
        and width_y % LANES == 0
        and powers
    ):
        arrays = (
            pressure, source, perm_x, perm_y, line_inverse, robin_below,
            tile_count, perf_owner, perf_well, perf_column, perf_index, well_rate,
        )
        return fused_shards(arrays, (groups, n_gx, n_gy))
    sheet = (width_x, width_y)
    coefs = 1 if groups == 2 else 3
    HBM = pl.BlockSpec(memory_space=pltpu.HBM)
    anywhere = pl.BlockSpec(memory_space=pl.ANY)
    dma = pltpu.SemaphoreType.DMA
    i32 = jnp.int32
    call = pl.pallas_call(
        functools.partial(kernel, (groups, n_gx, n_gy)),
        out_shape=(
            jax.ShapeDtypeStruct(pressure.shape, F32),
            jax.ShapeDtypeStruct((depth, slots), F32),
        ),
        in_specs=[HBM] * 12,
        out_specs=(anywhere, anywhere),
        scratch_shapes=[
            pltpu.VMEM(pressure.shape, F32),
            pltpu.VMEM(pressure.shape, F32),
            pltpu.VMEM(pressure.shape, F32),
            pltpu.VMEM(pressure.shape, F32),
            pltpu.VMEM((depth, depth) + sheet, F32),
            pltpu.VMEM(sheet, F32),
            pltpu.VMEM((1, 1), i32),
            pltpu.VMEM((1, slots), i32),
            pltpu.VMEM((1, slots), i32),
            pltpu.VMEM((1, slots), i32),
            pltpu.VMEM((depth, slots), F32),
            pltpu.VMEM((1, own_wells), F32),
            pltpu.VMEM(sheet, F32),
            pltpu.VMEM(pressure.shape, F32),
            pltpu.VMEM(pressure.shape, F32),
            pltpu.VMEM((depth, slots), F32),
            pltpu.VMEM((depth, width_y), F32),
            pltpu.VMEM((width_x, 128), F32),
            pltpu.VMEM((1, 2 * wells), F32),
            pltpu.VMEM((tiles, 1, 2 * wells), F32),
            pltpu.VMEM((1, wells), F32),
            pltpu.VMEM((tiles, 1, wells), F32),
            pltpu.VMEM((ITERS, 2, 2, depth, width_y), F32),
            pltpu.VMEM((ITERS, 2, 2, depth, width_y), F32),
            pltpu.VMEM((ITERS, 2, width_x, 128), F32),
            pltpu.VMEM((ITERS, 2, width_x, 128), F32),
            pltpu.VMEM((groups, coefs) + sheet, F32),
            pltpu.VMEM((ITERS,) + sheet, F32),
            pltpu.VMEM((ITERS, groups) + sheet, F32),
            pltpu.VMEM((ITERS,) + sheet, F32),
            pltpu.VMEM((ITERS, groups) + sheet, F32),
            pltpu.VMEM(sheet, F32),
            pltpu.VMEM((groups, 1, slots), i32),
            pltpu.VMEM((ITERS, 2, slots), F32),
            pltpu.VMEM((ITERS, groups, 2, slots), F32),
            dma((12,)),
            dma((2,)),
            dma((ITERS, tiles)),
            dma((ITERS, tiles)),
            dma((ITERS, 4)),
            dma((ITERS, 4)),
            dma((groups, coefs)),
            dma((groups, coefs)),
            dma((ITERS, groups)),
            dma((ITERS, groups)),
            dma((ITERS, groups)),
            dma((ITERS, groups)),
            dma((groups,)),
            dma((groups,)),
            dma((ITERS, groups)),
            dma((ITERS, groups)),
        ],
        compiler_params=pltpu.CompilerParams(collective_id=0, has_side_effects=True, vmem_limit_bytes=LIMIT),
        name="window",
    )
    operands = (
        pressure,
        source,
        perm_x,
        perm_y,
        line_inverse[0],
        robin_below[0],
        tile_count,
        perf_owner[:, :, 0],
        perf_well,
        perf_column,
        perf_index[0].T,
        well_rate,
    )
    field, flow = call(
        *[x if x.size == 1 else pltpu.with_memory_space_constraint(x, pltpu.HBM) for x in operands]
    )
    field, flow = pl.pallas_call(
        keep,
        out_shape=(
            jax.ShapeDtypeStruct(field.shape, F32),
            jax.ShapeDtypeStruct(flow.shape, F32),
        ),
        in_specs=[anywhere] * 2,
        out_specs=(HBM, HBM),
        scratch_shapes=[dma((2,))],
        compiler_params=pltpu.CompilerParams(vmem_limit_bytes=1 << 20),
        name="keep",
    )(field, flow)
    return field, flow.T[None]


def solution(mesh):
    placed = (
        P("layer", "gx", "gy"),
        P("layer", "gx", "gy"),
        P("layer", "gx", "gy"),
        P("layer", "gx", "gy"),
        P("layer", None, None, "gx", "gy"),
        P("layer", "gx", "gy"),
        P("layer", ("gx", "gy")),
        P("layer", ("gx", "gy"), None),
        P("layer", ("gx", "gy")),
        P("layer", ("gx", "gy")),
        P("layer", ("gx", "gy"), None),
        P("layer", ("gx", "gy")),
    )
    return jax.shard_map(
        shards,
        mesh=mesh,
        in_specs=placed,
        out_specs=(P("layer", "gx", "gy"), P("layer", ("gx", "gy"), None)),
        check_vma=False,
    )
```

```python
import functools
import math

import jax
import jax.numpy as jnp
from jax import lax
from jax.experimental import pallas as pl
from jax.experimental.pallas import tpu as pltpu
from jax.sharding import PartitionSpec as P

ITERS = 2
LIMIT = 24 << 20
MESH = pl.DeviceIdType.MESH
F32 = jnp.float32
BF16 = jnp.bfloat16
ROWS = 8
LANES = 128


def pieces(value):
    high = value.astype(BF16)
    rest = value - high.astype(F32)
    middle = rest.astype(BF16)
    low = (rest - middle.astype(F32)).astype(BF16)
    return jnp.concatenate([high, middle, low], axis=0)


def as_column(row):
    n = row.shape[1]
    eye = lax.broadcasted_iota(jnp.int32, (n, n), 0) == lax.broadcasted_iota(jnp.int32, (n, n), 1)
    return jnp.sum(jnp.where(eye, jnp.broadcast_to(row, (n, n)), 0.0), axis=1, keepdims=True)


def as_row(column):
    n = column.shape[0]
    eye = lax.broadcasted_iota(jnp.int32, (n, n), 0) == lax.broadcasted_iota(jnp.int32, (n, n), 1)
    return jnp.sum(jnp.where(eye, jnp.broadcast_to(column, (n, n)), 0.0), axis=0, keepdims=True)


def one_hots(column_row, width_x, width_y):
    slots = column_row.shape[1]
    column_col = as_column(column_row.astype(F32)).astype(jnp.int32)
    lane_x = lax.broadcasted_iota(jnp.int32, (slots, width_x), 1)
    in_x = (column_col >= lane_x * width_y) & (column_col < lane_x * width_y + width_y)
    x_of = jnp.sum(jnp.where(in_x, lane_x.astype(F32), 0.0), axis=1, keepdims=True).astype(jnp.int32)
    in_y = lax.broadcasted_iota(jnp.int32, (slots, width_y), 1) == column_col - x_of * width_y
    hot_x = jnp.where(in_x, 1.0, 0.0).astype(BF16)
    row_x = lax.broadcasted_iota(jnp.int32, (width_x, slots), 0)
    hot_xt = jnp.where(
        (column_row >= row_x * width_y) & (column_row < row_x * width_y + width_y), 1.0, 0.0
    ).astype(BF16)
    return in_y, jnp.concatenate([hot_x] * 3, axis=1), jnp.concatenate([hot_xt] * 3, axis=1)


def keep(field_in, flow_in, field_out, flow_out, sem):
    copies = [
        pltpu.make_async_copy(field_in, field_out, sem.at[0]),
        pltpu.make_async_copy(flow_in, flow_out, sem.at[1]),
    ]
    for copy in copies:
        copy.start()
    for copy in copies:
        copy.wait()


def kernel(
    dims,
    pressure,
    source,
    perm_x,
    perm_y,
    inverse,
    robin,
    count_in,
    owner_in,
    well_in,
    column_in,
    index_in,
    rate_in,
    field_out,
    flow_out,
    field,
    src,
    kx,
    ky,
    inv,
    lower,
    count_v,
    owner_v,
    well_v,
    column_v,
    index_v,
    rate_v,
    upper,
    rhs,
    solved,
    flow_v,
    halo_mult_x,
    halo_mult_y,
    well_send0,
    well_recv0,
    well_send1,
    well_recv1,
    row_send,
    row_recv,
    col_send,
    col_recv,
    coef_recv,
    down_send,
    down_recv,
    up_send,
    up_recv,
    own_down,
    spot_recv,
    delta_send,
    delta_recv,
    load_sem,
    store_sem,
    well_ssem,
    well_rsem,
    halo_ssem,
    halo_rsem,
    coef_ssem,
    coef_rsem,
    down_ssem,
    down_rsem,
    up_ssem,
    up_rsem,
    spot_ssem,
    spot_rsem,
    delta_ssem,
    delta_rsem,
):
    groups, n_gx, n_gy = dims
    tiles = n_gx * n_gy
    depth, width_x, width_y = field.shape
    slots = well_v.shape[1]
    own_wells = rate_v.shape[1]
    wells = tiles * own_wells
    me_l, me_x, me_y = lax.axis_index("layer"), lax.axis_index("gx"), lax.axis_index("gy")
    me = me_x * n_gy + me_y

    loads = [
        pltpu.make_async_copy(a, b, load_sem.at[i])
        for i, (a, b) in enumerate(
            [
                (pressure, field),
                (column_in, column_v),
                (well_in, well_v),
                (owner_in, owner_v),
                (index_in, index_v),
                (count_in, count_v),
                (rate_in, rate_v),
                (perm_x, kx),
                (perm_y, ky),
                (source, src),
                (robin, lower),
                (inverse, inv),
            ]
        )
    ]
    for load in loads:
        load.start()

    def peer(step):
        other = lax.rem(me + step, tiles)
        return {"gx": lax.div(other, n_gy), "gy": lax.rem(other, n_gy)}

    barrier = pltpu.get_barrier_semaphore()
    for step in range(1, tiles):
        pl.semaphore_signal(barrier, inc=1, device_id=peer(step), device_id_type=MESH)
    for step in range(1, groups):
        pl.semaphore_signal(
            barrier, inc=1, device_id={"layer": lax.rem(me_l + step, groups)}, device_id_type=MESH
        )

    for load in loads[1:7]:
        load.wait()
    live = lax.broadcasted_iota(jnp.int32, (slots, 1), 0) < count_v[...]
    in_y, hot_x3, hot_xt3 = one_hots(column_v[...], width_x, width_y)
    well_col = as_column(well_v[...].astype(F32)).astype(jnp.int32)
    owner_col = as_column(owner_v[...].astype(F32)).astype(jnp.int32)
    well_id = owner_col * own_wells + well_col
    member = jnp.where(
        (lax.broadcasted_iota(jnp.int32, (slots, wells), 1) == well_id) & live, 1.0, 0.0
    )
    layer_lane = lax.broadcasted_iota(jnp.int32, (slots, depth), 1)
    index = jnp.zeros((slots, depth), F32)
    for l in range(depth):
        index = jnp.where(layer_lane == l, as_column(index_v[l : l + 1, :]), index)
    rate_col = as_column(rate_v[...])
    rate_spot = (
        lax.broadcasted_iota(jnp.int32, (own_wells, wells), 1)
        == lax.broadcasted_iota(jnp.int32, (own_wells, wells), 0) + me * own_wells
    )
    rate_row = jnp.sum(jnp.where(rate_spot, rate_col, 0.0), axis=0, keepdims=True)

    def gathered(ref):
        at = jnp.zeros((slots, depth), F32)
        for l in range(depth):
            picked = jnp.dot(hot_x3, pieces(ref[l]), preferred_element_type=F32)
            one = jnp.sum(jnp.where(in_y, picked, 0.0), axis=1, keepdims=True)
            at = jnp.where(layer_lane == l, one, at)
        return at

    def well_row(at):
        share = jnp.sum(index * at, axis=1, keepdims=True)
        return jnp.sum(share * member, axis=0, keepdims=True) + rate_row

    def well_copy(it, step):
        send, recv = ((well_send0, well_recv0), (well_send1, well_recv1))[it]
        return pltpu.make_async_remote_copy(
            src_ref=send,
            dst_ref=recv.at[step],
            send_sem=well_ssem.at[it, step],
            recv_sem=well_rsem.at[it, step],
            device_id=peer(step),
            device_id_type=MESH,
        )

    sides = (
        ("gx", me_x, -1, me_x > 0),
        ("gx", me_x, 1, me_x < n_gx - 1),
        ("gy", me_y, -1, me_y > 0),
        ("gy", me_y, 1, me_y < n_gy - 1),
    )

    def halo_copy(it, side):
        axis, mine, way, _ = sides[side]
        send, recv = (row_send, row_recv) if side < 2 else (col_send, col_recv)
        width = slice(0, 2 if it == 0 else 1)
        if side < 2:
            source_ref = send.at[it, side, width]
            target_ref = recv.at[it, 1 - side, width]
        else:
            source_ref = send.at[it, side - 2]
            target_ref = recv.at[it, 3 - side]
        return pltpu.make_async_remote_copy(
            src_ref=source_ref,
            dst_ref=target_ref,
            send_sem=halo_ssem.at[it, side],
            recv_sem=halo_rsem.at[it, side ^ 1],
            device_id={axis: mine + way},
            device_id_type=MESH,
        )

    def halo_landing(it, side):
        axis, mine, way, _ = sides[side]
        if side < 2:
            width = slice(0, 2 if it == 0 else 1)
            ref, other = row_recv.at[it, side, width], row_send.at[it, 1 - side, width]
        else:
            ref, other = col_recv.at[it, side - 2], col_send.at[it, 3 - side]
        return pltpu.make_async_remote_copy(
            src_ref=other,
            dst_ref=ref,
            send_sem=halo_ssem.at[it, side],
            recv_sem=halo_rsem.at[it, side],
            device_id={axis: mine + way},
            device_id_type=MESH,
        )

    lane128 = lax.broadcasted_iota(jnp.int32, (width_x, 128), 1)

    def packed_columns(arrays, lane):
        out = jnp.zeros((width_x, 128), F32)
        at = 0
        for ref in arrays:
            for l in range(depth):
                out = jnp.where(lane128 == at, ref[l, :, lane : lane + 1], out)
                at += 1
        return out

    def stage_halos(it):
        for l in range(depth):
            row_send[it, 0, 0, l : l + 1, :] = field[l, 0:1, :]
            row_send[it, 1, 0, l : l + 1, :] = field[l, width_x - 1 : width_x, :]
            if it == 0:
                row_send[it, 0, 1, l : l + 1, :] = kx[l, 0:1, :]
                row_send[it, 1, 1, l : l + 1, :] = kx[l, width_x - 1 : width_x, :]
        arrays = (field, ky) if it == 0 else (field,)
        col_send[it, 0] = packed_columns(arrays, 0)
        col_send[it, 1] = packed_columns(arrays, width_y - 1)
        for side in range(4):

            @pl.when(jnp.logical_not(sides[side][3]))
            def _():
                if side < 2:
                    row_recv[it, side] = jnp.zeros(row_recv.shape[2:], F32)
                else:
                    col_recv[it, side - 2] = jnp.zeros(col_recv.shape[2:], F32)

    def start_halos(it):
        for side in range(4):
            @pl.when(sides[side][3])
            def _():
                halo_copy(it, side).start()

    def wait_halos(it):
        for side in range(4):
            @pl.when(sides[side][3])
            def _():
                halo_landing(it, side).wait_recv()

    last_x = lax.broadcasted_iota(jnp.int32, (width_x, width_y), 0) == width_x - 1
    first_x = lax.broadcasted_iota(jnp.int32, (width_x, width_y), 0) == 0
    last_y = lax.broadcasted_iota(jnp.int32, (width_x, width_y), 1) == width_y - 1
    first_y = lax.broadcasted_iota(jnp.int32, (width_x, width_y), 1) == 0

    def face_coefficients():
        for l in range(depth):
            mult = kx[l]
            kx[l] = 0.5 * (mult + pltpu.roll(mult, width_x - 1, 0))
            mult = ky[l]
            ky[l] = 0.5 * (mult + pltpu.roll(mult, width_y - 1, 1))

    def edge_coefficients():
        for l in range(depth):
            one = slice(l, l + 1)
            halo_mult_x[one, :] = 0.5 * (row_send[0, 0, 1, one, :] + row_recv[0, 0, 1, one, :])
            kx[l, width_x - 1 : width_x, :] = 0.5 * (
                row_send[0, 1, 1, one, :] + row_recv[0, 1, 1, one, :]
            )
            lane = slice(depth + l, depth + l + 1)
            ky[l, :, width_y - 1 : width_y] = 0.5 * (
                col_send[0, 1, :, lane] + col_recv[0, 1, :, lane]
            )
        halo_mult_y[...] = 0.5 * (col_send[0, 0] + col_recv[0, 0])

    def lateral_sum():
        for l in range(depth):
            now = field[l]
            face_x, face_y = kx[l], ky[l]
            east = jnp.where(last_x, 0.0, face_x * pltpu.roll(now, width_x - 1, 0))
            west = jnp.where(first_x, 0.0, pltpu.roll(face_x * now, 1, 0))
            north = jnp.where(last_y, 0.0, face_y * pltpu.roll(now, width_y - 1, 1))
            south = jnp.where(first_y, 0.0, pltpu.roll(face_y * now, 1, 1))
            rhs[l] = src[l] + ((east + west) + (north + south))

    def lateral_edges(it):
        end_x, end_y = slice(width_x - 1, width_x), slice(width_y - 1, width_y)
        for l in range(depth):
            one = slice(l, l + 1)
            lane = slice(depth + l, depth + l + 1)
            rhs[l, 0:1, :] += halo_mult_x[one, :] * row_recv[it, 0, 0, one, :]
            rhs[l, end_x, :] += kx[l, end_x, :] * row_recv[it, 1, 0, one, :]
            rhs[l, :, 0:1] += halo_mult_y[:, lane] * col_recv[it, 0, :, one]
            rhs[l, :, end_y] += ky[l, :, end_y] * col_recv[it, 1, :, one]

    def layer_copy(ref, target, ssem, rsem, other):
        return pltpu.make_async_remote_copy(
            src_ref=ref,
            dst_ref=target,
            send_sem=ssem,
            recv_sem=rsem,
            device_id={"layer": other},
            device_id_type=MESH,
        )

    last = depth - 1
    coef_at = ((0, 0), (0, last), (last, 0))[: 1 if groups == 2 else 3]

    def coef_copy(which, sender, other):
        i, j = coef_at[which]
        return layer_copy(
            inv.at[i, j],
            coef_recv.at[sender, which],
            coef_ssem.at[other, which],
            coef_rsem.at[sender, which],
            other,
        )

    def coef_sent(which, sender, other):
        if which == 0:
            return other < sender
        if which == 1:
            return other < sender < groups - 1
        return 0 < sender < groups - 1

    def spot_copy(step):
        return layer_copy(
            column_v, spot_recv.at[step], spot_ssem.at[step], spot_rsem.at[step],
            lax.rem(me_l + step, groups),
        )

    def delta_copy(it, step):
        return layer_copy(
            delta_send.at[it], delta_recv.at[it, step], delta_ssem.at[it, step],
            delta_rsem.at[it, step], lax.rem(me_l + step, groups),
        )

    def down_copy(it, sender, other):
        return layer_copy(
            down_send.at[it], down_recv.at[it, sender], down_ssem.at[it, other],
            down_rsem.at[it, sender], other,
        )

    def up_copy(it, sender, other):
        return layer_copy(
            up_send.at[it], up_recv.at[it, sender], up_ssem.at[it, other],
            up_rsem.at[it, sender], other,
        )

    def layer_sends(act, which):
        for g in range(groups):

            @pl.when(me_l == g)
            def _():
                for other in range(groups):
                    if other == g:
                        continue
                    if which == "coef":
                        for c in range(len(coef_at)):
                            if coef_sent(c, g, other):
                                getattr(coef_copy(c, g, other), act)()
                    else:
                        it = which
                        if g < groups - 1:
                            getattr(down_copy(it, g, other), act)()
                        if other < g:
                            getattr(up_copy(it, g, other), act)()

    def chunk_loop(body):
        def step(c, carry):
            body(pl.ds(pl.multiple_of(c * ROWS, ROWS), ROWS))
            return carry

        lax.fori_loop(0, width_x // ROWS, step, 0)

    def dot_layer(i, rows, terms):
        total = inv[i, 0, rows, :] * terms[0]
        for j in range(1, depth):
            total = total + inv[i, j, rows, :] * terms[j]
        return total

    def solve_faces(it):
        def body(rows):
            terms = [rhs[j, rows, :] for j in range(depth)]
            bottom = dot_layer(last, rows, terms)
            top = dot_layer(0, rows, terms)
            below = lower[rows, :]
            nothing = jnp.zeros_like(below)
            down_send[it, rows, :] = inv[last, 0, rows, :] * nothing + (
                (bottom + inv[last, last, rows, :] * below) - below
            )
            up_send[it, rows, :] = inv[0, last, rows, :] * nothing + top

        chunk_loop(body)

    def solve_all():
        def body(rows):
            terms = [rhs[j, rows, :] for j in range(depth)]
            for i in range(depth):
                value = dot_layer(i, rows, terms)
                solved[i, rows, :] = value
                if i == last:
                    below = lower[rows, :]
                    own_down[rows, :] = inv[last, 0, rows, :] * jnp.zeros_like(below) + (
                        (value + inv[last, last, rows, :] * below) - below
                    )

        chunk_loop(body)

    def sweeps(it):
        for g in range(groups):

            @pl.when(me_l == g)
            def _():
                for k in range(groups):
                    if k == g:
                        continue
                    if k < groups - 1:
                        down_copy(it, k, k).wait_recv()
                    if k > g:
                        up_copy(it, k, k).wait_recv()
                    if it == 0:
                        for c in range(len(coef_at)):
                            if coef_sent(c, k, g):
                                coef_copy(c, k, k).wait_recv()
                    step = (g - k) % groups
                    delta_copy(it, step).wait_recv()
                    other_y, _, other_xt3 = spots[step]
                    for row, wanted, ref in ((0, k < groups - 1, down_recv), (1, k > g, up_recv)):
                        if wanted:
                            spread = as_column(delta_recv[it, step, row : row + 1, :])
                            spread = pieces(jnp.where(other_y, spread, 0.0))
                            ref[it, k] = ref[it, k] + jnp.dot(
                                other_xt3, spread, preferred_element_type=F32
                            )

                def body(rows):
                    def coef(which, k):
                        i, j = coef_at[which]
                        return inv[i, j, rows, :] if k == g else coef_recv[k, which, rows, :]

                    above = [jnp.zeros((ROWS, width_y), F32)]
                    for k in range(groups - 1):
                        value = own_down[rows, :] if k == g else down_recv[it, k, rows, :]
                        if k > 0:
                            value = coef(2, k) * above[k] + value
                        above.append(value)
                    below = jnp.zeros((ROWS, width_y), F32)
                    for k in range(groups - 1, g, -1):
                        value = (up_recv[it, k, rows, :] + coef(0, k) * above[k]) - above[k]
                        if k < groups - 1:
                            value = coef(1, k) * below + value
                        below = value
                    upper[rows, :] = above[g]
                    lower[rows, :] = below

                chunk_loop(body)

    def update():
        def body(rows):
            above, below = upper[rows, :], lower[rows, :]
            for i in range(depth):
                field[i, rows, :] = (
                    solved[i, rows, :]
                    + inv[i, 0, rows, :] * above
                    + inv[i, last, rows, :] * below
                )

        chunk_loop(body)

    index_total = None
    spots = [None] * groups
    for it in range(ITERS):
        if it == 0:
            loads[0].wait()
        at = gathered(field)
        if it == 0:
            index_row = jnp.sum(
                jnp.sum(index, axis=1, keepdims=True) * member, axis=0, keepdims=True
            )
            well_send0[...] = jnp.concatenate([well_row(at), index_row], axis=1)
            loads[7].wait()
            loads[8].wait()
            stage_halos(it)
            pl.semaphore_wait(barrier, tiles - 1 + groups - 1)
        else:
            well_send1[...] = well_row(at)
        for step in range(1, tiles):
            well_copy(it, step).start()
        if it > 0:
            stage_halos(it)
        start_halos(it)
        if it == 0:
            for step in range(1, groups):
                spot_copy(step).start()
            for load in loads[9:]:
                load.wait()
            layer_sends("start", "coef")
        if it == 0:
            face_coefficients()
        lateral_sum()
        wait_halos(it)
        if it == 0:
            edge_coefficients()
        lateral_edges(it)
        solve_faces(it)
        layer_sends("start", it)
        if it == 0:
            for step in range(1, groups):
                spot_copy(step).wait_recv()
                spots[step] = one_hots(spot_recv[step], width_x, width_y)
            face_last, face_first = gathered(inv.at[last]), gathered(inv.at[0])
        total = (well_send0, well_send1)[it][...]
        for step in range(1, tiles):
            well_copy(it, step).wait_recv()
        for step in range(1, tiles):
            total = total + (well_recv0, well_recv1)[it][step]
        if it == 0:
            index_total = total[:, wells:] + 1.0
            total = total[:, :wells]
        bottom_hole = total / index_total
        hole = jnp.sum(member * bottom_hole, axis=1, keepdims=True)
        flow = jnp.where(live, index * (hole - at), 0.0)
        for row, face in enumerate((face_last, face_first)):
            delta_send[it, row : row + 1, :] = as_row(
                jnp.sum(face * flow, axis=1, keepdims=True)
            )
        for step in range(1, groups):
            delta_copy(it, step).start()
        if it == ITERS - 1:
            for l in range(depth):
                flow_v[l : l + 1, :] = as_row(flow[:, l : l + 1])
            flow_store = pltpu.make_async_copy(flow_v, flow_out, store_sem.at[0])
            flow_store.start()
        for l in range(depth):
            spread = jnp.where(in_y, flow[:, l : l + 1], 0.0)
            rhs[l] = rhs[l] + jnp.dot(hot_xt3, pieces(spread), preferred_element_type=F32)
        solve_all()
        sweeps(it)
        update()
    field_store = pltpu.make_async_copy(field, field_out, store_sem.at[1])
    field_store.start()
    for it in range(ITERS):
        for step in range(1, tiles):
            well_copy(it, step).wait_send()
        for side in range(4):

            @pl.when(sides[side][3])
            def _():
                halo_copy(it, side).wait_send()

        layer_sends("wait_send", it)
        for step in range(1, groups):
            delta_copy(it, step).wait_send()
    for step in range(1, groups):
        spot_copy(step).wait_send()
    layer_sends("wait_send", "coef")
    flow_store.wait()
    field_store.wait()


def split(value, count):
    out = []
    for _ in range(count - 1):
        part = value.astype(BF16).astype(F32)
        out.append(part)
        value = value - part
    out.append(value)
    return out


def fused(
    dims,
    pressure,
    source,
    perm_x,
    perm_y,
    inverse,
    robin,
    count_in,
    owner_in,
    well_in,
    column_in,
    index_in,
    rate_in,
    field,
    flow_out,
    start_at,
    rock,
    inv,
    lower,
    column_s,
    count_v,
    owner_v,
    well_v,
    column_v,
    index_v,
    rate_v,
    slabs,
    face_lines,
    lower_at,
    rhs,
    solved,
    spread,
    left,
    own,
    par,
    lines,
    at_send,
    at_recv,
    coef_x,
    coef_y,
    well_send0,
    well_recv0,
    well_send1,
    well_recv1,
    row_send,
    row_recv,
    col_send,
    col_recv,
    gain_x,
    gain_y,
    gain_xr,
    gain_yr,
    edge_send,
    edge_recv,
    edge_tile,
    edge_tile_in,
    x_send,
    x_recv,
    kappa,
    smem_sem,
    load_sem,
    rest_sem,
    well_ssem,
    well_rsem,
    side_ssem,
    halo_rsem,
    gain_rsem,
    edge_rsem,
    part_ssem,
    x_rsem,
    kappa_ssem,
    misc_rsem,
):
    groups, n_gx, n_gy, depth = dims
    tiles = n_gx * n_gy
    width_x, width_y = lower.shape
    slots = well_v.shape[1]
    own_wells = rate_v.shape[1]
    wells = tiles * own_wells
    me_l, me_x, me_y = lax.axis_index("layer"), lax.axis_index("gx"), lax.axis_index("gy")
    me = me_x * n_gy + me_y
    upper_group = me_l == 0
    phi = (1 - me_l) * (depth - 1)
    halves = width_y // LANES

    def sheet(i):
        return slice(i * width_x, (i + 1) * width_x)

    def dyn_sheet(i):
        return pl.ds(pl.multiple_of(i * width_x, width_x), width_x)

    def peer(dl, step):
        return {"layer": me_l ^ dl, "gx": me_x ^ (step // n_gy), "gy": me_y ^ (step % n_gy)}

    peers = [
        (dl, step)
        for step in reversed(range(tiles))
        for dl in reversed(range(groups))
        if (dl, step) != (0, 0)
    ]
    partner = {"layer": 1 - me_l}

    block = depth * width_x
    to_smem = pltpu.make_async_copy(column_in, column_s, smem_sem)
    to_smem.start()
    loads = [
        pltpu.make_async_copy(a, b, load_sem.at[i])
        for i, (a, b) in enumerate(
            [
                (column_in, column_v),
                (well_in, well_v),
                (owner_in, owner_v),
                (index_in, index_v),
                (count_in, count_v),
                (rate_in, rate_v),
                (robin, lower),
            ]
        )
    ]
    start_load = pltpu.make_async_copy(pressure, start_at, load_sem.at[7])
    rocks = [
        pltpu.make_async_copy(a, rock.at[n], load_sem.at[8])
        for n, a in enumerate((perm_x, perm_y, source))
    ]
    rock_loaded = pltpu.make_async_copy(rock, rock, load_sem.at[8])
    rock_x, rock_y, src = rock.at[0], rock.at[1], rock.at[2]
    barrier = pltpu.get_barrier_semaphore()
    for load in loads[:6] + [start_load]:
        load.start()
    for dl, step in peers:
        pl.semaphore_signal(barrier, inc=1, device_id=peer(dl, step), device_id_type=MESH)
    face_block = pl.ds(pl.multiple_of(phi * block, block), block)
    other_blocks = pl.ds(pl.multiple_of(me_l * block, block), (depth - 1) * block)

    def line_loads(rows, sem):
        return [
            pltpu.make_async_copy(
                inverse.at[rows, n * LANES : (n + 1) * LANES], inv.at[n, rows, :], sem
            )
            for n in range(halves)
        ]

    def lines_loaded(rows, sem):
        return pltpu.make_async_copy(inv.at[:, rows, :], inv.at[:, rows, :], sem)

    for load in rocks + line_loads(face_block, rest_sem.at[0]) + loads[6:]:
        load.start()

    lane = lax.broadcasted_iota(jnp.int32, (8, LANES), 1)
    sub = lax.broadcasted_iota(jnp.int32, (8, LANES), 0)

    own[...] = jnp.zeros(own.shape, F32)
    for load in loads[:6]:
        load.wait()
    live = lax.broadcasted_iota(jnp.int32, (depth, slots), 1) < count_v[...]
    own[0:depth, 0:slots] = jnp.where(live, index_v[...], 0.0)
    own[2 * depth : 2 * depth + 1, 0:slots] = column_v[...].astype(F32)
    own[2 * depth + 1 : 2 * depth + 2, 0:slots] = (owner_v[...] * own_wells + well_v[...]).astype(F32)
    index = own[0:depth, :]
    well_id = own[2 * depth + 1 : 2 * depth + 2, :]
    member = jnp.where(
        lax.broadcasted_iota(jnp.int32, (LANES, wells), 1).astype(F32) == as_column(well_id), 1.0, 0.0
    ).astype(BF16)
    rate_col = as_column(rate_v[...])
    rate_spot = (
        lax.broadcasted_iota(jnp.int32, (own_wells, wells), 1)
        == lax.broadcasted_iota(jnp.int32, (own_wells, wells), 0) + me * own_wells
    )
    rate_row = jnp.sum(jnp.where(rate_spot, rate_col, 0.0), axis=0, keepdims=True)

    def gather(jobs, span):
        shift = width_y.bit_length() - 1

        def step(c, accs):
            for k in range(span):
                s = c * span + k
                column = column_s[0, s]
                if width_y == 1 << shift:
                    x, y = lax.shift_right_logical(column, shift), column & (width_y - 1)
                else:
                    x, y = lax.div(column, width_y), lax.rem(column, width_y)
                tile = lax.shift_right_logical(y, LANES.bit_length() - 1)
                turn = (s + LANES - (y & (LANES - 1))) & (LANES - 1)
                found = []
                for ref, first, stride, count in jobs:
                    if count == 1:
                        value = ref[tile, pl.ds(first + x, 1), :]
                    else:
                        value = ref[tile, pl.ds(first + x, count, stride=stride), :]
                    found.append(pltpu.roll(value, turn, 1))
                accs = tuple(
                    jnp.where(lane[: value.shape[0]] == s, value, acc) for acc, value in zip(accs, found)
                )
            return accs

        accs = tuple(jnp.zeros((count, LANES), F32) for _, _, _, count in jobs)
        if span == slots:
            return step(0, accs)
        return lax.fori_loop(0, slots // span, step, accs)

    wide = lax.broadcasted_iota(jnp.int32, (16, LANES), 0)

    def binned(rows):
        at, out = 0, jnp.zeros((16, LANES), F32)
        for row in rows:
            for part in split(row, 3):
                out = jnp.where(wide == at, part, out)
                at += 1
        total = jnp.dot(out.astype(BF16), member, preferred_element_type=F32)
        return [jnp.sum(total[3 * k : 3 * k + 3, :], axis=0, keepdims=True) for k in range(len(rows))]

    def remote(a, b, ssem, rsem, device):
        return pltpu.make_async_remote_copy(
            src_ref=a, dst_ref=b, send_sem=ssem, recv_sem=rsem, device_id=device, device_id_type=MESH
        )

    def well_copy(it, dl, step):
        send, recv = ((well_send0, well_recv0), (well_send1, well_recv1))[it]
        return remote(
            send, recv.at[dl * tiles + step - 1], well_ssem.at[it], well_rsem.at[it], peer(dl, step)
        )

    def all_wells(it):
        recv = (well_recv0, well_recv1)[it]
        return remote(recv, recv, well_ssem.at[it], well_rsem.at[it], partner)

    sides = (
        ("gx", me_x, -1, me_x > 0),
        ("gx", me_x, 1, me_x < n_gx - 1),
        ("gy", me_y, -1, me_y > 0),
        ("gy", me_y, 1, me_y < n_gy - 1),
    )

    def across(side, flip=False):
        axis, mine, way, _ = sides[side]
        out = {axis: mine + way}
        if flip:
            out["layer"] = 1 - me_l
        return out

    def halo_copy(it, side, landing=False):
        other = side ^ 1
        at, to = (other, side) if landing else (side, other)
        width = slice(0, 2 if it == 0 else 1)
        if side < 2:
            a, b = row_send.at[it, at, width], row_recv.at[it, to, width]
        else:
            a, b = col_send.at[it, at - 2], col_recv.at[it, to - 2]
        return remote(a, b, side_ssem.at[at], halo_rsem.at[it, to], across(side))

    def gain_copy(side, landing=False):
        other = side ^ 1
        at, to = (other, side) if landing else (side, other)
        if side < 2:
            a, b = gain_x.at[at], gain_xr.at[to]
        else:
            a, b = gain_y.at[at - 2], gain_yr.at[to - 2]
        return remote(a, b, side_ssem.at[at], gain_rsem.at[to], across(side))

    def edge_copy(side, landing=False):
        other = side ^ 1
        at, to = (other, side) if landing else (side, other)
        return remote(
            edge_send.at[at], edge_recv.at[to], side_ssem.at[at], edge_rsem.at[to],
            across(side, True),
        )

    def edge_pack():
        return remote(edge_tile, edge_tile_in, part_ssem, edge_rsem.at[4], partner)

    def x_copy(it):
        return remote(x_send.at[it], x_recv.at[it], part_ssem, x_rsem.at[it], partner)

    slot_copy = remote(own, par, part_ssem, misc_rsem.at[0], partner)
    at_copy = remote(at_send, at_recv, part_ssem, misc_rsem.at[1], partner)
    kappa_copy = remote(inv.at[:, 0:width_x, :], kappa, kappa_ssem, misc_rsem.at[2], partner)

    lane_x = lax.broadcasted_iota(jnp.int32, (width_x, LANES), 1)

    def packed_columns(blocks, y):
        out = jnp.zeros((width_x, LANES), F32)
        for at, (ref, rows) in enumerate(blocks):
            tile = y - y % LANES
            value = ref[rows, tile : tile + LANES]
            out = jnp.where(lane_x == at, pltpu.roll(value, (at - y) % LANES, 1), out)
        return out

    def each(ref):
        return [(ref, sheet(l)) for l in range(depth)]

    ends_x, ends_y = (0, width_x - 1), (0, width_y - 1)

    def stage_halos(it):
        for side, x in enumerate(ends_x):
            for l in range(depth):
                row = l * width_x + x
                row_send[it, side, 0, l : l + 1, :] = (field if it else start_at)[row : row + 1, :]
                if it == 0:
                    row_send[it, side, 1, l : l + 1, :] = rock_x[row : row + 1, :]
        blocks = each(field) if it else each(start_at) + each(rock_y)
        for side, y in enumerate(ends_y):
            col_send[it, side] = packed_columns(blocks, y)

    def clear_halos(it):
        for side in range(4):

            @pl.when(jnp.logical_not(sides[side][3]))
            def _():
                if side < 2:
                    row_recv[it, side] = jnp.zeros(row_recv.shape[2:], F32)
                else:
                    col_recv[it, side - 2] = jnp.zeros(col_recv.shape[2:], F32)
                if it == 1:
                    edge_recv[side] = jnp.zeros(edge_recv.shape[1:], F32)

    def on_sides(body):
        for side in range(4):
            pl.when(sides[side][3])(functools.partial(body, side))

    first_x = lax.broadcasted_iota(jnp.int32, (width_x, width_y), 0) == width_x - 1
    first_y = lax.broadcasted_iota(jnp.int32, (width_x, width_y), 1) == width_y - 1

    def face_coefficients():
        for l in range(depth):
            mult = rock_x[sheet(l), :]
            rock_x[sheet(l), :] = jnp.where(first_x, 0.0, 0.5 * (mult + pltpu.roll(mult, width_x - 1, 0)))
            mult = rock_y[sheet(l), :]
            rock_y[sheet(l), :] = jnp.where(first_y, 0.0, 0.5 * (mult + pltpu.roll(mult, width_y - 1, 1)))

    def lateral_sum(now_at):
        for l in range(depth):
            now = now_at[sheet(l), :]
            face_x, face_y = rock_x[sheet(l), :], rock_y[sheet(l), :]
            east = face_x * pltpu.roll(now, width_x - 1, 0)
            west = pltpu.roll(face_x * now, 1, 0)
            north = face_y * pltpu.roll(now, width_y - 1, 1)
            south = pltpu.roll(face_y * now, 1, 1)
            rhs[sheet(l), :] = src[sheet(l), :] + ((east + west) + (north + south))

    def lateral_edges(it):
        for l in range(depth):
            one = slice(l, l + 1)
            for side, x in enumerate(ends_x):
                row = slice(l * width_x + x, l * width_x + x + 1)
                rhs[row, :] += coef_x[side, one, :] * row_recv[it, side, 0, one, :]
        for side, y in enumerate(ends_y):
            tile = y - y % LANES
            terms = coef_y[side] * col_recv[it, side]
            for l in range(depth):
                term = pltpu.roll(terms, (y - l) % LANES, 1)
                rhs[sheet(l), tile : tile + LANES] += jnp.where(lane_x == y - tile, term, 0.0)

    def edge_coefficients():
        for side in range(2):
            coef_x[side] = 0.5 * (row_send[0, side, 1] + row_recv[0, side, 1])
            coef_y[side] = pltpu.roll(
                0.5 * (col_send[0, side] + col_recv[0, side]), LANES - depth, 1
            )

    def chunk_loop(body):
        chunks = width_x // ROWS
        together = math.gcd(chunks, 4)

        def step(c, carry):
            for k in range(together):
                body(pl.multiple_of((c * together + k) * ROWS, ROWS))
            return carry

        lax.fori_loop(0, chunks // together, step, 0)

    def whole(ref, rows):
        return jnp.concatenate([ref[n, rows, :] for n in range(halves)], axis=1)

    def rows_of(i, at):
        return pl.ds(pl.multiple_of(i * width_x + at, ROWS), ROWS)

    def own_face(at):
        below = lower[pl.ds(at, ROWS), :]
        corner = whole(inv, rows_of(phi * depth + phi, at))
        return jnp.where(upper_group, corner * below - below, 0.0)

    def interior_face(it):
        def body(at):
            total = own_face(at)
            for j in range(depth):
                total = total + whole(inv, rows_of(phi * depth + j, at)) * rhs[rows_of(j, at), :]
            x_send[it, pl.ds(at, ROWS), :] = total

        chunk_loop(body)

    def solve_all():
        def body(at):
            terms = [rhs[rows_of(j, at), :] for j in range(depth)]
            for i in range(depth):
                total = whole(inv, rows_of(i * depth, at)) * terms[0]
                for j in range(1, depth):
                    total = total + whole(inv, rows_of(i * depth + j, at)) * terms[j]
                for n in range(halves):
                    solved[n, rows_of(i, at), :] = total[:, n * LANES : (n + 1) * LANES]

        chunk_loop(body)

    def inner_face(it, at):
        mine = whole(solved, rows_of(phi, at)) + own_face(at)
        return x_recv[it, pl.ds(at, ROWS), :] + jnp.where(
            upper_group, whole(kappa, pl.ds(at, ROWS)) * mine - mine, 0.0
        )

    def interior_data(it):
        def body(at):
            data = inner_face(it, at)
            lower[pl.ds(at, ROWS), :] = data
            for n in range(halves if it == 0 else 0):
                lower_at[n, pl.ds(at, ROWS), :] = data[:, n * LANES : (n + 1) * LANES]

        chunk_loop(body)

    def add_edges(ref, rows, columns):
        for x, row in zip(ends_x, rows):
            ref[x : x + 1, :] += row
        for y, column in zip(ends_y, columns):
            tile = y - y % LANES
            column = as_column(column)
            ref[:, tile : tile + LANES] += jnp.where(lane_x == y - tile, column, 0.0)

    to_smem.wait()
    start_load.wait()
    for load in line_loads(other_blocks, rest_sem.at[1]):
        load.start()
    for n in range(halves):
        slabs[n] = start_at[:, n * LANES : (n + 1) * LANES]
    at_own = gather([(slabs, 0, width_x, depth)], slots)[0]
    own[depth : 2 * depth, :] = at_own
    share, sums = binned(
        [jnp.sum(index * at_own, axis=0, keepdims=True), jnp.sum(index, axis=0, keepdims=True)]
    )
    well_send0[...] = jnp.concatenate([share + rate_row, sums], axis=1)
    clear_halos(0)
    clear_halos(1)
    rock_loaded.wait()
    stage_halos(0)
    loads[6].wait()
    lines_loaded(face_block, rest_sem.at[0]).wait()
    for n in range(halves):
        face_lines[n] = inv[n, face_block, :]
    own[3 * depth : 4 * depth, :] = gather([(face_lines, 0, width_x, depth)], slots)[0]
    pl.semaphore_wait(barrier, len(peers))
    for dl, step in peers:
        well_copy(0, dl, step).start()
    slot_copy.start()
    on_sides(lambda side: halo_copy(0, side).start())

    @pl.when(me_l == 1)
    def _():
        kappa_copy.start()
        kappa[...] = jnp.zeros(kappa.shape, F32)

    face_coefficients()
    lateral_sum(start_at)
    interior_face(0)
    x_copy(0).start()

    for side, x in enumerate(ends_x):
        for j in range(depth):
            gain_x[side, j : j + 1, :] = whole(inv, pl.ds((phi * depth + j) * width_x + x, 1))
    for side, y in enumerate(ends_y):
        n = y // LANES
        face = packed_columns(
            [(inv.at[n], dyn_sheet(phi * depth + j)) for j in range(depth)], y - n * LANES
        )
        gain_y[side] = jnp.where(lane_x < depth, face, 0.0)
    lines_loaded(other_blocks, rest_sem.at[1]).wait()

    def gather_lines(columns):
        found = gather([(inv, j * width_x, block, depth) for j in columns], 16)
        for j, value in zip(columns, found):
            lines[j] = value

    gather_lines(range(depth - 2))
    edge_tile[...] = jnp.zeros(edge_tile.shape, F32)
    on_sides(lambda side: halo_copy(0, side, True).wait_recv())
    edge_coefficients()
    for side in range(2):
        gain_x[side] = gain_x[side] * coef_x[side]
        edge = jnp.sum(gain_x[side] * row_recv[0, side, 0], axis=0, keepdims=True)
        for n in range(halves):
            edge_tile[side * halves + n : side * halves + n + 1, :] = edge[:, n * LANES : (n + 1) * LANES]
    for side in range(2):
        gain = gain_y[side] * coef_y[side]
        gain_y[side] = gain
        row = 2 * halves + side
        edge_tile[row : row + 1, 0:width_x] = as_row(
            jnp.sum(gain * col_recv[0, side], axis=1, keepdims=True)
        )
    edge_pack().start()
    gather_lines(range(depth - 2, depth))
    lateral_edges(0)
    solve_all()
    on_sides(lambda side: gain_copy(side).start())

    half = LANES // 2
    slot_copy.wait_recv()
    both = own[0 : 3 * depth, :] + pltpu.roll(par[0 : 3 * depth, :], half, 1)
    index2, at2 = both[0:depth], both[depth : 2 * depth]
    column_row, wells_row = both[2 * depth : 2 * depth + 1], both[2 * depth + 1 : 2 * depth + 2]
    wells_at = jnp.broadcast_to(wells_row, (8, LANES)).astype(jnp.int32)
    column_col = as_column(column_row)
    same = jnp.where(column_col == column_row, 1.0, 0.0).astype(BF16)

    def x_of(column):
        return jnp.floor((column + 0.5) * (1.0 / width_y))

    y_col = column_col - x_of(column_col) * width_y
    hot_y = jnp.where(
        lax.broadcasted_iota(jnp.int32, (LANES, width_y), 1).astype(F32) == y_col, 1.0, 0.0
    ).astype(BF16)
    hot_y = jnp.concatenate([hot_y, hot_y], axis=0)
    in_x = lax.broadcasted_iota(jnp.int32, (width_x, LANES), 0).astype(F32) == x_of(column_row)
    lower_half = lane < half
    x_row = x_of(column_row)
    y_row = column_row - x_row * width_y
    x_all, y_all = (jnp.broadcast_to(v, (8, LANES)).astype(jnp.int32) for v in (x_row, y_row))
    edge_lanes = jnp.where(sub < 2 * halves, y_all & (LANES - 1), x_all)
    edge_spots = jnp.zeros((8, LANES), jnp.int32)
    for side, x in enumerate(ends_x):
        for n in range(halves):
            here = (x_all == x) & (y_all >= n * LANES) & (y_all < (n + 1) * LANES)
            edge_spots = jnp.where((sub == side * halves + n) & here, 1, edge_spots)
    for side, y in enumerate(ends_y):
        edge_spots = jnp.where((sub == 2 * halves + side) & (y_all == y), 1, edge_spots)
    edge_spots = edge_spots > 0
    face_par = pltpu.roll(par[3 * depth : 4 * depth, :], half, 1)

    def well_totals(it):
        send, recv = ((well_send0, well_recv0), (well_send1, well_recv1))[it]
        all_wells(it).wait_recv()
        mine, other = send[...], recv[tiles - 1]
        for step in range(1, tiles):
            mine, other = mine + recv[step - 1], other + recv[tiles + step - 1]
        return mine, other

    def flows(mine, other, at_slots):
        def at_wells(row):
            return jnp.take_along_axis(
                jnp.broadcast_to(row, (8, LANES)), wells_at, axis=1, mode="promise_in_bounds"
            )

        hole = jnp.where(lower_half, at_wells(mine), at_wells(other))
        return index2 * (hole - at_slots)

    def responses(flow):
        change = jnp.zeros((depth, LANES), F32)
        for j in range(depth):
            change = change + lines[j] * flow[j : j + 1, :]
        out = jnp.sum(jnp.where(sub == phi, change, 0.0), axis=0, keepdims=True)
        theirs = jnp.sum(face_par * flow, axis=0, keepdims=True)
        return change, out, theirs

    def spread_out(change, data):
        order = [depth] + list(range(depth))
        for first in range(0, depth + 1, 3):
            some = order[first : first + 3]
            rows = slice(first * width_x, (first + len(some)) * width_x)
            for n, i in enumerate(some):
                row = change[i : i + 1, :] if i < depth else data
                left[sheet(first + n), :] = jnp.concatenate(
                    [jnp.where(in_x, part, 0.0).astype(BF16) for part in split(row, 2)], axis=1
                )
            spread[rows, :] = jnp.dot(left[rows, :], hot_y, preferred_element_type=F32)

    def update():
        lower[...] = lower[...] + spread[sheet(0), :]
        for i in range(depth):
            field[sheet(i), :] = (
                whole(solved, sheet(i))
                + spread[sheet(i + 1), :]
                + whole(inv, dyn_sheet(i * depth + phi)) * lower[...]
            )

    (solved_at,) = gather([(solved, 0, width_x, depth)], slots)
    mine, other = well_totals(0)
    index_mine, index_other = mine[:, wells:] + 1.0, other[:, wells:] + 1.0
    flow = flows(mine[:, :wells] / index_mine, other[:, :wells] / index_other, at2)
    change, out, theirs = responses(flow)

    @pl.when(upper_group)
    def _():
        kappa_copy.wait_recv()

    x_copy(0).wait_recv()
    interior_data(0)
    data_at, kappa_at = gather([(lower_at, 0, 1, 1), (kappa, 0, 1, 1)], slots)
    kappa_gain = jnp.where(upper_group & lower_half[0:1], kappa_at - 1.0, 0.0)
    data = kappa_gain * out + theirs
    edge_pack().wait_recv()
    edges = edge_tile_in[...]
    data_at = data_at + jnp.sum(
        jnp.where(
            edge_spots,
            jnp.take_along_axis(edges, edge_lanes, axis=1, mode="promise_in_bounds"),
            0.0,
        ),
        axis=0,
        keepdims=True,
    )
    stack = jnp.concatenate([change, jnp.broadcast_to(data, (8, LANES))], axis=0)
    pile = jnp.concatenate(split(stack, 3), axis=0).astype(BF16)
    summed = jnp.dot(pile, same, preferred_element_type=F32)
    summed = (summed[0:16] + summed[16:32]) + summed[32:48]
    at_own = (solved_at + summed[0:8]) + lines[phi] * (data_at + summed[8:9])
    at_send[...] = at_own
    (share,) = binned([jnp.sum(index * at_own, axis=0, keepdims=True)])
    well_send1[...] = share + rate_row
    for dl, step in peers:
        well_copy(1, dl, step).start()
    at_copy.start()
    spread_out(change, data)
    add_edges(
        lower,
        [
            jnp.concatenate([edges[side * halves + n : side * halves + n + 1] for n in range(halves)], axis=1)
            for side in range(2)
        ],
        [edges[2 * halves + side : 2 * halves + side + 1, 0:width_x] for side in range(2)],
    )
    update()

    lateral_sum(field)
    interior_face(1)
    x_copy(1).start()
    stage_halos(1)
    on_sides(lambda side: halo_copy(1, side).start())
    on_sides(lambda side: gain_copy(side, True).wait_recv())
    for side in range(4):

        @pl.when(sides[side][3])
        def _():
            if side < 2:
                edge = jnp.sum(gain_xr[side] * row_send[1, side, 0], axis=0, keepdims=True)
                for n in range(halves):
                    edge_send[side, n : n + 1, :] = edge[:, n * LANES : (n + 1) * LANES]
            else:
                edge_send[side, 0:1, 0:width_x] = as_row(
                    jnp.sum(gain_yr[side - 2] * col_send[1, side - 2], axis=1, keepdims=True)
                )
            edge_copy(side).start()

    on_sides(lambda side: halo_copy(1, side, True).wait_recv())
    lateral_edges(1)
    solve_all()
    at_copy.wait_recv()
    at2 = jnp.where(lower_half, at_own, pltpu.roll(at_recv[...], half, 1))
    mine, other = well_totals(1)
    flow = flows(mine / index_mine, other / index_other, at2)
    flow_out[...] = flow[:, 0:slots]
    change, out, theirs = responses(flow)
    spread_out(change, kappa_gain * out + theirs)
    x_copy(1).wait_recv()
    on_sides(lambda side: edge_copy(side, True).wait_recv())
    add_edges(
        x_recv.at[1],
        [
            jnp.concatenate([edge_recv[side, n : n + 1, :] for n in range(halves)], axis=1)
            for side in range(2)
        ],
        [edge_recv[2 + side, 0:1, 0:width_x] for side in range(2)],
    )
    interior_data(1)
    update()

    def sent(sem, buffers):
        rows = sum(math.prod(b.shape) for b in buffers) // LANES
        span = solved.at[0, 0:rows, :]
        remote(span, span, sem, sem, partner).wait_send()

    def side_sent(side):
        if side < 2:
            pieces = [row_send.at[0, 0], row_send.at[0, 0, 0], gain_x.at[0], edge_send.at[0]]
        else:
            pieces = [col_send.at[0, 0], col_send.at[0, 0], gain_y.at[0], edge_send.at[0]]
        sent(side_ssem.at[side], pieces)

    for it in range(ITERS):
        all_wells(it).wait_send()
    on_sides(side_sent)
    sent(part_ssem, [own, edge_tile, at_send, x_send])

    @pl.when(me_l == 1)
    def _():
        kappa_copy.wait_send()


def fused_shards(arrays, dims):
    (
        pressure, source, perm_x, perm_y, line_inverse, robin_below,
        tile_count, perf_owner, perf_well, perf_column, perf_index, well_rate,
    ) = arrays
    groups, n_gx, n_gy = dims
    depth, width_x, width_y = pressure.shape
    tiles = n_gx * n_gy
    slots = perf_well.shape[1]
    own_wells = well_rate.shape[1]
    wells = tiles * own_wells
    sheet = (width_x, width_y)
    stack = (depth * width_x, width_y)
    halves = width_y // LANES
    HBM = pl.BlockSpec(memory_space=pltpu.HBM)
    VMEM = pl.BlockSpec(memory_space=pltpu.VMEM)
    anywhere = pl.BlockSpec(memory_space=pl.ANY)
    dma = pltpu.SemaphoreType.DMA
    i32 = jnp.int32

    def vmem(*shape):
        return pltpu.VMEM(shape, F32)

    call = pl.pallas_call(
        functools.partial(fused, (groups, n_gx, n_gy, depth)),
        out_shape=(jax.ShapeDtypeStruct(stack, F32), jax.ShapeDtypeStruct((depth, slots), F32)),
        in_specs=[HBM] * 12,
        out_specs=(VMEM, VMEM),
        scratch_shapes=[
            vmem(*stack),
            vmem(3, *stack),
            vmem(halves, depth * depth * width_x, LANES),
            vmem(*sheet),
            pltpu.SMEM((1, slots), i32),
            pltpu.VMEM((1, 1), i32),
            pltpu.VMEM((1, slots), i32),
            pltpu.VMEM((1, slots), i32),
            pltpu.VMEM((1, slots), i32),
            vmem(depth, slots),
            vmem(1, own_wells),
            vmem(halves, depth * width_x, LANES),
            vmem(halves, depth * width_x, LANES),
            vmem(halves, width_x, LANES),
            vmem(*stack),
            vmem(halves, depth * width_x, LANES),
            vmem((depth + 1) * width_x, width_y),
            pltpu.VMEM(((depth + 1) * width_x, 2 * LANES), BF16),
            vmem(4 * depth, LANES),
            vmem(4 * depth, LANES),
            vmem(depth, depth, LANES),
            vmem(depth, LANES),
            vmem(depth, LANES),
            vmem(2, depth, width_y),
            vmem(2, width_x, LANES),
            vmem(1, 2 * wells),
            vmem(groups * tiles - 1, 1, 2 * wells),
            vmem(1, wells),
            vmem(groups * tiles - 1, 1, wells),
            vmem(ITERS, 2, 2, depth, width_y),
            vmem(ITERS, 2, 2, depth, width_y),
            vmem(ITERS, 2, width_x, LANES),
            vmem(ITERS, 2, width_x, LANES),
            vmem(2, depth, width_y),
            vmem(2, width_x, LANES),
            vmem(2, depth, width_y),
            vmem(2, width_x, LANES),
            vmem(4, depth, LANES),
            vmem(4, depth, LANES),
            vmem(depth, LANES),
            vmem(depth, LANES),
            vmem(ITERS, *sheet),
            vmem(ITERS, *sheet),
            vmem(halves, width_x, LANES),
            dma,
            dma((9,)),
            dma((2,)),
            dma((ITERS,)),
            dma((ITERS,)),
            dma((4,)),
            dma((ITERS, 4)),
            dma((4,)),
            dma((5,)),
            dma,
            dma((ITERS,)),
            dma,
            dma((3,)),
        ],
        compiler_params=pltpu.CompilerParams(
            collective_id=0, has_side_effects=True, vmem_limit_bytes=LIMIT
        ),
        name="window",
    )
    operands = (
        pressure.reshape(stack),
        source.reshape(stack),
        perm_x.reshape(stack),
        perm_y.reshape(stack),
        line_inverse.reshape(depth * depth * width_x, width_y),
        robin_below[0],
        tile_count,
        perf_owner[:, :, 0],
        perf_well,
        perf_column,
        perf_index[0].T,
        well_rate,
    )
    field, flow = call(
        *[x if x.size == 1 else pltpu.with_memory_space_constraint(x, pltpu.HBM) for x in operands]
    )
    field, flow = pl.pallas_call(
        keep,
        out_shape=(
            jax.ShapeDtypeStruct(field.shape, F32),
            jax.ShapeDtypeStruct(flow.shape, F32),
        ),
        in_specs=[anywhere] * 2,
        out_specs=(HBM, HBM),
        scratch_shapes=[dma((2,))],
        compiler_params=pltpu.CompilerParams(vmem_limit_bytes=1 << 20),
        name="keep",
    )(field, flow)
    return field.reshape(pressure.shape), flow.T[None]


def shards(
    pressure,
    source,
    perm_x,
    perm_y,
    line_inverse,
    robin_below,
    tile_count,
    perf_owner,
    perf_well,
    perf_column,
    perf_index,
    well_rate,
):
    depth, width_x, width_y = pressure.shape
    groups, n_gx, n_gy = (lax.axis_size(a) for a in ("layer", "gx", "gy"))
    tiles = n_gx * n_gy
    slots = perf_well.shape[1]
    own_wells = well_rate.shape[1]
    wells = tiles * own_wells
    powers = all(n == 1 << (n.bit_length() - 1) for n in (n_gx, n_gy))
    if (
        groups == 2
        and depth == 8
        and wells == LANES
        and slots <= LANES // 2
        and slots % 16 == 0
        and width_x <= LANES
        and width_y % LANES == 0
        and 2 * (width_y // LANES) + 2 <= depth
        and powers
    ):
        arrays = (
            pressure, source, perm_x, perm_y, line_inverse, robin_below,
            tile_count, perf_owner, perf_well, perf_column, perf_index, well_rate,
        )
        return fused_shards(arrays, (groups, n_gx, n_gy))
    sheet = (width_x, width_y)
    coefs = 1 if groups == 2 else 3
    HBM = pl.BlockSpec(memory_space=pltpu.HBM)
    anywhere = pl.BlockSpec(memory_space=pl.ANY)
    dma = pltpu.SemaphoreType.DMA
    i32 = jnp.int32
    call = pl.pallas_call(
        functools.partial(kernel, (groups, n_gx, n_gy)),
        out_shape=(
            jax.ShapeDtypeStruct(pressure.shape, F32),
            jax.ShapeDtypeStruct((depth, slots), F32),
        ),
        in_specs=[HBM] * 12,
        out_specs=(anywhere, anywhere),
        scratch_shapes=[
            pltpu.VMEM(pressure.shape, F32),
            pltpu.VMEM(pressure.shape, F32),
            pltpu.VMEM(pressure.shape, F32),
            pltpu.VMEM(pressure.shape, F32),
            pltpu.VMEM((depth, depth) + sheet, F32),
            pltpu.VMEM(sheet, F32),
            pltpu.VMEM((1, 1), i32),
            pltpu.VMEM((1, slots), i32),
            pltpu.VMEM((1, slots), i32),
            pltpu.VMEM((1, slots), i32),
            pltpu.VMEM((depth, slots), F32),
            pltpu.VMEM((1, own_wells), F32),
            pltpu.VMEM(sheet, F32),
            pltpu.VMEM(pressure.shape, F32),
            pltpu.VMEM(pressure.shape, F32),
            pltpu.VMEM((depth, slots), F32),
            pltpu.VMEM((depth, width_y), F32),
            pltpu.VMEM((width_x, 128), F32),
            pltpu.VMEM((1, 2 * wells), F32),
            pltpu.VMEM((tiles, 1, 2 * wells), F32),
            pltpu.VMEM((1, wells), F32),
            pltpu.VMEM((tiles, 1, wells), F32),
            pltpu.VMEM((ITERS, 2, 2, depth, width_y), F32),
            pltpu.VMEM((ITERS, 2, 2, depth, width_y), F32),
            pltpu.VMEM((ITERS, 2, width_x, 128), F32),
            pltpu.VMEM((ITERS, 2, width_x, 128), F32),
            pltpu.VMEM((groups, coefs) + sheet, F32),
            pltpu.VMEM((ITERS,) + sheet, F32),
            pltpu.VMEM((ITERS, groups) + sheet, F32),
            pltpu.VMEM((ITERS,) + sheet, F32),
            pltpu.VMEM((ITERS, groups) + sheet, F32),
            pltpu.VMEM(sheet, F32),
            pltpu.VMEM((groups, 1, slots), i32),
            pltpu.VMEM((ITERS, 2, slots), F32),
            pltpu.VMEM((ITERS, groups, 2, slots), F32),
            dma((12,)),
            dma((2,)),
            dma((ITERS, tiles)),
            dma((ITERS, tiles)),
            dma((ITERS, 4)),
            dma((ITERS, 4)),
            dma((groups, coefs)),
            dma((groups, coefs)),
            dma((ITERS, groups)),
            dma((ITERS, groups)),
            dma((ITERS, groups)),
            dma((ITERS, groups)),
            dma((groups,)),
            dma((groups,)),
            dma((ITERS, groups)),
            dma((ITERS, groups)),
        ],
        compiler_params=pltpu.CompilerParams(collective_id=0, has_side_effects=True, vmem_limit_bytes=LIMIT),
        name="window",
    )
    operands = (
        pressure,
        source,
        perm_x,
        perm_y,
        line_inverse[0],
        robin_below[0],
        tile_count,
        perf_owner[:, :, 0],
        perf_well,
        perf_column,
        perf_index[0].T,
        well_rate,
    )
    field, flow = call(
        *[x if x.size == 1 else pltpu.with_memory_space_constraint(x, pltpu.HBM) for x in operands]
    )
    field, flow = pl.pallas_call(
        keep,
        out_shape=(
            jax.ShapeDtypeStruct(field.shape, F32),
            jax.ShapeDtypeStruct(flow.shape, F32),
        ),
        in_specs=[anywhere] * 2,
        out_specs=(HBM, HBM),
        scratch_shapes=[dma((2,))],
        compiler_params=pltpu.CompilerParams(vmem_limit_bytes=1 << 20),
        name="keep",
    )(field, flow)
    return field, flow.T[None]


def solution(mesh):
    placed = (
        P("layer", "gx", "gy"),
        P("layer", "gx", "gy"),
        P("layer", "gx", "gy"),
        P("layer", "gx", "gy"),
        P("layer", None, None, "gx", "gy"),
        P("layer", "gx", "gy"),
        P("layer", ("gx", "gy")),
        P("layer", ("gx", "gy"), None),
        P("layer", ("gx", "gy")),
        P("layer", ("gx", "gy")),
        P("layer", ("gx", "gy"), None),
        P("layer", ("gx", "gy")),
    )
    return jax.shard_map(
        shards,
        mesh=mesh,
        in_specs=placed,
        out_specs=(P("layer", "gx", "gy"), P("layer", ("gx", "gy"), None)),
        check_vma=False,
    )
```

```python
import functools
import math

import jax
import jax.numpy as jnp
from jax import lax
from jax.experimental import pallas as pl
from jax.experimental.pallas import tpu as pltpu
from jax.sharding import PartitionSpec as P

ITERS = 2
LIMIT = 24 << 20
MESH = pl.DeviceIdType.MESH
F32 = jnp.float32
BF16 = jnp.bfloat16
ROWS = 8
LANES = 128
PACK = 16


def pieces(value):
    high = value.astype(BF16)
    rest = value - high.astype(F32)
    middle = rest.astype(BF16)
    low = (rest - middle.astype(F32)).astype(BF16)
    return jnp.concatenate([high, middle, low], axis=0)


def as_column(row):
    n = row.shape[1]
    eye = lax.broadcasted_iota(jnp.int32, (n, n), 0) == lax.broadcasted_iota(jnp.int32, (n, n), 1)
    return jnp.sum(jnp.where(eye, jnp.broadcast_to(row, (n, n)), 0.0), axis=1, keepdims=True)


def as_row(column):
    n = column.shape[0]
    eye = lax.broadcasted_iota(jnp.int32, (n, n), 0) == lax.broadcasted_iota(jnp.int32, (n, n), 1)
    return jnp.sum(jnp.where(eye, jnp.broadcast_to(column, (n, n)), 0.0), axis=0, keepdims=True)


def one_hots(column_row, width_x, width_y):
    slots = column_row.shape[1]
    column_col = as_column(column_row.astype(F32)).astype(jnp.int32)
    lane_x = lax.broadcasted_iota(jnp.int32, (slots, width_x), 1)
    in_x = (column_col >= lane_x * width_y) & (column_col < lane_x * width_y + width_y)
    x_of = jnp.sum(jnp.where(in_x, lane_x.astype(F32), 0.0), axis=1, keepdims=True).astype(jnp.int32)
    in_y = lax.broadcasted_iota(jnp.int32, (slots, width_y), 1) == column_col - x_of * width_y
    hot_x = jnp.where(in_x, 1.0, 0.0).astype(BF16)
    row_x = lax.broadcasted_iota(jnp.int32, (width_x, slots), 0)
    hot_xt = jnp.where(
        (column_row >= row_x * width_y) & (column_row < row_x * width_y + width_y), 1.0, 0.0
    ).astype(BF16)
    return in_y, jnp.concatenate([hot_x] * 3, axis=1), jnp.concatenate([hot_xt] * 3, axis=1)


def keep(field_in, flow_in, field_out, flow_out, sem):
    copies = [
        pltpu.make_async_copy(field_in, field_out, sem.at[0]),
        pltpu.make_async_copy(flow_in, flow_out, sem.at[1]),
    ]
    for copy in copies:
        copy.start()
    for copy in copies:
        copy.wait()


def kernel(
    dims,
    pressure,
    source,
    perm_x,
    perm_y,
    inverse,
    robin,
    count_in,
    owner_in,
    well_in,
    column_in,
    index_in,
    rate_in,
    field_out,
    flow_out,
    field,
    src,
    kx,
    ky,
    inv,
    lower,
    count_v,
    owner_v,
    well_v,
    column_v,
    index_v,
    rate_v,
    upper,
    rhs,
    solved,
    flow_v,
    halo_mult_x,
    halo_mult_y,
    well_send0,
    well_recv0,
    well_send1,
    well_recv1,
    row_send,
    row_recv,
    col_send,
    col_recv,
    coef_recv,
    down_send,
    down_recv,
    up_send,
    up_recv,
    own_down,
    spot_recv,
    delta_send,
    delta_recv,
    load_sem,
    store_sem,
    well_ssem,
    well_rsem,
    halo_ssem,
    halo_rsem,
    coef_ssem,
    coef_rsem,
    down_ssem,
    down_rsem,
    up_ssem,
    up_rsem,
    spot_ssem,
    spot_rsem,
    delta_ssem,
    delta_rsem,
):
    groups, n_gx, n_gy = dims
    tiles = n_gx * n_gy
    depth, width_x, width_y = field.shape
    slots = well_v.shape[1]
    own_wells = rate_v.shape[1]
    wells = tiles * own_wells
    me_l, me_x, me_y = lax.axis_index("layer"), lax.axis_index("gx"), lax.axis_index("gy")
    me = me_x * n_gy + me_y

    loads = [
        pltpu.make_async_copy(a, b, load_sem.at[i])
        for i, (a, b) in enumerate(
            [
                (pressure, field),
                (column_in, column_v),
                (well_in, well_v),
                (owner_in, owner_v),
                (index_in, index_v),
                (count_in, count_v),
                (rate_in, rate_v),
                (perm_x, kx),
                (perm_y, ky),
                (source, src),
                (robin, lower),
                (inverse, inv),
            ]
        )
    ]
    for load in loads:
        load.start()

    def peer(step):
        other = lax.rem(me + step, tiles)
        return {"gx": lax.div(other, n_gy), "gy": lax.rem(other, n_gy)}

    barrier = pltpu.get_barrier_semaphore()
    for step in range(1, tiles):
        pl.semaphore_signal(barrier, inc=1, device_id=peer(step), device_id_type=MESH)
    for step in range(1, groups):
        pl.semaphore_signal(
            barrier, inc=1, device_id={"layer": lax.rem(me_l + step, groups)}, device_id_type=MESH
        )

    for load in loads[1:7]:
        load.wait()
    live = lax.broadcasted_iota(jnp.int32, (slots, 1), 0) < count_v[...]
    in_y, hot_x3, hot_xt3 = one_hots(column_v[...], width_x, width_y)
    well_col = as_column(well_v[...].astype(F32)).astype(jnp.int32)
    owner_col = as_column(owner_v[...].astype(F32)).astype(jnp.int32)
    well_id = owner_col * own_wells + well_col
    member = jnp.where(
        (lax.broadcasted_iota(jnp.int32, (slots, wells), 1) == well_id) & live, 1.0, 0.0
    )
    layer_lane = lax.broadcasted_iota(jnp.int32, (slots, depth), 1)
    index = jnp.zeros((slots, depth), F32)
    for l in range(depth):
        index = jnp.where(layer_lane == l, as_column(index_v[l : l + 1, :]), index)
    rate_col = as_column(rate_v[...])
    rate_spot = (
        lax.broadcasted_iota(jnp.int32, (own_wells, wells), 1)
        == lax.broadcasted_iota(jnp.int32, (own_wells, wells), 0) + me * own_wells
    )
    rate_row = jnp.sum(jnp.where(rate_spot, rate_col, 0.0), axis=0, keepdims=True)

    def gathered(ref):
        at = jnp.zeros((slots, depth), F32)
        for l in range(depth):
            picked = jnp.dot(hot_x3, pieces(ref[l]), preferred_element_type=F32)
            one = jnp.sum(jnp.where(in_y, picked, 0.0), axis=1, keepdims=True)
            at = jnp.where(layer_lane == l, one, at)
        return at

    def well_row(at):
        share = jnp.sum(index * at, axis=1, keepdims=True)
        return jnp.sum(share * member, axis=0, keepdims=True) + rate_row

    def well_copy(it, step):
        send, recv = ((well_send0, well_recv0), (well_send1, well_recv1))[it]
        return pltpu.make_async_remote_copy(
            src_ref=send,
            dst_ref=recv.at[step],
            send_sem=well_ssem.at[it, step],
            recv_sem=well_rsem.at[it, step],
            device_id=peer(step),
            device_id_type=MESH,
        )

    sides = (
        ("gx", me_x, -1, me_x > 0),
        ("gx", me_x, 1, me_x < n_gx - 1),
        ("gy", me_y, -1, me_y > 0),
        ("gy", me_y, 1, me_y < n_gy - 1),
    )

    def halo_copy(it, side):
        axis, mine, way, _ = sides[side]
        send, recv = (row_send, row_recv) if side < 2 else (col_send, col_recv)
        width = slice(0, 2 if it == 0 else 1)
        if side < 2:
            source_ref = send.at[it, side, width]
            target_ref = recv.at[it, 1 - side, width]
        else:
            source_ref = send.at[it, side - 2]
            target_ref = recv.at[it, 3 - side]
        return pltpu.make_async_remote_copy(
            src_ref=source_ref,
            dst_ref=target_ref,
            send_sem=halo_ssem.at[it, side],
            recv_sem=halo_rsem.at[it, side ^ 1],
            device_id={axis: mine + way},
            device_id_type=MESH,
        )

    def halo_landing(it, side):
        axis, mine, way, _ = sides[side]
        if side < 2:
            width = slice(0, 2 if it == 0 else 1)
            ref, other = row_recv.at[it, side, width], row_send.at[it, 1 - side, width]
        else:
            ref, other = col_recv.at[it, side - 2], col_send.at[it, 3 - side]
        return pltpu.make_async_remote_copy(
            src_ref=other,
            dst_ref=ref,
            send_sem=halo_ssem.at[it, side],
            recv_sem=halo_rsem.at[it, side],
            device_id={axis: mine + way},
            device_id_type=MESH,
        )

    lane128 = lax.broadcasted_iota(jnp.int32, (width_x, 128), 1)

    def packed_columns(arrays, lane):
        out = jnp.zeros((width_x, 128), F32)
        at = 0
        for ref in arrays:
            for l in range(depth):
                out = jnp.where(lane128 == at, ref[l, :, lane : lane + 1], out)
                at += 1
        return out

    def stage_halos(it):
        for l in range(depth):
            row_send[it, 0, 0, l : l + 1, :] = field[l, 0:1, :]
            row_send[it, 1, 0, l : l + 1, :] = field[l, width_x - 1 : width_x, :]
            if it == 0:
                row_send[it, 0, 1, l : l + 1, :] = kx[l, 0:1, :]
                row_send[it, 1, 1, l : l + 1, :] = kx[l, width_x - 1 : width_x, :]
        arrays = (field, ky) if it == 0 else (field,)
        col_send[it, 0] = packed_columns(arrays, 0)
        col_send[it, 1] = packed_columns(arrays, width_y - 1)
        for side in range(4):

            @pl.when(jnp.logical_not(sides[side][3]))
            def _():
                if side < 2:
                    row_recv[it, side] = jnp.zeros(row_recv.shape[2:], F32)
                else:
                    col_recv[it, side - 2] = jnp.zeros(col_recv.shape[2:], F32)

    def start_halos(it):
        for side in range(4):
            @pl.when(sides[side][3])
            def _():
                halo_copy(it, side).start()

    def wait_halos(it):
        for side in range(4):
            @pl.when(sides[side][3])
            def _():
                halo_landing(it, side).wait_recv()

    last_x = lax.broadcasted_iota(jnp.int32, (width_x, width_y), 0) == width_x - 1
    first_x = lax.broadcasted_iota(jnp.int32, (width_x, width_y), 0) == 0
    last_y = lax.broadcasted_iota(jnp.int32, (width_x, width_y), 1) == width_y - 1
    first_y = lax.broadcasted_iota(jnp.int32, (width_x, width_y), 1) == 0

    def face_coefficients():
        for l in range(depth):
            mult = kx[l]
            kx[l] = 0.5 * (mult + pltpu.roll(mult, width_x - 1, 0))
            mult = ky[l]
            ky[l] = 0.5 * (mult + pltpu.roll(mult, width_y - 1, 1))

    def edge_coefficients():
        for l in range(depth):
            one = slice(l, l + 1)
            halo_mult_x[one, :] = 0.5 * (row_send[0, 0, 1, one, :] + row_recv[0, 0, 1, one, :])
            kx[l, width_x - 1 : width_x, :] = 0.5 * (
                row_send[0, 1, 1, one, :] + row_recv[0, 1, 1, one, :]
            )
            lane = slice(depth + l, depth + l + 1)
            ky[l, :, width_y - 1 : width_y] = 0.5 * (
                col_send[0, 1, :, lane] + col_recv[0, 1, :, lane]
            )
        halo_mult_y[...] = 0.5 * (col_send[0, 0] + col_recv[0, 0])

    def lateral_sum():
        for l in range(depth):
            now = field[l]
            face_x, face_y = kx[l], ky[l]
            east = jnp.where(last_x, 0.0, face_x * pltpu.roll(now, width_x - 1, 0))
            west = jnp.where(first_x, 0.0, pltpu.roll(face_x * now, 1, 0))
            north = jnp.where(last_y, 0.0, face_y * pltpu.roll(now, width_y - 1, 1))
            south = jnp.where(first_y, 0.0, pltpu.roll(face_y * now, 1, 1))
            rhs[l] = src[l] + ((east + west) + (north + south))

    def lateral_edges(it):
        end_x, end_y = slice(width_x - 1, width_x), slice(width_y - 1, width_y)
        for l in range(depth):
            one = slice(l, l + 1)
            lane = slice(depth + l, depth + l + 1)
            rhs[l, 0:1, :] += halo_mult_x[one, :] * row_recv[it, 0, 0, one, :]
            rhs[l, end_x, :] += kx[l, end_x, :] * row_recv[it, 1, 0, one, :]
            rhs[l, :, 0:1] += halo_mult_y[:, lane] * col_recv[it, 0, :, one]
            rhs[l, :, end_y] += ky[l, :, end_y] * col_recv[it, 1, :, one]

    def layer_copy(ref, target, ssem, rsem, other):
        return pltpu.make_async_remote_copy(
            src_ref=ref,
            dst_ref=target,
            send_sem=ssem,
            recv_sem=rsem,
            device_id={"layer": other},
            device_id_type=MESH,
        )

    last = depth - 1
    coef_at = ((0, 0), (0, last), (last, 0))[: 1 if groups == 2 else 3]

    def coef_copy(which, sender, other):
        i, j = coef_at[which]
        return layer_copy(
            inv.at[i, j],
            coef_recv.at[sender, which],
            coef_ssem.at[other, which],
            coef_rsem.at[sender, which],
            other,
        )

    def coef_sent(which, sender, other):
        if which == 0:
            return other < sender
        if which == 1:
            return other < sender < groups - 1
        return 0 < sender < groups - 1

    def spot_copy(step):
        return layer_copy(
            column_v, spot_recv.at[step], spot_ssem.at[step], spot_rsem.at[step],
            lax.rem(me_l + step, groups),
        )

    def delta_copy(it, step):
        return layer_copy(
            delta_send.at[it], delta_recv.at[it, step], delta_ssem.at[it, step],
            delta_rsem.at[it, step], lax.rem(me_l + step, groups),
        )

    def down_copy(it, sender, other):
        return layer_copy(
            down_send.at[it], down_recv.at[it, sender], down_ssem.at[it, other],
            down_rsem.at[it, sender], other,
        )

    def up_copy(it, sender, other):
        return layer_copy(
            up_send.at[it], up_recv.at[it, sender], up_ssem.at[it, other],
            up_rsem.at[it, sender], other,
        )

    def layer_sends(act, which):
        for g in range(groups):

            @pl.when(me_l == g)
            def _():
                for other in range(groups):
                    if other == g:
                        continue
                    if which == "coef":
                        for c in range(len(coef_at)):
                            if coef_sent(c, g, other):
                                getattr(coef_copy(c, g, other), act)()
                    else:
                        it = which
                        if g < groups - 1:
                            getattr(down_copy(it, g, other), act)()
                        if other < g:
                            getattr(up_copy(it, g, other), act)()

    def chunk_loop(body):
        def step(c, carry):
            body(pl.ds(pl.multiple_of(c * ROWS, ROWS), ROWS))
            return carry

        lax.fori_loop(0, width_x // ROWS, step, 0)

    def dot_layer(i, rows, terms):
        total = inv[i, 0, rows, :] * terms[0]
        for j in range(1, depth):
            total = total + inv[i, j, rows, :] * terms[j]
        return total

    def solve_faces(it):
        def body(rows):
            terms = [rhs[j, rows, :] for j in range(depth)]
            bottom = dot_layer(last, rows, terms)
            top = dot_layer(0, rows, terms)
            below = lower[rows, :]
            nothing = jnp.zeros_like(below)
            down_send[it, rows, :] = inv[last, 0, rows, :] * nothing + (
                (bottom + inv[last, last, rows, :] * below) - below
            )
            up_send[it, rows, :] = inv[0, last, rows, :] * nothing + top

        chunk_loop(body)

    def solve_all():
        def body(rows):
            terms = [rhs[j, rows, :] for j in range(depth)]
            for i in range(depth):
                value = dot_layer(i, rows, terms)
                solved[i, rows, :] = value
                if i == last:
                    below = lower[rows, :]
                    own_down[rows, :] = inv[last, 0, rows, :] * jnp.zeros_like(below) + (
                        (value + inv[last, last, rows, :] * below) - below
                    )

        chunk_loop(body)

    def sweeps(it):
        for g in range(groups):

            @pl.when(me_l == g)
            def _():
                for k in range(groups):
                    if k == g:
                        continue
                    if k < groups - 1:
                        down_copy(it, k, k).wait_recv()
                    if k > g:
                        up_copy(it, k, k).wait_recv()
                    if it == 0:
                        for c in range(len(coef_at)):
                            if coef_sent(c, k, g):
                                coef_copy(c, k, k).wait_recv()
                    step = (g - k) % groups
                    delta_copy(it, step).wait_recv()
                    other_y, _, other_xt3 = spots[step]
                    for row, wanted, ref in ((0, k < groups - 1, down_recv), (1, k > g, up_recv)):
                        if wanted:
                            spread = as_column(delta_recv[it, step, row : row + 1, :])
                            spread = pieces(jnp.where(other_y, spread, 0.0))
                            ref[it, k] = ref[it, k] + jnp.dot(
                                other_xt3, spread, preferred_element_type=F32
                            )

                def body(rows):
                    def coef(which, k):
                        i, j = coef_at[which]
                        return inv[i, j, rows, :] if k == g else coef_recv[k, which, rows, :]

                    above = [jnp.zeros((ROWS, width_y), F32)]
                    for k in range(groups - 1):
                        value = own_down[rows, :] if k == g else down_recv[it, k, rows, :]
                        if k > 0:
                            value = coef(2, k) * above[k] + value
                        above.append(value)
                    below = jnp.zeros((ROWS, width_y), F32)
                    for k in range(groups - 1, g, -1):
                        value = (up_recv[it, k, rows, :] + coef(0, k) * above[k]) - above[k]
                        if k < groups - 1:
                            value = coef(1, k) * below + value
                        below = value
                    upper[rows, :] = above[g]
                    lower[rows, :] = below

                chunk_loop(body)

    def update():
        def body(rows):
            above, below = upper[rows, :], lower[rows, :]
            for i in range(depth):
                field[i, rows, :] = (
                    solved[i, rows, :]
                    + inv[i, 0, rows, :] * above
                    + inv[i, last, rows, :] * below
                )

        chunk_loop(body)

    index_total = None
    spots = [None] * groups
    for it in range(ITERS):
        if it == 0:
            loads[0].wait()
        at = gathered(field)
        if it == 0:
            index_row = jnp.sum(
                jnp.sum(index, axis=1, keepdims=True) * member, axis=0, keepdims=True
            )
            well_send0[...] = jnp.concatenate([well_row(at), index_row], axis=1)
            loads[7].wait()
            loads[8].wait()
            stage_halos(it)
            pl.semaphore_wait(barrier, tiles - 1 + groups - 1)
        else:
            well_send1[...] = well_row(at)
        for step in range(1, tiles):
            well_copy(it, step).start()
        if it > 0:
            stage_halos(it)
        start_halos(it)
        if it == 0:
            for step in range(1, groups):
                spot_copy(step).start()
            for load in loads[9:]:
                load.wait()
            layer_sends("start", "coef")
        if it == 0:
            face_coefficients()
        lateral_sum()
        wait_halos(it)
        if it == 0:
            edge_coefficients()
        lateral_edges(it)
        solve_faces(it)
        layer_sends("start", it)
        if it == 0:
            for step in range(1, groups):
                spot_copy(step).wait_recv()
                spots[step] = one_hots(spot_recv[step], width_x, width_y)
            face_last, face_first = gathered(inv.at[last]), gathered(inv.at[0])
        total = (well_send0, well_send1)[it][...]
        for step in range(1, tiles):
            well_copy(it, step).wait_recv()
        for step in range(1, tiles):
            total = total + (well_recv0, well_recv1)[it][step]
        if it == 0:
            index_total = total[:, wells:] + 1.0
            total = total[:, :wells]
        bottom_hole = total / index_total
        hole = jnp.sum(member * bottom_hole, axis=1, keepdims=True)
        flow = jnp.where(live, index * (hole - at), 0.0)
        for row, face in enumerate((face_last, face_first)):
            delta_send[it, row : row + 1, :] = as_row(
                jnp.sum(face * flow, axis=1, keepdims=True)
            )
        for step in range(1, groups):
            delta_copy(it, step).start()
        if it == ITERS - 1:
            for l in range(depth):
                flow_v[l : l + 1, :] = as_row(flow[:, l : l + 1])
            flow_store = pltpu.make_async_copy(flow_v, flow_out, store_sem.at[0])
            flow_store.start()
        for l in range(depth):
            spread = jnp.where(in_y, flow[:, l : l + 1], 0.0)
            rhs[l] = rhs[l] + jnp.dot(hot_xt3, pieces(spread), preferred_element_type=F32)
        solve_all()
        sweeps(it)
        update()
    field_store = pltpu.make_async_copy(field, field_out, store_sem.at[1])
    field_store.start()
    for it in range(ITERS):
        for step in range(1, tiles):
            well_copy(it, step).wait_send()
        for side in range(4):

            @pl.when(sides[side][3])
            def _():
                halo_copy(it, side).wait_send()

        layer_sends("wait_send", it)
        for step in range(1, groups):
            delta_copy(it, step).wait_send()
    for step in range(1, groups):
        spot_copy(step).wait_send()
    layer_sends("wait_send", "coef")
    flow_store.wait()
    field_store.wait()


def split(value, count):
    out = []
    for _ in range(count - 1):
        part = value.astype(BF16).astype(F32)
        out.append(part)
        value = value - part
    out.append(value)
    return out


def fused(
    dims,
    pressure,
    source,
    perm_x,
    perm_y,
    inverse,
    robin,
    count_in,
    owner_in,
    well_in,
    column_in,
    index_in,
    rate_in,
    field,
    flow_out,
    start_at,
    rock,
    inv,
    lower,
    column_s,
    count_v,
    owner_v,
    well_v,
    column_v,
    index_v,
    rate_v,
    slabs,
    face_lines,
    lower_at,
    rhs,
    solved,
    spread,
    left,
    own,
    par,
    lines,
    at_send,
    at_recv,
    coef_x,
    coef_y,
    well_send0,
    well_recv0,
    well_send1,
    well_recv1,
    row_send,
    row_recv,
    col_send,
    col_recv,
    gain_x,
    gain_y,
    gain_xr,
    gain_yr,
    edge_send,
    edge_recv,
    edge_tile,
    edge_tile_in,
    x_send,
    x_recv,
    kappa,
    smem_sem,
    load_sem,
    rest_sem,
    well_ssem,
    well_rsem,
    side_ssem,
    halo_rsem,
    gain_rsem,
    edge_rsem,
    part_ssem,
    x_rsem,
    kappa_ssem,
    misc_rsem,
):
    groups, n_gx, n_gy, depth = dims
    tiles = n_gx * n_gy
    width_x, width_y = lower.shape
    slots = well_v.shape[1]
    own_wells = rate_v.shape[1]
    wells = tiles * own_wells
    me_l, me_x, me_y = lax.axis_index("layer"), lax.axis_index("gx"), lax.axis_index("gy")
    me = me_x * n_gy + me_y
    upper_group = me_l == 0
    phi = (1 - me_l) * (depth - 1)
    halves = width_y // LANES

    def sheet(i):
        return slice(i * width_x, (i + 1) * width_x)

    def dyn_sheet(i):
        return pl.ds(pl.multiple_of(i * width_x, width_x), width_x)

    def peer(dl, step):
        return {"layer": me_l ^ dl, "gx": me_x ^ (step // n_gy), "gy": me_y ^ (step % n_gy)}

    peers = [
        (dl, step)
        for step in reversed(range(tiles))
        for dl in reversed(range(groups))
        if (dl, step) != (0, 0)
    ]
    partner = {"layer": 1 - me_l}

    block = depth * width_x
    to_smem = pltpu.make_async_copy(column_in, column_s, smem_sem)
    to_smem.start()
    loads = [
        pltpu.make_async_copy(a, b, load_sem.at[i])
        for i, (a, b) in enumerate(
            [
                (column_in, column_v),
                (well_in, well_v),
                (owner_in, owner_v),
                (index_in, index_v),
                (count_in, count_v),
                (rate_in, rate_v),
                (robin, lower),
            ]
        )
    ]
    start_load = pltpu.make_async_copy(pressure, start_at, load_sem.at[7])
    rocks = [
        pltpu.make_async_copy(a, rock.at[n], load_sem.at[8])
        for n, a in enumerate((perm_x, perm_y, source))
    ]
    rock_loaded = pltpu.make_async_copy(rock, rock, load_sem.at[8])
    rock_x, rock_y, src = rock.at[0], rock.at[1], rock.at[2]
    barrier = pltpu.get_barrier_semaphore()
    for load in loads[:6] + [start_load]:
        load.start()
    for dl, step in peers:
        pl.semaphore_signal(barrier, inc=1, device_id=peer(dl, step), device_id_type=MESH)
    face_block = pl.ds(pl.multiple_of(phi * block, block), block)
    other_blocks = pl.ds(pl.multiple_of(me_l * block, block), (depth - 1) * block)

    def line_loads(rows, sem):
        return [
            pltpu.make_async_copy(
                inverse.at[rows, n * LANES : (n + 1) * LANES], inv.at[n, rows, :], sem
            )
            for n in range(halves)
        ]

    def lines_loaded(rows, sem):
        return pltpu.make_async_copy(inv.at[:, rows, :], inv.at[:, rows, :], sem)

    for load in rocks + line_loads(face_block, rest_sem.at[0]) + loads[6:]:
        load.start()

    lane = lax.broadcasted_iota(jnp.int32, (8, LANES), 1)
    sub = lax.broadcasted_iota(jnp.int32, (8, LANES), 0)

    own[...] = jnp.zeros(own.shape, F32)
    for load in loads[:6]:
        load.wait()
    live = lax.broadcasted_iota(jnp.int32, (depth, slots), 1) < count_v[...]
    own[0:depth, 0:slots] = jnp.where(live, index_v[...], 0.0)
    own[2 * depth : 2 * depth + 1, 0:slots] = column_v[...].astype(F32)
    own[2 * depth + 1 : 2 * depth + 2, 0:slots] = (owner_v[...] * own_wells + well_v[...]).astype(F32)
    index = own[0:depth, :]
    well_id = own[2 * depth + 1 : 2 * depth + 2, :]
    member = jnp.where(
        lax.broadcasted_iota(jnp.int32, (LANES, wells), 1).astype(F32) == as_column(well_id), 1.0, 0.0
    ).astype(BF16)
    rate_col = as_column(rate_v[...])
    rate_spot = (
        lax.broadcasted_iota(jnp.int32, (own_wells, wells), 1)
        == lax.broadcasted_iota(jnp.int32, (own_wells, wells), 0) + me * own_wells
    )
    rate_row = jnp.sum(jnp.where(rate_spot, rate_col, 0.0), axis=0, keepdims=True)

    def gather(jobs, span):
        shift = width_y.bit_length() - 1

        def step(c, accs):
            for k in range(span):
                s = c * span + k
                column = column_s[0, s]
                if width_y == 1 << shift:
                    x, y = lax.shift_right_logical(column, shift), column & (width_y - 1)
                else:
                    x, y = lax.div(column, width_y), lax.rem(column, width_y)
                tile = lax.shift_right_logical(y, LANES.bit_length() - 1)
                turn = (s + LANES - (y & (LANES - 1))) & (LANES - 1)
                found = []
                for ref, first, stride, count in jobs:
                    if count == 1:
                        value = ref[tile, pl.ds(first + x, 1), :]
                    else:
                        value = ref[tile, pl.ds(first + x, count, stride=stride), :]
                    found.append(pltpu.roll(value, turn, 1))
                accs = tuple(
                    jnp.where(lane[: value.shape[0]] == s, value, acc) for acc, value in zip(accs, found)
                )
            return accs

        accs = tuple(jnp.zeros((count, LANES), F32) for _, _, _, count in jobs)
        if span == slots:
            return step(0, accs)
        return lax.fori_loop(0, slots // span, step, accs)

    wide = lax.broadcasted_iota(jnp.int32, (16, LANES), 0)

    def binned(rows):
        at, out = 0, jnp.zeros((16, LANES), F32)
        for row in rows:
            for part in split(row, 3):
                out = jnp.where(wide == at, part, out)
                at += 1
        total = jnp.dot(out.astype(BF16), member, preferred_element_type=F32)
        return [jnp.sum(total[3 * k : 3 * k + 3, :], axis=0, keepdims=True) for k in range(len(rows))]

    def remote(a, b, ssem, rsem, device):
        return pltpu.make_async_remote_copy(
            src_ref=a, dst_ref=b, send_sem=ssem, recv_sem=rsem, device_id=device, device_id_type=MESH
        )

    def well_copy(it, dl, step):
        send, recv = ((well_send0, well_recv0), (well_send1, well_recv1))[it]
        return remote(
            send, recv.at[dl * tiles + step - 1], well_ssem.at[it], well_rsem.at[it], peer(dl, step)
        )

    def all_wells(it):
        recv = (well_recv0, well_recv1)[it]
        return remote(recv, recv, well_ssem.at[it], well_rsem.at[it], partner)

    sides = (
        ("gx", me_x, -1, me_x > 0),
        ("gx", me_x, 1, me_x < n_gx - 1),
        ("gy", me_y, -1, me_y > 0),
        ("gy", me_y, 1, me_y < n_gy - 1),
    )

    def across(side, flip=False):
        axis, mine, way, _ = sides[side]
        out = {axis: mine + way}
        if flip:
            out["layer"] = 1 - me_l
        return out

    def halo_copy(it, side, landing=False):
        other = side ^ 1
        at, to = (other, side) if landing else (side, other)
        width = slice(0, 2 if it == 0 else 1)
        if side < 2:
            a, b = row_send.at[it, at, width], row_recv.at[it, to, width]
        else:
            a, b = col_send.at[it, at - 2], col_recv.at[it, to - 2]
        return remote(a, b, side_ssem.at[at], halo_rsem.at[it, to], across(side))

    def gain_copy(side, landing=False):
        other = side ^ 1
        at, to = (other, side) if landing else (side, other)
        if side < 2:
            a, b = gain_x.at[at], gain_xr.at[to]
        else:
            a, b = gain_y.at[at - 2], gain_yr.at[to - 2]
        return remote(a, b, side_ssem.at[at], gain_rsem.at[to], across(side))

    def edge_copy(side, landing=False):
        other = side ^ 1
        at, to = (other, side) if landing else (side, other)
        return remote(
            edge_send.at[at], edge_recv.at[to], side_ssem.at[at], edge_rsem.at[to],
            across(side, True),
        )

    def edge_pack():
        return remote(edge_tile, edge_tile_in, part_ssem, edge_rsem.at[4], partner)

    def x_copy(it):
        return remote(x_send.at[it], x_recv.at[it], part_ssem, x_rsem.at[it], partner)

    slot_copy = remote(own, par, part_ssem, misc_rsem.at[0], partner)
    at_copy = remote(at_send, at_recv, part_ssem, misc_rsem.at[1], partner)
    kappa_copy = remote(inv.at[:, 0:width_x, :], kappa, kappa_ssem, misc_rsem.at[2], partner)

    lane_x = lax.broadcasted_iota(jnp.int32, (width_x, LANES), 1)

    parts = width_x // ROWS

    def packed_columns(blocks, y):
        out = jnp.zeros((ROWS, LANES), F32)
        tile = y - y % LANES
        for at, (ref, first) in enumerate(blocks):
            for n in range(parts):
                value = ref[pl.ds(first + n * ROWS, ROWS), tile : tile + LANES]
                to = n * PACK + at
                out = jnp.where(lane == to, pltpu.roll(value, (to - y) % LANES, 1), out)
        return out

    entry = lax.broadcasted_iota(jnp.int32, (LANES, LANES), 0)
    cell = lax.broadcasted_iota(jnp.int32, (LANES, LANES), 1)
    own_entries = ((entry & (PACK - 1)) < depth) & ((entry >> (PACK.bit_length() - 1)) == (cell >> 3))
    own_entries = jnp.where(own_entries, 1.0, 0.0).astype(BF16)

    def column_sums(values):
        pile = jnp.concatenate([part for value in values for part in split(value, 3)], axis=0)
        total = jnp.dot(pile.astype(BF16), own_entries, preferred_element_type=F32)
        at_row = (lane & (ROWS - 1)) == sub
        rows = []
        for n in range(len(values)):
            some = [total[(3 * n + k) * ROWS : (3 * n + k + 1) * ROWS] for k in range(3)]
            picked = jnp.where(at_row, (some[0] + some[1]) + some[2], 0.0)
            rows.append(jnp.sum(picked, axis=0, keepdims=True)[:, 0:width_x])
        return rows

    def each(ref):
        return [(ref, l * width_x) for l in range(depth)]

    ends_x, ends_y = (0, width_x - 1), (0, width_y - 1)

    def stage_halos(it):
        for side, x in enumerate(ends_x):
            for l in range(depth):
                row = l * width_x + x
                row_send[it, side, 0, l : l + 1, :] = (field if it else start_at)[row : row + 1, :]
                if it == 0:
                    row_send[it, side, 1, l : l + 1, :] = rock_x[row : row + 1, :]
        blocks = each(field) if it else each(start_at) + each(rock_y)
        for side, y in enumerate(ends_y):
            col_send[it, side] = packed_columns(blocks, y)

    def clear_halos(it):
        for side in range(4):

            @pl.when(jnp.logical_not(sides[side][3]))
            def _():
                if side < 2:
                    row_recv[it, side] = jnp.zeros(row_recv.shape[2:], F32)
                else:
                    col_recv[it, side - 2] = jnp.zeros(col_recv.shape[2:], F32)
                if it == 1:
                    if side < 2:
                        gain_xr[side] = jnp.zeros(gain_xr.shape[1:], F32)
                    else:
                        gain_yr[side - 2] = jnp.zeros(gain_yr.shape[1:], F32)
                    edge_recv[side] = jnp.zeros(edge_recv.shape[1:], F32)

    def on_sides(body):
        for side in range(4):
            pl.when(sides[side][3])(functools.partial(body, side))

    first_x = lax.broadcasted_iota(jnp.int32, (width_x, width_y), 0) == width_x - 1
    first_y = lax.broadcasted_iota(jnp.int32, (width_x, width_y), 1) == width_y - 1

    def face_coefficients():
        for l in range(depth):
            mult = rock_x[sheet(l), :]
            rock_x[sheet(l), :] = jnp.where(first_x, 0.0, 0.5 * (mult + pltpu.roll(mult, width_x - 1, 0)))
            mult = rock_y[sheet(l), :]
            rock_y[sheet(l), :] = jnp.where(first_y, 0.0, 0.5 * (mult + pltpu.roll(mult, width_y - 1, 1)))

    def lateral_sum(now_at):
        for l in range(depth):
            now = now_at[sheet(l), :]
            face_x, face_y = rock_x[sheet(l), :], rock_y[sheet(l), :]
            east = face_x * pltpu.roll(now, width_x - 1, 0)
            west = pltpu.roll(face_x * now, 1, 0)
            north = face_y * pltpu.roll(now, width_y - 1, 1)
            south = pltpu.roll(face_y * now, 1, 1)
            rhs[sheet(l), :] = src[sheet(l), :] + ((east + west) + (north + south))

    def lateral_edges(it):
        for l in range(depth):
            one = slice(l, l + 1)
            for side, x in enumerate(ends_x):
                row = slice(l * width_x + x, l * width_x + x + 1)
                rhs[row, :] += coef_x[side, one, :] * row_recv[it, side, 0, one, :]
        for side, y in enumerate(ends_y):
            tile = y - y % LANES
            terms = coef_y[side] * col_recv[it, side]
            for l in range(depth):
                for n in range(parts):
                    term = pltpu.roll(terms, (y - n * PACK - l) % LANES, 1)
                    rows = slice(l * width_x + n * ROWS, l * width_x + (n + 1) * ROWS)
                    rhs[rows, tile : tile + LANES] += jnp.where(lane == y - tile, term, 0.0)

    def edge_coefficients():
        for side in range(2):
            coef_x[side] = 0.5 * (row_send[0, side, 1] + row_recv[0, side, 1])
            coef_y[side] = pltpu.roll(
                0.5 * (col_send[0, side] + col_recv[0, side]), LANES - depth, 1
            )

    def chunk_loop(body):
        chunks = width_x // ROWS
        together = math.gcd(chunks, 4)

        def step(c, carry):
            for k in range(together):
                body(pl.multiple_of((c * together + k) * ROWS, ROWS))
            return carry

        lax.fori_loop(0, chunks // together, step, 0)

    def whole(ref, rows):
        return jnp.concatenate([ref[n, rows, :] for n in range(halves)], axis=1)

    def rows_of(i, at):
        return pl.ds(pl.multiple_of(i * width_x + at, ROWS), ROWS)

    def own_face(at):
        below = lower[pl.ds(at, ROWS), :]
        corner = whole(inv, rows_of(phi * depth + phi, at))
        return jnp.where(upper_group, corner * below - below, 0.0)

    def interior_face(it):
        def body(at):
            total = own_face(at)
            for j in range(depth):
                total = total + whole(inv, rows_of(phi * depth + j, at)) * rhs[rows_of(j, at), :]
            x_send[it, pl.ds(at, ROWS), :] = total

        chunk_loop(body)

    def solve_all():
        def body(at):
            terms = [rhs[rows_of(j, at), :] for j in range(depth)]
            for i in range(depth):
                total = whole(inv, rows_of(i * depth, at)) * terms[0]
                for j in range(1, depth):
                    total = total + whole(inv, rows_of(i * depth + j, at)) * terms[j]
                for n in range(halves):
                    solved[n, rows_of(i, at), :] = total[:, n * LANES : (n + 1) * LANES]

        chunk_loop(body)

    def inner_face(it, at):
        mine = whole(solved, rows_of(phi, at)) + own_face(at)
        return x_recv[it, pl.ds(at, ROWS), :] + jnp.where(
            upper_group, whole(kappa, pl.ds(at, ROWS)) * mine - mine, 0.0
        )

    def interior_data(it):
        def body(at):
            data = inner_face(it, at)
            lower[pl.ds(at, ROWS), :] = data
            for n in range(halves if it == 0 else 0):
                lower_at[n, pl.ds(at, ROWS), :] = data[:, n * LANES : (n + 1) * LANES]

        chunk_loop(body)

    def add_edges(ref, rows, columns):
        for x, row in zip(ends_x, rows):
            ref[x : x + 1, :] += row
        for y, column in zip(ends_y, columns):
            tile = y - y % LANES
            column = as_column(column)
            ref[:, tile : tile + LANES] += jnp.where(lane_x == y - tile, column, 0.0)

    to_smem.wait()
    start_load.wait()
    for load in line_loads(other_blocks, rest_sem.at[1]):
        load.start()
    for n in range(halves):
        slabs[n] = start_at[:, n * LANES : (n + 1) * LANES]
    at_own = gather([(slabs, 0, width_x, depth)], slots)[0]
    own[depth : 2 * depth, :] = at_own
    share, index_sums = binned(
        [jnp.sum(index * at_own, axis=0, keepdims=True), jnp.sum(index, axis=0, keepdims=True)]
    )
    well_send0[...] = jnp.concatenate([share + rate_row, index_sums], axis=1)
    clear_halos(0)
    clear_halos(1)
    rock_loaded.wait()
    stage_halos(0)
    loads[6].wait()
    lines_loaded(face_block, rest_sem.at[0]).wait()
    for n in range(halves):
        face_lines[n] = inv[n, face_block, :]
    own[3 * depth : 4 * depth, :] = gather([(face_lines, 0, width_x, depth)], slots)[0]
    pl.semaphore_wait(barrier, len(peers))
    on_sides(lambda side: halo_copy(0, side).start())
    slot_copy.start()
    for dl, step in peers:
        well_copy(0, dl, step).start()

    @pl.when(me_l == 1)
    def _():
        kappa_copy.start()
        kappa[...] = jnp.zeros(kappa.shape, F32)

    face_coefficients()
    lateral_sum(start_at)
    interior_face(0)
    x_copy(0).start()

    for side, x in enumerate(ends_x):
        for j in range(depth):
            gain_x[side, j : j + 1, :] = whole(inv, pl.ds((phi * depth + j) * width_x + x, 1))
    for side, y in enumerate(ends_y):
        n = y // LANES
        face = packed_columns(
            [(inv.at[n], pl.multiple_of((phi * depth + j) * width_x, width_x)) for j in range(depth)],
            y - n * LANES,
        )
        gain_y[side] = jnp.where((lane & (PACK - 1)) < depth, face, 0.0)
    lines_loaded(other_blocks, rest_sem.at[1]).wait()

    def gather_lines(columns):
        found = gather([(inv, j * width_x, block, depth) for j in columns], 16)
        for j, value in zip(columns, found):
            lines[j] = value

    gather_lines(range(depth - 2))
    edge_tile[...] = jnp.zeros(edge_tile.shape, F32)
    on_sides(lambda side: halo_copy(0, side, True).wait_recv())
    edge_coefficients()
    for side in range(2):
        gain_x[side] = gain_x[side] * coef_x[side]
        edge = jnp.sum(gain_x[side] * row_recv[0, side, 0], axis=0, keepdims=True)
        for n in range(halves):
            edge_tile[side * halves + n : side * halves + n + 1, :] = edge[:, n * LANES : (n + 1) * LANES]
    sums = column_sums([gain_y[side] * coef_y[side] * col_recv[0, side] for side in range(2)])
    for side in range(2):
        gain_y[side] = gain_y[side] * coef_y[side]
        row = 2 * halves + side
        edge_tile[row : row + 1, 0:width_x] = sums[side]
    edge_pack().start()
    gather_lines(range(depth - 2, depth))
    lateral_edges(0)
    solve_all()
    on_sides(lambda side: gain_copy(side).start())

    half = LANES // 2
    slot_copy.wait_recv()
    both = own[0 : 3 * depth, :] + pltpu.roll(par[0 : 3 * depth, :], half, 1)
    index2, at2 = both[0:depth], both[depth : 2 * depth]
    column_row, wells_row = both[2 * depth : 2 * depth + 1], both[2 * depth + 1 : 2 * depth + 2]
    wells_at = jnp.broadcast_to(wells_row, (8, LANES)).astype(jnp.int32)
    column_col = as_column(column_row)
    same = jnp.where(column_col == column_row, 1.0, 0.0).astype(BF16)

    def x_of(column):
        return jnp.floor((column + 0.5) * (1.0 / width_y))

    y_col = column_col - x_of(column_col) * width_y
    hot_y = jnp.where(
        lax.broadcasted_iota(jnp.int32, (LANES, width_y), 1).astype(F32) == y_col, 1.0, 0.0
    ).astype(BF16)
    hot_y = jnp.concatenate([hot_y, hot_y], axis=0)
    in_x = lax.broadcasted_iota(jnp.int32, (width_x, LANES), 0).astype(F32) == x_of(column_row)
    lower_half = lane < half
    x_row = x_of(column_row)
    y_row = column_row - x_row * width_y
    x_all, y_all = (jnp.broadcast_to(v, (8, LANES)).astype(jnp.int32) for v in (x_row, y_row))
    edge_lanes = jnp.where(sub < 2 * halves, y_all & (LANES - 1), x_all)
    edge_spots = jnp.zeros((8, LANES), jnp.int32)
    for side, x in enumerate(ends_x):
        for n in range(halves):
            here = (x_all == x) & (y_all >= n * LANES) & (y_all < (n + 1) * LANES)
            edge_spots = jnp.where((sub == side * halves + n) & here, 1, edge_spots)
    for side, y in enumerate(ends_y):
        edge_spots = jnp.where((sub == 2 * halves + side) & (y_all == y), 1, edge_spots)
    edge_spots = edge_spots > 0
    face_par = pltpu.roll(par[3 * depth : 4 * depth, :], half, 1)

    def well_totals(it):
        send, recv = ((well_send0, well_recv0), (well_send1, well_recv1))[it]
        all_wells(it).wait_recv()
        mine, other = send[...], recv[tiles - 1]
        for step in range(1, tiles):
            mine, other = mine + recv[step - 1], other + recv[tiles + step - 1]
        return mine, other

    def flows(mine, other, at_slots):
        def at_wells(row):
            return jnp.take_along_axis(
                jnp.broadcast_to(row, (8, LANES)), wells_at, axis=1, mode="promise_in_bounds"
            )

        hole = jnp.where(lower_half, at_wells(mine), at_wells(other))
        return index2 * (hole - at_slots)

    def responses(flow):
        change = jnp.zeros((depth, LANES), F32)
        for j in range(depth):
            change = change + lines[j] * flow[j : j + 1, :]
        out = jnp.sum(jnp.where(sub == phi, change, 0.0), axis=0, keepdims=True)
        theirs = jnp.sum(face_par * flow, axis=0, keepdims=True)
        return change, out, theirs

    def spread_out(change, data):
        order = [depth] + list(range(depth))
        for first in range(0, depth + 1, 3):
            some = order[first : first + 3]
            rows = slice(first * width_x, (first + len(some)) * width_x)
            for n, i in enumerate(some):
                row = change[i : i + 1, :] if i < depth else data
                left[sheet(first + n), :] = jnp.concatenate(
                    [jnp.where(in_x, part, 0.0).astype(BF16) for part in split(row, 2)], axis=1
                )
            spread[rows, :] = jnp.dot(left[rows, :], hot_y, preferred_element_type=F32)

    def update():
        lower[...] = lower[...] + spread[sheet(0), :]
        for i in range(depth):
            field[sheet(i), :] = (
                whole(solved, sheet(i))
                + spread[sheet(i + 1), :]
                + whole(inv, dyn_sheet(i * depth + phi)) * lower[...]
            )

    (solved_at,) = gather([(solved, 0, width_x, depth)], slots)
    mine, other = well_totals(0)
    index_mine, index_other = mine[:, wells:] + 1.0, other[:, wells:] + 1.0
    flow = flows(mine[:, :wells] / index_mine, other[:, :wells] / index_other, at2)
    change, out, theirs = responses(flow)
    stack = jnp.concatenate([change, jnp.where(sub == 0, out, theirs)], axis=0)
    pile = jnp.concatenate(split(stack, 3), axis=0).astype(BF16)
    summed = jnp.dot(pile, same, preferred_element_type=F32)
    summed = (summed[0:16] + summed[16:32]) + summed[32:48]
    inner_at = lines[phi]

    @pl.when(upper_group)
    def _():
        kappa_copy.wait_recv()

    x_copy(0).wait_recv()
    interior_data(0)
    data_at, kappa_at = gather([(lower_at, 0, 1, 1), (kappa, 0, 1, 1)], slots)
    kappa_gain = jnp.where(upper_group & lower_half[0:1], kappa_at - 1.0, 0.0)
    data = kappa_gain * out + theirs
    at_own = (solved_at + summed[0:8]) + inner_at * (
        data_at + (kappa_gain * summed[8:9] + summed[9:10])
    )
    edge_pack().wait_recv()
    edges = edge_tile_in[...]
    at_own = at_own + inner_at * jnp.sum(
        jnp.where(
            edge_spots,
            jnp.take_along_axis(edges, edge_lanes, axis=1, mode="promise_in_bounds"),
            0.0,
        ),
        axis=0,
        keepdims=True,
    )
    (share,) = binned([jnp.sum(index * at_own, axis=0, keepdims=True)])
    well_send1[...] = share + rate_row
    for dl, step in peers:
        well_copy(1, dl, step).start()
    at_send[...] = at_own
    at_copy.start()
    spread_out(change, data)
    add_edges(
        lower,
        [
            jnp.concatenate([edges[side * halves + n : side * halves + n + 1] for n in range(halves)], axis=1)
            for side in range(2)
        ],
        [edges[2 * halves + side : 2 * halves + side + 1, 0:width_x] for side in range(2)],
    )
    update()

    stage_halos(1)
    on_sides(lambda side: halo_copy(1, side).start())
    lateral_sum(field)
    interior_face(1)
    x_copy(1).start()
    on_sides(lambda side: gain_copy(side, True).wait_recv())
    for side in range(2):
        edge = jnp.sum(gain_xr[side] * row_send[1, side, 0], axis=0, keepdims=True)
        for n in range(halves):
            edge_send[side, n : n + 1, :] = edge[:, n * LANES : (n + 1) * LANES]
    sums = column_sums([gain_yr[side] * col_send[1, side] for side in range(2)])
    for side in range(2):
        edge_send[2 + side, 0:1, 0:width_x] = sums[side]
    on_sides(lambda side: edge_copy(side).start())
    on_sides(lambda side: halo_copy(1, side, True).wait_recv())
    lateral_edges(1)
    solve_all()
    at_copy.wait_recv()
    at2 = jnp.where(lower_half, at_own, pltpu.roll(at_recv[...], half, 1))
    mine, other = well_totals(1)
    flow = flows(mine / index_mine, other / index_other, at2)
    flow_out[...] = flow[:, 0:slots]
    change, out, theirs = responses(flow)
    spread_out(change, kappa_gain * out + theirs)
    x_copy(1).wait_recv()
    on_sides(lambda side: edge_copy(side, True).wait_recv())
    add_edges(
        x_recv.at[1],
        [
            jnp.concatenate([edge_recv[side, n : n + 1, :] for n in range(halves)], axis=1)
            for side in range(2)
        ],
        [edge_recv[2 + side, 0:1, 0:width_x] for side in range(2)],
    )
    interior_data(1)
    update()

    def sent(sem, buffers):
        rows = sum(math.prod(b.shape) for b in buffers) // LANES
        span = solved.at[0, 0:rows, :]
        remote(span, span, sem, sem, partner).wait_send()

    def side_sent(side):
        if side < 2:
            pieces = [row_send.at[0, 0], row_send.at[0, 0, 0], gain_x.at[0], edge_send.at[0]]
        else:
            pieces = [col_send.at[0, 0], col_send.at[0, 0], gain_y.at[0], edge_send.at[0]]
        sent(side_ssem.at[side], pieces)

    for it in range(ITERS):
        all_wells(it).wait_send()
    on_sides(side_sent)
    sent(part_ssem, [own, edge_tile, at_send, x_send])

    @pl.when(me_l == 1)
    def _():
        kappa_copy.wait_send()


def fused_shards(arrays, dims):
    (
        pressure, source, perm_x, perm_y, line_inverse, robin_below,
        tile_count, perf_owner, perf_well, perf_column, perf_index, well_rate,
    ) = arrays
    groups, n_gx, n_gy = dims
    depth, width_x, width_y = pressure.shape
    tiles = n_gx * n_gy
    slots = perf_well.shape[1]
    own_wells = well_rate.shape[1]
    wells = tiles * own_wells
    sheet = (width_x, width_y)
    stack = (depth * width_x, width_y)
    halves = width_y // LANES
    HBM = pl.BlockSpec(memory_space=pltpu.HBM)
    VMEM = pl.BlockSpec(memory_space=pltpu.VMEM)
    anywhere = pl.BlockSpec(memory_space=pl.ANY)
    dma = pltpu.SemaphoreType.DMA
    i32 = jnp.int32

    def vmem(*shape):
        return pltpu.VMEM(shape, F32)

    call = pl.pallas_call(
        functools.partial(fused, (groups, n_gx, n_gy, depth)),
        out_shape=(jax.ShapeDtypeStruct(stack, F32), jax.ShapeDtypeStruct((depth, slots), F32)),
        in_specs=[HBM] * 12,
        out_specs=(VMEM, VMEM),
        scratch_shapes=[
            vmem(*stack),
            vmem(3, *stack),
            vmem(halves, depth * depth * width_x, LANES),
            vmem(*sheet),
            pltpu.SMEM((1, slots), i32),
            pltpu.VMEM((1, 1), i32),
            pltpu.VMEM((1, slots), i32),
            pltpu.VMEM((1, slots), i32),
            pltpu.VMEM((1, slots), i32),
            vmem(depth, slots),
            vmem(1, own_wells),
            vmem(halves, depth * width_x, LANES),
            vmem(halves, depth * width_x, LANES),
            vmem(halves, width_x, LANES),
            vmem(*stack),
            vmem(halves, depth * width_x, LANES),
            vmem((depth + 1) * width_x, width_y),
            pltpu.VMEM(((depth + 1) * width_x, 2 * LANES), BF16),
            vmem(4 * depth, LANES),
            vmem(4 * depth, LANES),
            vmem(depth, depth, LANES),
            vmem(depth, LANES),
            vmem(depth, LANES),
            vmem(2, depth, width_y),
            vmem(2, ROWS, LANES),
            vmem(1, 2 * wells),
            vmem(groups * tiles - 1, 1, 2 * wells),
            vmem(1, wells),
            vmem(groups * tiles - 1, 1, wells),
            vmem(ITERS, 2, 2, depth, width_y),
            vmem(ITERS, 2, 2, depth, width_y),
            vmem(ITERS, 2, ROWS, LANES),
            vmem(ITERS, 2, ROWS, LANES),
            vmem(2, depth, width_y),
            vmem(2, ROWS, LANES),
            vmem(2, depth, width_y),
            vmem(2, ROWS, LANES),
            vmem(4, depth, LANES),
            vmem(4, depth, LANES),
            vmem(depth, LANES),
            vmem(depth, LANES),
            vmem(ITERS, *sheet),
            vmem(ITERS, *sheet),
            vmem(halves, width_x, LANES),
            dma,
            dma((9,)),
            dma((2,)),
            dma((ITERS,)),
            dma((ITERS,)),
            dma((4,)),
            dma((ITERS, 4)),
            dma((4,)),
            dma((5,)),
            dma,
            dma((ITERS,)),
            dma,
            dma((3,)),
        ],
        compiler_params=pltpu.CompilerParams(
            collective_id=0, has_side_effects=True, vmem_limit_bytes=LIMIT
        ),
        name="window",
    )
    operands = (
        pressure.reshape(stack),
        source.reshape(stack),
        perm_x.reshape(stack),
        perm_y.reshape(stack),
        line_inverse.reshape(depth * depth * width_x, width_y),
        robin_below[0],
        tile_count,
        perf_owner[:, :, 0],
        perf_well,
        perf_column,
        perf_index[0].T,
        well_rate,
    )
    field, flow = call(
        *[x if x.size == 1 else pltpu.with_memory_space_constraint(x, pltpu.HBM) for x in operands]
    )
    field, flow = pl.pallas_call(
        keep,
        out_shape=(
            jax.ShapeDtypeStruct(field.shape, F32),
            jax.ShapeDtypeStruct(flow.shape, F32),
        ),
        in_specs=[anywhere] * 2,
        out_specs=(HBM, HBM),
        scratch_shapes=[dma((2,))],
        compiler_params=pltpu.CompilerParams(vmem_limit_bytes=1 << 20),
        name="keep",
    )(field, flow)
    return field.reshape(pressure.shape), flow.T[None]


def shards(
    pressure,
    source,
    perm_x,
    perm_y,
    line_inverse,
    robin_below,
    tile_count,
    perf_owner,
    perf_well,
    perf_column,
    perf_index,
    well_rate,
):
    depth, width_x, width_y = pressure.shape
    groups, n_gx, n_gy = (lax.axis_size(a) for a in ("layer", "gx", "gy"))
    tiles = n_gx * n_gy
    slots = perf_well.shape[1]
    own_wells = well_rate.shape[1]
    wells = tiles * own_wells
    powers = all(n == 1 << (n.bit_length() - 1) for n in (n_gx, n_gy))
    if (
        groups == 2
        and depth == 8
        and wells == LANES
        and slots <= LANES // 2
        and slots % 16 == 0
        and width_x % ROWS == 0
        and width_x // ROWS * PACK <= LANES
        and width_y % LANES == 0
        and 2 * (width_y // LANES) + 2 <= depth
        and powers
    ):
        arrays = (
            pressure, source, perm_x, perm_y, line_inverse, robin_below,
            tile_count, perf_owner, perf_well, perf_column, perf_index, well_rate,
        )
        return fused_shards(arrays, (groups, n_gx, n_gy))
    sheet = (width_x, width_y)
    coefs = 1 if groups == 2 else 3
    HBM = pl.BlockSpec(memory_space=pltpu.HBM)
    anywhere = pl.BlockSpec(memory_space=pl.ANY)
    dma = pltpu.SemaphoreType.DMA
    i32 = jnp.int32
    call = pl.pallas_call(
        functools.partial(kernel, (groups, n_gx, n_gy)),
        out_shape=(
            jax.ShapeDtypeStruct(pressure.shape, F32),
            jax.ShapeDtypeStruct((depth, slots), F32),
        ),
        in_specs=[HBM] * 12,
        out_specs=(anywhere, anywhere),
        scratch_shapes=[
            pltpu.VMEM(pressure.shape, F32),
            pltpu.VMEM(pressure.shape, F32),
            pltpu.VMEM(pressure.shape, F32),
            pltpu.VMEM(pressure.shape, F32),
            pltpu.VMEM((depth, depth) + sheet, F32),
            pltpu.VMEM(sheet, F32),
            pltpu.VMEM((1, 1), i32),
            pltpu.VMEM((1, slots), i32),
            pltpu.VMEM((1, slots), i32),
            pltpu.VMEM((1, slots), i32),
            pltpu.VMEM((depth, slots), F32),
            pltpu.VMEM((1, own_wells), F32),
            pltpu.VMEM(sheet, F32),
            pltpu.VMEM(pressure.shape, F32),
            pltpu.VMEM(pressure.shape, F32),
            pltpu.VMEM((depth, slots), F32),
            pltpu.VMEM((depth, width_y), F32),
            pltpu.VMEM((width_x, 128), F32),
            pltpu.VMEM((1, 2 * wells), F32),
            pltpu.VMEM((tiles, 1, 2 * wells), F32),
            pltpu.VMEM((1, wells), F32),
            pltpu.VMEM((tiles, 1, wells), F32),
            pltpu.VMEM((ITERS, 2, 2, depth, width_y), F32),
            pltpu.VMEM((ITERS, 2, 2, depth, width_y), F32),
            pltpu.VMEM((ITERS, 2, width_x, 128), F32),
            pltpu.VMEM((ITERS, 2, width_x, 128), F32),
            pltpu.VMEM((groups, coefs) + sheet, F32),
            pltpu.VMEM((ITERS,) + sheet, F32),
            pltpu.VMEM((ITERS, groups) + sheet, F32),
            pltpu.VMEM((ITERS,) + sheet, F32),
            pltpu.VMEM((ITERS, groups) + sheet, F32),
            pltpu.VMEM(sheet, F32),
            pltpu.VMEM((groups, 1, slots), i32),
            pltpu.VMEM((ITERS, 2, slots), F32),
            pltpu.VMEM((ITERS, groups, 2, slots), F32),
            dma((12,)),
            dma((2,)),
            dma((ITERS, tiles)),
            dma((ITERS, tiles)),
            dma((ITERS, 4)),
            dma((ITERS, 4)),
            dma((groups, coefs)),
            dma((groups, coefs)),
            dma((ITERS, groups)),
            dma((ITERS, groups)),
            dma((ITERS, groups)),
            dma((ITERS, groups)),
            dma((groups,)),
            dma((groups,)),
            dma((ITERS, groups)),
            dma((ITERS, groups)),
        ],
        compiler_params=pltpu.CompilerParams(collective_id=0, has_side_effects=True, vmem_limit_bytes=LIMIT),
        name="window",
    )
    operands = (
        pressure,
        source,
        perm_x,
        perm_y,
        line_inverse[0],
        robin_below[0],
        tile_count,
        perf_owner[:, :, 0],
        perf_well,
        perf_column,
        perf_index[0].T,
        well_rate,
    )
    field, flow = call(
        *[x if x.size == 1 else pltpu.with_memory_space_constraint(x, pltpu.HBM) for x in operands]
    )
    field, flow = pl.pallas_call(
        keep,
        out_shape=(
            jax.ShapeDtypeStruct(field.shape, F32),
            jax.ShapeDtypeStruct(flow.shape, F32),
        ),
        in_specs=[anywhere] * 2,
        out_specs=(HBM, HBM),
        scratch_shapes=[dma((2,))],
        compiler_params=pltpu.CompilerParams(vmem_limit_bytes=1 << 20),
        name="keep",
    )(field, flow)
    return field, flow.T[None]


def solution(mesh):
    placed = (
        P("layer", "gx", "gy"),
        P("layer", "gx", "gy"),
        P("layer", "gx", "gy"),
        P("layer", "gx", "gy"),
        P("layer", None, None, "gx", "gy"),
        P("layer", "gx", "gy"),
        P("layer", ("gx", "gy")),
        P("layer", ("gx", "gy"), None),
        P("layer", ("gx", "gy")),
        P("layer", ("gx", "gy")),
        P("layer", ("gx", "gy"), None),
        P("layer", ("gx", "gy")),
    )
    return jax.shard_map(
        shards,
        mesh=mesh,
        in_specs=placed,
        out_specs=(P("layer", "gx", "gy"), P("layer", ("gx", "gy"), None)),
        check_vma=False,
    )
```

```python
import functools
import math

import jax
import jax.numpy as jnp
from jax import lax
from jax.experimental import pallas as pl
from jax.experimental.pallas import tpu as pltpu
from jax.sharding import PartitionSpec as P

ITERS = 2
LIMIT = 24 << 20
MESH = pl.DeviceIdType.MESH
F32 = jnp.float32
BF16 = jnp.bfloat16
ROWS = 8
LANES = 128
PACK = 16


def pieces(value):
    high = value.astype(BF16)
    rest = value - high.astype(F32)
    middle = rest.astype(BF16)
    low = (rest - middle.astype(F32)).astype(BF16)
    return jnp.concatenate([high, middle, low], axis=0)


def as_column(row):
    n = row.shape[1]
    eye = lax.broadcasted_iota(jnp.int32, (n, n), 0) == lax.broadcasted_iota(jnp.int32, (n, n), 1)
    return jnp.sum(jnp.where(eye, jnp.broadcast_to(row, (n, n)), 0.0), axis=1, keepdims=True)


def as_row(column):
    n = column.shape[0]
    eye = lax.broadcasted_iota(jnp.int32, (n, n), 0) == lax.broadcasted_iota(jnp.int32, (n, n), 1)
    return jnp.sum(jnp.where(eye, jnp.broadcast_to(column, (n, n)), 0.0), axis=0, keepdims=True)


def one_hots(column_row, width_x, width_y):
    slots = column_row.shape[1]
    column_col = as_column(column_row.astype(F32)).astype(jnp.int32)
    lane_x = lax.broadcasted_iota(jnp.int32, (slots, width_x), 1)
    in_x = (column_col >= lane_x * width_y) & (column_col < lane_x * width_y + width_y)
    x_of = jnp.sum(jnp.where(in_x, lane_x.astype(F32), 0.0), axis=1, keepdims=True).astype(jnp.int32)
    in_y = lax.broadcasted_iota(jnp.int32, (slots, width_y), 1) == column_col - x_of * width_y
    hot_x = jnp.where(in_x, 1.0, 0.0).astype(BF16)
    row_x = lax.broadcasted_iota(jnp.int32, (width_x, slots), 0)
    hot_xt = jnp.where(
        (column_row >= row_x * width_y) & (column_row < row_x * width_y + width_y), 1.0, 0.0
    ).astype(BF16)
    return in_y, jnp.concatenate([hot_x] * 3, axis=1), jnp.concatenate([hot_xt] * 3, axis=1)


def keep(field_in, flow_in, field_out, flow_out, sem):
    copies = [
        pltpu.make_async_copy(field_in, field_out, sem.at[0]),
        pltpu.make_async_copy(flow_in, flow_out, sem.at[1]),
    ]
    for copy in copies:
        copy.start()
    for copy in copies:
        copy.wait()


def kernel(
    dims,
    pressure,
    source,
    perm_x,
    perm_y,
    inverse,
    robin,
    count_in,
    owner_in,
    well_in,
    column_in,
    index_in,
    rate_in,
    field_out,
    flow_out,
    field,
    src,
    kx,
    ky,
    inv,
    lower,
    count_v,
    owner_v,
    well_v,
    column_v,
    index_v,
    rate_v,
    upper,
    rhs,
    solved,
    flow_v,
    halo_mult_x,
    halo_mult_y,
    well_send0,
    well_recv0,
    well_send1,
    well_recv1,
    row_send,
    row_recv,
    col_send,
    col_recv,
    coef_recv,
    down_send,
    down_recv,
    up_send,
    up_recv,
    own_down,
    spot_recv,
    delta_send,
    delta_recv,
    load_sem,
    store_sem,
    well_ssem,
    well_rsem,
    halo_ssem,
    halo_rsem,
    coef_ssem,
    coef_rsem,
    down_ssem,
    down_rsem,
    up_ssem,
    up_rsem,
    spot_ssem,
    spot_rsem,
    delta_ssem,
    delta_rsem,
):
    groups, n_gx, n_gy = dims
    tiles = n_gx * n_gy
    depth, width_x, width_y = field.shape
    slots = well_v.shape[1]
    own_wells = rate_v.shape[1]
    wells = tiles * own_wells
    me_l, me_x, me_y = lax.axis_index("layer"), lax.axis_index("gx"), lax.axis_index("gy")
    me = me_x * n_gy + me_y

    loads = [
        pltpu.make_async_copy(a, b, load_sem.at[i])
        for i, (a, b) in enumerate(
            [
                (pressure, field),
                (column_in, column_v),
                (well_in, well_v),
                (owner_in, owner_v),
                (index_in, index_v),
                (count_in, count_v),
                (rate_in, rate_v),
                (perm_x, kx),
                (perm_y, ky),
                (source, src),
                (robin, lower),
                (inverse, inv),
            ]
        )
    ]
    for load in loads:
        load.start()

    def peer(step):
        other = lax.rem(me + step, tiles)
        return {"gx": lax.div(other, n_gy), "gy": lax.rem(other, n_gy)}

    barrier = pltpu.get_barrier_semaphore()
    for step in range(1, tiles):
        pl.semaphore_signal(barrier, inc=1, device_id=peer(step), device_id_type=MESH)
    for step in range(1, groups):
        pl.semaphore_signal(
            barrier, inc=1, device_id={"layer": lax.rem(me_l + step, groups)}, device_id_type=MESH
        )

    for load in loads[1:7]:
        load.wait()
    live = lax.broadcasted_iota(jnp.int32, (slots, 1), 0) < count_v[...]
    in_y, hot_x3, hot_xt3 = one_hots(column_v[...], width_x, width_y)
    well_col = as_column(well_v[...].astype(F32)).astype(jnp.int32)
    owner_col = as_column(owner_v[...].astype(F32)).astype(jnp.int32)
    well_id = owner_col * own_wells + well_col
    member = jnp.where(
        (lax.broadcasted_iota(jnp.int32, (slots, wells), 1) == well_id) & live, 1.0, 0.0
    )
    layer_lane = lax.broadcasted_iota(jnp.int32, (slots, depth), 1)
    index = jnp.zeros((slots, depth), F32)
    for l in range(depth):
        index = jnp.where(layer_lane == l, as_column(index_v[l : l + 1, :]), index)
    rate_col = as_column(rate_v[...])
    rate_spot = (
        lax.broadcasted_iota(jnp.int32, (own_wells, wells), 1)
        == lax.broadcasted_iota(jnp.int32, (own_wells, wells), 0) + me * own_wells
    )
    rate_row = jnp.sum(jnp.where(rate_spot, rate_col, 0.0), axis=0, keepdims=True)

    def gathered(ref):
        at = jnp.zeros((slots, depth), F32)
        for l in range(depth):
            picked = jnp.dot(hot_x3, pieces(ref[l]), preferred_element_type=F32)
            one = jnp.sum(jnp.where(in_y, picked, 0.0), axis=1, keepdims=True)
            at = jnp.where(layer_lane == l, one, at)
        return at

    def well_row(at):
        share = jnp.sum(index * at, axis=1, keepdims=True)
        return jnp.sum(share * member, axis=0, keepdims=True) + rate_row

    def well_copy(it, step):
        send, recv = ((well_send0, well_recv0), (well_send1, well_recv1))[it]
        return pltpu.make_async_remote_copy(
            src_ref=send,
            dst_ref=recv.at[step],
            send_sem=well_ssem.at[it, step],
            recv_sem=well_rsem.at[it, step],
            device_id=peer(step),
            device_id_type=MESH,
        )

    sides = (
        ("gx", me_x, -1, me_x > 0),
        ("gx", me_x, 1, me_x < n_gx - 1),
        ("gy", me_y, -1, me_y > 0),
        ("gy", me_y, 1, me_y < n_gy - 1),
    )

    def halo_copy(it, side):
        axis, mine, way, _ = sides[side]
        send, recv = (row_send, row_recv) if side < 2 else (col_send, col_recv)
        width = slice(0, 2 if it == 0 else 1)
        if side < 2:
            source_ref = send.at[it, side, width]
            target_ref = recv.at[it, 1 - side, width]
        else:
            source_ref = send.at[it, side - 2]
            target_ref = recv.at[it, 3 - side]
        return pltpu.make_async_remote_copy(
            src_ref=source_ref,
            dst_ref=target_ref,
            send_sem=halo_ssem.at[it, side],
            recv_sem=halo_rsem.at[it, side ^ 1],
            device_id={axis: mine + way},
            device_id_type=MESH,
        )

    def halo_landing(it, side):
        axis, mine, way, _ = sides[side]
        if side < 2:
            width = slice(0, 2 if it == 0 else 1)
            ref, other = row_recv.at[it, side, width], row_send.at[it, 1 - side, width]
        else:
            ref, other = col_recv.at[it, side - 2], col_send.at[it, 3 - side]
        return pltpu.make_async_remote_copy(
            src_ref=other,
            dst_ref=ref,
            send_sem=halo_ssem.at[it, side],
            recv_sem=halo_rsem.at[it, side],
            device_id={axis: mine + way},
            device_id_type=MESH,
        )

    lane128 = lax.broadcasted_iota(jnp.int32, (width_x, 128), 1)

    def packed_columns(arrays, lane):
        out = jnp.zeros((width_x, 128), F32)
        at = 0
        for ref in arrays:
            for l in range(depth):
                out = jnp.where(lane128 == at, ref[l, :, lane : lane + 1], out)
                at += 1
        return out

    def stage_halos(it):
        for l in range(depth):
            row_send[it, 0, 0, l : l + 1, :] = field[l, 0:1, :]
            row_send[it, 1, 0, l : l + 1, :] = field[l, width_x - 1 : width_x, :]
            if it == 0:
                row_send[it, 0, 1, l : l + 1, :] = kx[l, 0:1, :]
                row_send[it, 1, 1, l : l + 1, :] = kx[l, width_x - 1 : width_x, :]
        arrays = (field, ky) if it == 0 else (field,)
        col_send[it, 0] = packed_columns(arrays, 0)
        col_send[it, 1] = packed_columns(arrays, width_y - 1)
        for side in range(4):

            @pl.when(jnp.logical_not(sides[side][3]))
            def _():
                if side < 2:
                    row_recv[it, side] = jnp.zeros(row_recv.shape[2:], F32)
                else:
                    col_recv[it, side - 2] = jnp.zeros(col_recv.shape[2:], F32)

    def start_halos(it):
        for side in range(4):
            @pl.when(sides[side][3])
            def _():
                halo_copy(it, side).start()

    def wait_halos(it):
        for side in range(4):
            @pl.when(sides[side][3])
            def _():
                halo_landing(it, side).wait_recv()

    last_x = lax.broadcasted_iota(jnp.int32, (width_x, width_y), 0) == width_x - 1
    first_x = lax.broadcasted_iota(jnp.int32, (width_x, width_y), 0) == 0
    last_y = lax.broadcasted_iota(jnp.int32, (width_x, width_y), 1) == width_y - 1
    first_y = lax.broadcasted_iota(jnp.int32, (width_x, width_y), 1) == 0

    def face_coefficients():
        for l in range(depth):
            mult = kx[l]
            kx[l] = 0.5 * (mult + pltpu.roll(mult, width_x - 1, 0))
            mult = ky[l]
            ky[l] = 0.5 * (mult + pltpu.roll(mult, width_y - 1, 1))

    def edge_coefficients():
        for l in range(depth):
            one = slice(l, l + 1)
            halo_mult_x[one, :] = 0.5 * (row_send[0, 0, 1, one, :] + row_recv[0, 0, 1, one, :])
            kx[l, width_x - 1 : width_x, :] = 0.5 * (
                row_send[0, 1, 1, one, :] + row_recv[0, 1, 1, one, :]
            )
            lane = slice(depth + l, depth + l + 1)
            ky[l, :, width_y - 1 : width_y] = 0.5 * (
                col_send[0, 1, :, lane] + col_recv[0, 1, :, lane]
            )
        halo_mult_y[...] = 0.5 * (col_send[0, 0] + col_recv[0, 0])

    def lateral_sum():
        for l in range(depth):
            now = field[l]
            face_x, face_y = kx[l], ky[l]
            east = jnp.where(last_x, 0.0, face_x * pltpu.roll(now, width_x - 1, 0))
            west = jnp.where(first_x, 0.0, pltpu.roll(face_x * now, 1, 0))
            north = jnp.where(last_y, 0.0, face_y * pltpu.roll(now, width_y - 1, 1))
            south = jnp.where(first_y, 0.0, pltpu.roll(face_y * now, 1, 1))
            rhs[l] = src[l] + ((east + west) + (north + south))

    def lateral_edges(it):
        end_x, end_y = slice(width_x - 1, width_x), slice(width_y - 1, width_y)
        for l in range(depth):
            one = slice(l, l + 1)
            lane = slice(depth + l, depth + l + 1)
            rhs[l, 0:1, :] += halo_mult_x[one, :] * row_recv[it, 0, 0, one, :]
            rhs[l, end_x, :] += kx[l, end_x, :] * row_recv[it, 1, 0, one, :]
            rhs[l, :, 0:1] += halo_mult_y[:, lane] * col_recv[it, 0, :, one]
            rhs[l, :, end_y] += ky[l, :, end_y] * col_recv[it, 1, :, one]

    def layer_copy(ref, target, ssem, rsem, other):
        return pltpu.make_async_remote_copy(
            src_ref=ref,
            dst_ref=target,
            send_sem=ssem,
            recv_sem=rsem,
            device_id={"layer": other},
            device_id_type=MESH,
        )

    last = depth - 1
    coef_at = ((0, 0), (0, last), (last, 0))[: 1 if groups == 2 else 3]

    def coef_copy(which, sender, other):
        i, j = coef_at[which]
        return layer_copy(
            inv.at[i, j],
            coef_recv.at[sender, which],
            coef_ssem.at[other, which],
            coef_rsem.at[sender, which],
            other,
        )

    def coef_sent(which, sender, other):
        if which == 0:
            return other < sender
        if which == 1:
            return other < sender < groups - 1
        return 0 < sender < groups - 1

    def spot_copy(step):
        return layer_copy(
            column_v, spot_recv.at[step], spot_ssem.at[step], spot_rsem.at[step],
            lax.rem(me_l + step, groups),
        )

    def delta_copy(it, step):
        return layer_copy(
            delta_send.at[it], delta_recv.at[it, step], delta_ssem.at[it, step],
            delta_rsem.at[it, step], lax.rem(me_l + step, groups),
        )

    def down_copy(it, sender, other):
        return layer_copy(
            down_send.at[it], down_recv.at[it, sender], down_ssem.at[it, other],
            down_rsem.at[it, sender], other,
        )

    def up_copy(it, sender, other):
        return layer_copy(
            up_send.at[it], up_recv.at[it, sender], up_ssem.at[it, other],
            up_rsem.at[it, sender], other,
        )

    def layer_sends(act, which):
        for g in range(groups):

            @pl.when(me_l == g)
            def _():
                for other in range(groups):
                    if other == g:
                        continue
                    if which == "coef":
                        for c in range(len(coef_at)):
                            if coef_sent(c, g, other):
                                getattr(coef_copy(c, g, other), act)()
                    else:
                        it = which
                        if g < groups - 1:
                            getattr(down_copy(it, g, other), act)()
                        if other < g:
                            getattr(up_copy(it, g, other), act)()

    def chunk_loop(body):
        def step(c, carry):
            body(pl.ds(pl.multiple_of(c * ROWS, ROWS), ROWS))
            return carry

        lax.fori_loop(0, width_x // ROWS, step, 0)

    def dot_layer(i, rows, terms):
        total = inv[i, 0, rows, :] * terms[0]
        for j in range(1, depth):
            total = total + inv[i, j, rows, :] * terms[j]
        return total

    def solve_faces(it):
        def body(rows):
            terms = [rhs[j, rows, :] for j in range(depth)]
            bottom = dot_layer(last, rows, terms)
            top = dot_layer(0, rows, terms)
            below = lower[rows, :]
            nothing = jnp.zeros_like(below)
            down_send[it, rows, :] = inv[last, 0, rows, :] * nothing + (
                (bottom + inv[last, last, rows, :] * below) - below
            )
            up_send[it, rows, :] = inv[0, last, rows, :] * nothing + top

        chunk_loop(body)

    def solve_all():
        def body(rows):
            terms = [rhs[j, rows, :] for j in range(depth)]
            for i in range(depth):
                value = dot_layer(i, rows, terms)
                solved[i, rows, :] = value
                if i == last:
                    below = lower[rows, :]
                    own_down[rows, :] = inv[last, 0, rows, :] * jnp.zeros_like(below) + (
                        (value + inv[last, last, rows, :] * below) - below
                    )

        chunk_loop(body)

    def sweeps(it):
        for g in range(groups):

            @pl.when(me_l == g)
            def _():
                for k in range(groups):
                    if k == g:
                        continue
                    if k < groups - 1:
                        down_copy(it, k, k).wait_recv()
                    if k > g:
                        up_copy(it, k, k).wait_recv()
                    if it == 0:
                        for c in range(len(coef_at)):
                            if coef_sent(c, k, g):
                                coef_copy(c, k, k).wait_recv()
                    step = (g - k) % groups
                    delta_copy(it, step).wait_recv()
                    other_y, _, other_xt3 = spots[step]
                    for row, wanted, ref in ((0, k < groups - 1, down_recv), (1, k > g, up_recv)):
                        if wanted:
                            spread = as_column(delta_recv[it, step, row : row + 1, :])
                            spread = pieces(jnp.where(other_y, spread, 0.0))
                            ref[it, k] = ref[it, k] + jnp.dot(
                                other_xt3, spread, preferred_element_type=F32
                            )

                def body(rows):
                    def coef(which, k):
                        i, j = coef_at[which]
                        return inv[i, j, rows, :] if k == g else coef_recv[k, which, rows, :]

                    above = [jnp.zeros((ROWS, width_y), F32)]
                    for k in range(groups - 1):
                        value = own_down[rows, :] if k == g else down_recv[it, k, rows, :]
                        if k > 0:
                            value = coef(2, k) * above[k] + value
                        above.append(value)
                    below = jnp.zeros((ROWS, width_y), F32)
                    for k in range(groups - 1, g, -1):
                        value = (up_recv[it, k, rows, :] + coef(0, k) * above[k]) - above[k]
                        if k < groups - 1:
                            value = coef(1, k) * below + value
                        below = value
                    upper[rows, :] = above[g]
                    lower[rows, :] = below

                chunk_loop(body)

    def update():
        def body(rows):
            above, below = upper[rows, :], lower[rows, :]
            for i in range(depth):
                field[i, rows, :] = (
                    solved[i, rows, :]
                    + inv[i, 0, rows, :] * above
                    + inv[i, last, rows, :] * below
                )

        chunk_loop(body)

    index_total = None
    spots = [None] * groups
    for it in range(ITERS):
        if it == 0:
            loads[0].wait()
        at = gathered(field)
        if it == 0:
            index_row = jnp.sum(
                jnp.sum(index, axis=1, keepdims=True) * member, axis=0, keepdims=True
            )
            well_send0[...] = jnp.concatenate([well_row(at), index_row], axis=1)
            loads[7].wait()
            loads[8].wait()
            stage_halos(it)
            pl.semaphore_wait(barrier, tiles - 1 + groups - 1)
        else:
            well_send1[...] = well_row(at)
        for step in range(1, tiles):
            well_copy(it, step).start()
        if it > 0:
            stage_halos(it)
        start_halos(it)
        if it == 0:
            for step in range(1, groups):
                spot_copy(step).start()
            for load in loads[9:]:
                load.wait()
            layer_sends("start", "coef")
        if it == 0:
            face_coefficients()
        lateral_sum()
        wait_halos(it)
        if it == 0:
            edge_coefficients()
        lateral_edges(it)
        solve_faces(it)
        layer_sends("start", it)
        if it == 0:
            for step in range(1, groups):
                spot_copy(step).wait_recv()
                spots[step] = one_hots(spot_recv[step], width_x, width_y)
            face_last, face_first = gathered(inv.at[last]), gathered(inv.at[0])
        total = (well_send0, well_send1)[it][...]
        for step in range(1, tiles):
            well_copy(it, step).wait_recv()
        for step in range(1, tiles):
            total = total + (well_recv0, well_recv1)[it][step]
        if it == 0:
            index_total = total[:, wells:] + 1.0
            total = total[:, :wells]
        bottom_hole = total / index_total
        hole = jnp.sum(member * bottom_hole, axis=1, keepdims=True)
        flow = jnp.where(live, index * (hole - at), 0.0)
        for row, face in enumerate((face_last, face_first)):
            delta_send[it, row : row + 1, :] = as_row(
                jnp.sum(face * flow, axis=1, keepdims=True)
            )
        for step in range(1, groups):
            delta_copy(it, step).start()
        if it == ITERS - 1:
            for l in range(depth):
                flow_v[l : l + 1, :] = as_row(flow[:, l : l + 1])
            flow_store = pltpu.make_async_copy(flow_v, flow_out, store_sem.at[0])
            flow_store.start()
        for l in range(depth):
            spread = jnp.where(in_y, flow[:, l : l + 1], 0.0)
            rhs[l] = rhs[l] + jnp.dot(hot_xt3, pieces(spread), preferred_element_type=F32)
        solve_all()
        sweeps(it)
        update()
    field_store = pltpu.make_async_copy(field, field_out, store_sem.at[1])
    field_store.start()
    for it in range(ITERS):
        for step in range(1, tiles):
            well_copy(it, step).wait_send()
        for side in range(4):

            @pl.when(sides[side][3])
            def _():
                halo_copy(it, side).wait_send()

        layer_sends("wait_send", it)
        for step in range(1, groups):
            delta_copy(it, step).wait_send()
    for step in range(1, groups):
        spot_copy(step).wait_send()
    layer_sends("wait_send", "coef")
    flow_store.wait()
    field_store.wait()


def split(value, count):
    out = []
    for _ in range(count - 1):
        part = value.astype(BF16).astype(F32)
        out.append(part)
        value = value - part
    out.append(value)
    return out


def fused(
    dims,
    pressure,
    source,
    perm_x,
    perm_y,
    inverse,
    robin,
    count_in,
    owner_in,
    well_in,
    column_in,
    index_in,
    rate_in,
    field,
    flow_out,
    start_at,
    rock,
    inv,
    lower,
    column_s,
    count_v,
    owner_v,
    well_v,
    column_v,
    index_v,
    rate_v,
    slabs,
    face_lines,
    lower_at,
    rhs,
    solved,
    spread,
    left,
    own,
    par,
    lines,
    at_send,
    at_recv,
    coef_x,
    coef_y,
    well_send0,
    well_recv0,
    well_send1,
    well_recv1,
    row_send,
    row_recv,
    col_send,
    col_recv,
    gain_x,
    gain_y,
    gain_xr,
    gain_yr,
    edge_send,
    edge_recv,
    edge_tile,
    edge_tile_in,
    x_send,
    x_recv,
    kappa,
    smem_sem,
    load_sem,
    rest_sem,
    well_ssem,
    well_rsem,
    side_ssem,
    halo_rsem,
    gain_rsem,
    edge_rsem,
    part_ssem,
    x_rsem,
    kappa_ssem,
    misc_rsem,
):
    groups, n_gx, n_gy, depth = dims
    tiles = n_gx * n_gy
    width_x, width_y = lower.shape
    slots = well_v.shape[1]
    own_wells = rate_v.shape[1]
    wells = tiles * own_wells
    me_l, me_x, me_y = lax.axis_index("layer"), lax.axis_index("gx"), lax.axis_index("gy")
    me = me_x * n_gy + me_y
    upper_group = me_l == 0
    phi = (1 - me_l) * (depth - 1)
    halves = width_y // LANES

    def sheet(i):
        return slice(i * width_x, (i + 1) * width_x)

    def dyn_sheet(i):
        return pl.ds(pl.multiple_of(i * width_x, width_x), width_x)

    def peer(dl, step):
        return {"layer": me_l ^ dl, "gx": me_x ^ (step // n_gy), "gy": me_y ^ (step % n_gy)}

    peers = [
        (dl, step)
        for step in reversed(range(tiles))
        for dl in reversed(range(groups))
        if (dl, step) != (0, 0)
    ]
    partner = {"layer": 1 - me_l}

    block = depth * width_x
    to_smem = pltpu.make_async_copy(column_in, column_s, smem_sem)
    to_smem.start()
    loads = [
        pltpu.make_async_copy(a, b, load_sem.at[i])
        for i, (a, b) in enumerate(
            [
                (column_in, column_v),
                (well_in, well_v),
                (owner_in, owner_v),
                (index_in, index_v),
                (count_in, count_v),
                (rate_in, rate_v),
                (robin, lower),
            ]
        )
    ]
    start_load = pltpu.make_async_copy(pressure, start_at, load_sem.at[7])
    rocks = [
        pltpu.make_async_copy(a, rock.at[n], load_sem.at[8])
        for n, a in enumerate((perm_x, perm_y, source))
    ]
    rock_loaded = pltpu.make_async_copy(rock, rock, load_sem.at[8])
    rock_x, rock_y, src = rock.at[0], rock.at[1], rock.at[2]
    barrier = pltpu.get_barrier_semaphore()
    for load in loads[:6] + [start_load]:
        load.start()
    for dl, step in peers:
        pl.semaphore_signal(barrier, inc=1, device_id=peer(dl, step), device_id_type=MESH)
    face_block = pl.ds(pl.multiple_of(phi * block, block), block)
    other_blocks = pl.ds(pl.multiple_of(me_l * block, block), (depth - 1) * block)

    def line_loads(rows, sem):
        return [
            pltpu.make_async_copy(
                inverse.at[rows, n * LANES : (n + 1) * LANES], inv.at[n, rows, :], sem
            )
            for n in range(halves)
        ]

    def lines_loaded(rows, sem):
        return pltpu.make_async_copy(inv.at[:, rows, :], inv.at[:, rows, :], sem)

    for load in rocks + line_loads(face_block, rest_sem.at[0]) + loads[6:]:
        load.start()

    lane = lax.broadcasted_iota(jnp.int32, (8, LANES), 1)
    sub = lax.broadcasted_iota(jnp.int32, (8, LANES), 0)

    own[...] = jnp.zeros(own.shape, F32)
    for load in loads[:6]:
        load.wait()
    live = lax.broadcasted_iota(jnp.int32, (depth, slots), 1) < count_v[...]
    own[0:depth, 0:slots] = jnp.where(live, index_v[...], 0.0)
    own[2 * depth : 2 * depth + 1, 0:slots] = column_v[...].astype(F32)
    own[2 * depth + 1 : 2 * depth + 2, 0:slots] = (owner_v[...] * own_wells + well_v[...]).astype(F32)
    index = own[0:depth, :]
    well_id = own[2 * depth + 1 : 2 * depth + 2, :]
    member = jnp.where(
        lax.broadcasted_iota(jnp.int32, (LANES, wells), 1).astype(F32) == as_column(well_id), 1.0, 0.0
    ).astype(BF16)
    rate_col = as_column(rate_v[...])
    rate_spot = (
        lax.broadcasted_iota(jnp.int32, (own_wells, wells), 1)
        == lax.broadcasted_iota(jnp.int32, (own_wells, wells), 0) + me * own_wells
    )
    rate_row = jnp.sum(jnp.where(rate_spot, rate_col, 0.0), axis=0, keepdims=True)

    def gather(jobs, span):
        shift = width_y.bit_length() - 1

        def step(c, accs):
            for k in range(span):
                s = c * span + k
                column = column_s[0, s]
                if width_y == 1 << shift:
                    x, y = lax.shift_right_logical(column, shift), column & (width_y - 1)
                else:
                    x, y = lax.div(column, width_y), lax.rem(column, width_y)
                tile = lax.shift_right_logical(y, LANES.bit_length() - 1)
                turn = (s + LANES - (y & (LANES - 1))) & (LANES - 1)
                found = []
                for ref, first, stride, count in jobs:
                    if count == 1:
                        value = ref[tile, pl.ds(first + x, 1), :]
                    else:
                        value = ref[tile, pl.ds(first + x, count, stride=stride), :]
                    found.append(pltpu.roll(value, turn, 1))
                accs = tuple(
                    jnp.where(lane[: value.shape[0]] == s, value, acc) for acc, value in zip(accs, found)
                )
            return accs

        accs = tuple(jnp.zeros((count, LANES), F32) for _, _, _, count in jobs)
        if span == slots:
            return step(0, accs)
        return lax.fori_loop(0, slots // span, step, accs)

    wide = lax.broadcasted_iota(jnp.int32, (16, LANES), 0)

    def binned(rows):
        at, out = 0, jnp.zeros((16, LANES), F32)
        for row in rows:
            for part in split(row, 3):
                out = jnp.where(wide == at, part, out)
                at += 1
        total = jnp.dot(out.astype(BF16), member, preferred_element_type=F32)
        return [jnp.sum(total[3 * k : 3 * k + 3, :], axis=0, keepdims=True) for k in range(len(rows))]

    def remote(a, b, ssem, rsem, device):
        return pltpu.make_async_remote_copy(
            src_ref=a, dst_ref=b, send_sem=ssem, recv_sem=rsem, device_id=device, device_id_type=MESH
        )

    def well_copy(it, dl, step):
        send, recv = ((well_send0, well_recv0), (well_send1, well_recv1))[it]
        return remote(
            send, recv.at[dl * tiles + step - 1], well_ssem.at[it], well_rsem.at[it], peer(dl, step)
        )

    def all_wells(it):
        recv = (well_recv0, well_recv1)[it]
        return remote(recv, recv, well_ssem.at[it], well_rsem.at[it], partner)

    sides = (
        ("gx", me_x, -1, me_x > 0),
        ("gx", me_x, 1, me_x < n_gx - 1),
        ("gy", me_y, -1, me_y > 0),
        ("gy", me_y, 1, me_y < n_gy - 1),
    )

    def across(side, flip=False):
        axis, mine, way, _ = sides[side]
        out = {axis: mine + way}
        if flip:
            out["layer"] = 1 - me_l
        return out

    def halo_copy(it, side, landing=False):
        other = side ^ 1
        at, to = (other, side) if landing else (side, other)
        width = slice(0, 2 if it == 0 else 1)
        if side < 2:
            a, b = row_send.at[it, at, width], row_recv.at[it, to, width]
        else:
            a, b = col_send.at[it, at - 2], col_recv.at[it, to - 2]
        return remote(a, b, side_ssem.at[at], halo_rsem.at[it, to], across(side))

    def gain_copy(side, landing=False):
        other = side ^ 1
        at, to = (other, side) if landing else (side, other)
        if side < 2:
            a, b = gain_x.at[at], gain_xr.at[to]
        else:
            a, b = gain_y.at[at - 2], gain_yr.at[to - 2]
        return remote(a, b, side_ssem.at[at], gain_rsem.at[to], across(side))

    def edge_copy(side, landing=False):
        other = side ^ 1
        at, to = (other, side) if landing else (side, other)
        return remote(
            edge_send.at[at], edge_recv.at[to], side_ssem.at[at], edge_rsem.at[to],
            across(side, True),
        )

    def edge_pack():
        return remote(edge_tile, edge_tile_in, part_ssem, edge_rsem.at[4], partner)

    def x_copy(it):
        return remote(x_send.at[it], x_recv.at[it], part_ssem, x_rsem.at[it], partner)

    slot_copy = remote(own, par, part_ssem, misc_rsem.at[0], partner)
    at_copy = remote(at_send, at_recv, part_ssem, misc_rsem.at[1], partner)
    kappa_copy = remote(inv.at[:, 0:width_x, :], kappa, kappa_ssem, misc_rsem.at[2], partner)

    lane_x = lax.broadcasted_iota(jnp.int32, (width_x, LANES), 1)

    parts = width_x // ROWS

    def packed_columns(blocks, y):
        out = jnp.zeros((ROWS, LANES), F32)
        tile = y - y % LANES
        for at, (ref, first) in enumerate(blocks):
            for n in range(parts):
                value = ref[pl.ds(first + n * ROWS, ROWS), tile : tile + LANES]
                to = n * PACK + at
                out = jnp.where(lane == to, pltpu.roll(value, (to - y) % LANES, 1), out)
        return out

    entry = lax.broadcasted_iota(jnp.int32, (LANES, LANES), 0)
    cell = lax.broadcasted_iota(jnp.int32, (LANES, LANES), 1)
    own_entries = ((entry & (PACK - 1)) < depth) & ((entry >> (PACK.bit_length() - 1)) == (cell >> 3))
    own_entries = jnp.where(own_entries, 1.0, 0.0).astype(BF16)

    def column_sums(values):
        pile = jnp.concatenate([part for value in values for part in split(value, 3)], axis=0)
        total = jnp.dot(pile.astype(BF16), own_entries, preferred_element_type=F32)
        at_row = (lane & (ROWS - 1)) == sub
        rows = []
        for n in range(len(values)):
            some = [total[(3 * n + k) * ROWS : (3 * n + k + 1) * ROWS] for k in range(3)]
            picked = jnp.where(at_row, (some[0] + some[1]) + some[2], 0.0)
            rows.append(jnp.sum(picked, axis=0, keepdims=True)[:, 0:width_x])
        return rows

    def each(ref):
        return [(ref, l * width_x) for l in range(depth)]

    ends_x, ends_y = (0, width_x - 1), (0, width_y - 1)

    def stage_halos(it):
        for side, x in enumerate(ends_x):
            for l in range(depth):
                row = l * width_x + x
                row_send[it, side, 0, l : l + 1, :] = (field if it else start_at)[row : row + 1, :]
                if it == 0:
                    row_send[it, side, 1, l : l + 1, :] = rock_x[row : row + 1, :]
        blocks = each(field) if it else each(start_at) + each(rock_y)
        for side, y in enumerate(ends_y):
            col_send[it, side] = packed_columns(blocks, y)

    def clear_halos(it):
        for side in range(4):

            @pl.when(jnp.logical_not(sides[side][3]))
            def _():
                if side < 2:
                    row_recv[it, side] = jnp.zeros(row_recv.shape[2:], F32)
                else:
                    col_recv[it, side - 2] = jnp.zeros(col_recv.shape[2:], F32)
                if it == 1:
                    if side < 2:
                        gain_xr[side] = jnp.zeros(gain_xr.shape[1:], F32)
                    else:
                        gain_yr[side - 2] = jnp.zeros(gain_yr.shape[1:], F32)
                    edge_recv[side] = jnp.zeros(edge_recv.shape[1:], F32)

    def on_sides(body):
        for side in range(4):
            pl.when(sides[side][3])(functools.partial(body, side))

    first_x = lax.broadcasted_iota(jnp.int32, (width_x, width_y), 0) == width_x - 1
    first_y = lax.broadcasted_iota(jnp.int32, (width_x, width_y), 1) == width_y - 1

    def face_coefficients():
        for l in range(depth):
            mult = rock_x[sheet(l), :]
            rock_x[sheet(l), :] = jnp.where(first_x, 0.0, 0.5 * (mult + pltpu.roll(mult, width_x - 1, 0)))
            mult = rock_y[sheet(l), :]
            rock_y[sheet(l), :] = jnp.where(first_y, 0.0, 0.5 * (mult + pltpu.roll(mult, width_y - 1, 1)))

    def lateral_sum(now_at):
        for l in range(depth):
            now = now_at[sheet(l), :]
            face_x, face_y = rock_x[sheet(l), :], rock_y[sheet(l), :]
            east = face_x * pltpu.roll(now, width_x - 1, 0)
            west = pltpu.roll(face_x * now, 1, 0)
            north = face_y * pltpu.roll(now, width_y - 1, 1)
            south = pltpu.roll(face_y * now, 1, 1)
            rhs[sheet(l), :] = src[sheet(l), :] + ((east + west) + (north + south))

    def lateral_edges(it):
        for l in range(depth):
            one = slice(l, l + 1)
            for side, x in enumerate(ends_x):
                row = slice(l * width_x + x, l * width_x + x + 1)
                rhs[row, :] += coef_x[side, one, :] * row_recv[it, side, 0, one, :]
        for side, y in enumerate(ends_y):
            tile = y - y % LANES
            terms = coef_y[side] * col_recv[it, side]
            for l in range(depth):
                for n in range(parts):
                    term = pltpu.roll(terms, (y - n * PACK - l) % LANES, 1)
                    rows = slice(l * width_x + n * ROWS, l * width_x + (n + 1) * ROWS)
                    rhs[rows, tile : tile + LANES] += jnp.where(lane == y - tile, term, 0.0)

    def edge_coefficients():
        for side in range(2):
            coef_x[side] = 0.5 * (row_send[0, side, 1] + row_recv[0, side, 1])
            coef_y[side] = pltpu.roll(
                0.5 * (col_send[0, side] + col_recv[0, side]), LANES - depth, 1
            )

    def chunk_loop(body):
        chunks = width_x // ROWS
        together = math.gcd(chunks, 8)

        def step(c, carry):
            for k in range(together):
                body(pl.multiple_of((c * together + k) * ROWS, ROWS))
            return carry

        lax.fori_loop(0, chunks // together, step, 0)

    def whole(ref, rows):
        return jnp.concatenate([ref[n, rows, :] for n in range(halves)], axis=1)

    def rows_of(i, at):
        return pl.ds(pl.multiple_of(i * width_x + at, ROWS), ROWS)

    def own_face(at):
        below = lower[pl.ds(at, ROWS), :]
        corner = whole(inv, rows_of(phi * depth + phi, at))
        return jnp.where(upper_group, corner * below - below, 0.0)

    def interior_face(it):
        def body(at):
            total = own_face(at)
            for j in range(depth):
                total = total + whole(inv, rows_of(phi * depth + j, at)) * rhs[rows_of(j, at), :]
            x_send[it, pl.ds(at, ROWS), :] = total

        chunk_loop(body)

    def solve_all():
        def body(at):
            terms = [rhs[rows_of(j, at), :] for j in range(depth)]
            for i in range(depth):
                total = whole(inv, rows_of(i * depth, at)) * terms[0]
                for j in range(1, depth):
                    total = total + whole(inv, rows_of(i * depth + j, at)) * terms[j]
                for n in range(halves):
                    solved[n, rows_of(i, at), :] = total[:, n * LANES : (n + 1) * LANES]

        chunk_loop(body)

    def inner_face(it, at):
        mine = whole(solved, rows_of(phi, at)) + own_face(at)
        return x_recv[it, pl.ds(at, ROWS), :] + jnp.where(
            upper_group, whole(kappa, pl.ds(at, ROWS)) * mine - mine, 0.0
        )

    def interior_data(it):
        def body(at):
            data = inner_face(it, at)
            lower[pl.ds(at, ROWS), :] = data
            for n in range(halves if it == 0 else 0):
                lower_at[n, pl.ds(at, ROWS), :] = data[:, n * LANES : (n + 1) * LANES]

        chunk_loop(body)

    def add_edges(ref, rows, columns):
        for x, row in zip(ends_x, rows):
            ref[x : x + 1, :] += row
        for y, column in zip(ends_y, columns):
            tile = y - y % LANES
            column = as_column(column)
            ref[:, tile : tile + LANES] += jnp.where(lane_x == y - tile, column, 0.0)

    to_smem.wait()
    start_load.wait()
    for load in line_loads(other_blocks, rest_sem.at[1]):
        load.start()
    for n in range(halves):
        slabs[n] = start_at[:, n * LANES : (n + 1) * LANES]
    at_own = gather([(slabs, 0, width_x, depth)], slots)[0]
    own[depth : 2 * depth, :] = at_own
    share, index_sums = binned(
        [jnp.sum(index * at_own, axis=0, keepdims=True), jnp.sum(index, axis=0, keepdims=True)]
    )
    well_send0[...] = jnp.concatenate([share + rate_row, index_sums], axis=1)
    clear_halos(0)
    clear_halos(1)
    rock_loaded.wait()
    stage_halos(0)
    loads[6].wait()
    lines_loaded(face_block, rest_sem.at[0]).wait()
    for n in range(halves):
        face_lines[n] = inv[n, face_block, :]
    own[3 * depth : 4 * depth, :] = gather([(face_lines, 0, width_x, depth)], slots)[0]
    pl.semaphore_wait(barrier, len(peers))
    on_sides(lambda side: halo_copy(0, side).start())
    slot_copy.start()
    for dl, step in peers:
        well_copy(0, dl, step).start()

    @pl.when(me_l == 1)
    def _():
        kappa_copy.start()
        kappa[...] = jnp.zeros(kappa.shape, F32)

    face_coefficients()
    lateral_sum(start_at)
    interior_face(0)
    x_copy(0).start()

    for side, x in enumerate(ends_x):
        for j in range(depth):
            gain_x[side, j : j + 1, :] = whole(inv, pl.ds((phi * depth + j) * width_x + x, 1))
    for side, y in enumerate(ends_y):
        n = y // LANES
        face = packed_columns(
            [(inv.at[n], pl.multiple_of((phi * depth + j) * width_x, width_x)) for j in range(depth)],
            y - n * LANES,
        )
        gain_y[side] = jnp.where((lane & (PACK - 1)) < depth, face, 0.0)
    lines_loaded(other_blocks, rest_sem.at[1]).wait()

    def gather_lines(columns):
        found = gather([(inv, j * width_x, block, depth) for j in columns], 16)
        for j, value in zip(columns, found):
            lines[j] = value

    gather_lines(range(depth - 2))
    edge_tile[...] = jnp.zeros(edge_tile.shape, F32)
    on_sides(lambda side: halo_copy(0, side, True).wait_recv())
    edge_coefficients()
    for side in range(2):
        gain_x[side] = gain_x[side] * coef_x[side]
        edge = jnp.sum(gain_x[side] * row_recv[0, side, 0], axis=0, keepdims=True)
        for n in range(halves):
            edge_tile[side * halves + n : side * halves + n + 1, :] = edge[:, n * LANES : (n + 1) * LANES]
    sums = column_sums([gain_y[side] * coef_y[side] * col_recv[0, side] for side in range(2)])
    for side in range(2):
        gain_y[side] = gain_y[side] * coef_y[side]
        row = 2 * halves + side
        edge_tile[row : row + 1, 0:width_x] = sums[side]
    edge_pack().start()
    gather_lines(range(depth - 2, depth))
    lateral_edges(0)
    solve_all()
    on_sides(lambda side: gain_copy(side).start())

    half = LANES // 2
    slot_copy.wait_recv()
    both = own[0 : 3 * depth, :] + pltpu.roll(par[0 : 3 * depth, :], half, 1)
    index2, at2 = both[0:depth], both[depth : 2 * depth]
    column_row, wells_row = both[2 * depth : 2 * depth + 1], both[2 * depth + 1 : 2 * depth + 2]
    wells_at = jnp.broadcast_to(wells_row, (8, LANES)).astype(jnp.int32)
    column_col = as_column(column_row)
    same = jnp.where(column_col == column_row, 1.0, 0.0).astype(BF16)

    def x_of(column):
        return jnp.floor((column + 0.5) * (1.0 / width_y))

    y_col = column_col - x_of(column_col) * width_y
    hot_y = jnp.where(
        lax.broadcasted_iota(jnp.int32, (LANES, width_y), 1).astype(F32) == y_col, 1.0, 0.0
    ).astype(BF16)
    hot_y = jnp.concatenate([hot_y, hot_y], axis=0)
    in_x = lax.broadcasted_iota(jnp.int32, (width_x, LANES), 0).astype(F32) == x_of(column_row)
    lower_half = lane < half
    x_row = x_of(column_row)
    y_row = column_row - x_row * width_y
    x_all, y_all = (jnp.broadcast_to(v, (8, LANES)).astype(jnp.int32) for v in (x_row, y_row))
    edge_lanes = jnp.where(sub < 2 * halves, y_all & (LANES - 1), x_all)
    edge_spots = jnp.zeros((8, LANES), jnp.int32)
    for side, x in enumerate(ends_x):
        for n in range(halves):
            here = (x_all == x) & (y_all >= n * LANES) & (y_all < (n + 1) * LANES)
            edge_spots = jnp.where((sub == side * halves + n) & here, 1, edge_spots)
    for side, y in enumerate(ends_y):
        edge_spots = jnp.where((sub == 2 * halves + side) & (y_all == y), 1, edge_spots)
    edge_spots = edge_spots > 0
    face_par = pltpu.roll(par[3 * depth : 4 * depth, :], half, 1)

    def well_totals(it):
        send, recv = ((well_send0, well_recv0), (well_send1, well_recv1))[it]
        all_wells(it).wait_recv()
        mine, other = send[...], recv[tiles - 1]
        for step in range(1, tiles):
            mine, other = mine + recv[step - 1], other + recv[tiles + step - 1]
        return mine, other

    def flows(mine, other, at_slots):
        def at_wells(row):
            return jnp.take_along_axis(
                jnp.broadcast_to(row, (8, LANES)), wells_at, axis=1, mode="promise_in_bounds"
            )

        hole = jnp.where(lower_half, at_wells(mine), at_wells(other))
        return index2 * (hole - at_slots)

    def responses(flow):
        change = jnp.zeros((depth, LANES), F32)
        for j in range(depth):
            change = change + lines[j] * flow[j : j + 1, :]
        out = jnp.sum(jnp.where(sub == phi, change, 0.0), axis=0, keepdims=True)
        theirs = jnp.sum(face_par * flow, axis=0, keepdims=True)
        return change, out, theirs

    def spread_out(change, data):
        order = [depth] + list(range(depth))
        for first in range(0, depth + 1, 3):
            some = order[first : first + 3]
            rows = slice(first * width_x, (first + len(some)) * width_x)
            for n, i in enumerate(some):
                row = change[i : i + 1, :] if i < depth else data
                left[sheet(first + n), :] = jnp.concatenate(
                    [jnp.where(in_x, part, 0.0).astype(BF16) for part in split(row, 2)], axis=1
                )
            spread[rows, :] = jnp.dot(left[rows, :], hot_y, preferred_element_type=F32)

    def update():
        lower[...] = lower[...] + spread[sheet(0), :]
        for i in range(depth):
            field[sheet(i), :] = (
                whole(solved, sheet(i))
                + spread[sheet(i + 1), :]
                + whole(inv, dyn_sheet(i * depth + phi)) * lower[...]
            )

    (solved_at,) = gather([(solved, 0, width_x, depth)], slots)
    mine, other = well_totals(0)
    index_mine, index_other = mine[:, wells:] + 1.0, other[:, wells:] + 1.0
    flow = flows(mine[:, :wells] / index_mine, other[:, :wells] / index_other, at2)
    change, out, theirs = responses(flow)
    stack = jnp.concatenate([change, jnp.where(sub == 0, out, theirs)], axis=0)
    pile = jnp.concatenate(split(stack, 3), axis=0).astype(BF16)
    summed = jnp.dot(pile, same, preferred_element_type=F32)
    summed = (summed[0:16] + summed[16:32]) + summed[32:48]
    inner_at = lines[phi]

    @pl.when(upper_group)
    def _():
        kappa_copy.wait_recv()

    x_copy(0).wait_recv()
    interior_data(0)
    data_at, kappa_at = gather([(lower_at, 0, 1, 1), (kappa, 0, 1, 1)], slots)
    kappa_gain = jnp.where(upper_group & lower_half[0:1], kappa_at - 1.0, 0.0)
    data = kappa_gain * out + theirs
    at_own = (solved_at + summed[0:8]) + inner_at * (
        data_at + (kappa_gain * summed[8:9] + summed[9:10])
    )
    edge_pack().wait_recv()
    edges = edge_tile_in[...]
    at_own = at_own + inner_at * jnp.sum(
        jnp.where(
            edge_spots,
            jnp.take_along_axis(edges, edge_lanes, axis=1, mode="promise_in_bounds"),
            0.0,
        ),
        axis=0,
        keepdims=True,
    )
    (share,) = binned([jnp.sum(index * at_own, axis=0, keepdims=True)])
    well_send1[...] = share + rate_row
    for dl, step in peers:
        well_copy(1, dl, step).start()
    at_send[...] = at_own
    at_copy.start()
    spread_out(change, data)
    add_edges(
        lower,
        [
            jnp.concatenate([edges[side * halves + n : side * halves + n + 1] for n in range(halves)], axis=1)
            for side in range(2)
        ],
        [edges[2 * halves + side : 2 * halves + side + 1, 0:width_x] for side in range(2)],
    )
    update()

    stage_halos(1)
    on_sides(lambda side: halo_copy(1, side).start())
    lateral_sum(field)
    interior_face(1)
    x_copy(1).start()
    on_sides(lambda side: gain_copy(side, True).wait_recv())
    for side in range(2):
        edge = jnp.sum(gain_xr[side] * row_send[1, side, 0], axis=0, keepdims=True)
        for n in range(halves):
            edge_send[side, n : n + 1, :] = edge[:, n * LANES : (n + 1) * LANES]
    sums = column_sums([gain_yr[side] * col_send[1, side] for side in range(2)])
    for side in range(2):
        edge_send[2 + side, 0:1, 0:width_x] = sums[side]
    on_sides(lambda side: edge_copy(side).start())
    on_sides(lambda side: halo_copy(1, side, True).wait_recv())
    lateral_edges(1)
    solve_all()
    at_copy.wait_recv()
    at2 = jnp.where(lower_half, at_own, pltpu.roll(at_recv[...], half, 1))
    mine, other = well_totals(1)
    flow = flows(mine / index_mine, other / index_other, at2)
    flow_out[...] = flow[:, 0:slots]
    change, out, theirs = responses(flow)
    spread_out(change, kappa_gain * out + theirs)
    x_copy(1).wait_recv()
    on_sides(lambda side: edge_copy(side, True).wait_recv())
    add_edges(
        x_recv.at[1],
        [
            jnp.concatenate([edge_recv[side, n : n + 1, :] for n in range(halves)], axis=1)
            for side in range(2)
        ],
        [edge_recv[2 + side, 0:1, 0:width_x] for side in range(2)],
    )
    interior_data(1)
    update()

    def sent(sem, buffers):
        rows = sum(math.prod(b.shape) for b in buffers) // LANES
        span = solved.at[0, 0:rows, :]
        remote(span, span, sem, sem, partner).wait_send()

    def side_sent(side):
        if side < 2:
            pieces = [row_send.at[0, 0], row_send.at[0, 0, 0], gain_x.at[0], edge_send.at[0]]
        else:
            pieces = [col_send.at[0, 0], col_send.at[0, 0], gain_y.at[0], edge_send.at[0]]
        sent(side_ssem.at[side], pieces)

    for it in range(ITERS):
        all_wells(it).wait_send()
    on_sides(side_sent)
    sent(part_ssem, [own, edge_tile, at_send, x_send])

    @pl.when(me_l == 1)
    def _():
        kappa_copy.wait_send()


def fused_shards(arrays, dims):
    (
        pressure, source, perm_x, perm_y, line_inverse, robin_below,
        tile_count, perf_owner, perf_well, perf_column, perf_index, well_rate,
    ) = arrays
    groups, n_gx, n_gy = dims
    depth, width_x, width_y = pressure.shape
    tiles = n_gx * n_gy
    slots = perf_well.shape[1]
    own_wells = well_rate.shape[1]
    wells = tiles * own_wells
    sheet = (width_x, width_y)
    stack = (depth * width_x, width_y)
    halves = width_y // LANES
    HBM = pl.BlockSpec(memory_space=pltpu.HBM)
    VMEM = pl.BlockSpec(memory_space=pltpu.VMEM)
    anywhere = pl.BlockSpec(memory_space=pl.ANY)
    dma = pltpu.SemaphoreType.DMA
    i32 = jnp.int32

    def vmem(*shape):
        return pltpu.VMEM(shape, F32)

    call = pl.pallas_call(
        functools.partial(fused, (groups, n_gx, n_gy, depth)),
        out_shape=(jax.ShapeDtypeStruct(stack, F32), jax.ShapeDtypeStruct((depth, slots), F32)),
        in_specs=[HBM] * 12,
        out_specs=(VMEM, VMEM),
        scratch_shapes=[
            vmem(*stack),
            vmem(3, *stack),
            vmem(halves, depth * depth * width_x, LANES),
            vmem(*sheet),
            pltpu.SMEM((1, slots), i32),
            pltpu.VMEM((1, 1), i32),
            pltpu.VMEM((1, slots), i32),
            pltpu.VMEM((1, slots), i32),
            pltpu.VMEM((1, slots), i32),
            vmem(depth, slots),
            vmem(1, own_wells),
            vmem(halves, depth * width_x, LANES),
            vmem(halves, depth * width_x, LANES),
            vmem(halves, width_x, LANES),
            vmem(*stack),
            vmem(halves, depth * width_x, LANES),
            vmem((depth + 1) * width_x, width_y),
            pltpu.VMEM(((depth + 1) * width_x, 2 * LANES), BF16),
            vmem(4 * depth, LANES),
            vmem(4 * depth, LANES),
            vmem(depth, depth, LANES),
            vmem(depth, LANES),
            vmem(depth, LANES),
            vmem(2, depth, width_y),
            vmem(2, ROWS, LANES),
            vmem(1, 2 * wells),
            vmem(groups * tiles - 1, 1, 2 * wells),
            vmem(1, wells),
            vmem(groups * tiles - 1, 1, wells),
            vmem(ITERS, 2, 2, depth, width_y),
            vmem(ITERS, 2, 2, depth, width_y),
            vmem(ITERS, 2, ROWS, LANES),
            vmem(ITERS, 2, ROWS, LANES),
            vmem(2, depth, width_y),
            vmem(2, ROWS, LANES),
            vmem(2, depth, width_y),
            vmem(2, ROWS, LANES),
            vmem(4, depth, LANES),
            vmem(4, depth, LANES),
            vmem(depth, LANES),
            vmem(depth, LANES),
            vmem(ITERS, *sheet),
            vmem(ITERS, *sheet),
            vmem(halves, width_x, LANES),
            dma,
            dma((9,)),
            dma((2,)),
            dma((ITERS,)),
            dma((ITERS,)),
            dma((4,)),
            dma((ITERS, 4)),
            dma((4,)),
            dma((5,)),
            dma,
            dma((ITERS,)),
            dma,
            dma((3,)),
        ],
        compiler_params=pltpu.CompilerParams(
            collective_id=0, has_side_effects=True, vmem_limit_bytes=LIMIT
        ),
        name="window",
    )
    operands = (
        pressure.reshape(stack),
        source.reshape(stack),
        perm_x.reshape(stack),
        perm_y.reshape(stack),
        line_inverse.reshape(depth * depth * width_x, width_y),
        robin_below[0],
        tile_count,
        perf_owner[:, :, 0],
        perf_well,
        perf_column,
        perf_index[0].T,
        well_rate,
    )
    field, flow = call(
        *[x if x.size == 1 else pltpu.with_memory_space_constraint(x, pltpu.HBM) for x in operands]
    )
    field, flow = pl.pallas_call(
        keep,
        out_shape=(
            jax.ShapeDtypeStruct(field.shape, F32),
            jax.ShapeDtypeStruct(flow.shape, F32),
        ),
        in_specs=[anywhere] * 2,
        out_specs=(HBM, HBM),
        scratch_shapes=[dma((2,))],
        compiler_params=pltpu.CompilerParams(vmem_limit_bytes=1 << 20),
        name="keep",
    )(field, flow)
    return field.reshape(pressure.shape), flow.T[None]


def shards(
    pressure,
    source,
    perm_x,
    perm_y,
    line_inverse,
    robin_below,
    tile_count,
    perf_owner,
    perf_well,
    perf_column,
    perf_index,
    well_rate,
):
    depth, width_x, width_y = pressure.shape
    groups, n_gx, n_gy = (lax.axis_size(a) for a in ("layer", "gx", "gy"))
    tiles = n_gx * n_gy
    slots = perf_well.shape[1]
    own_wells = well_rate.shape[1]
    wells = tiles * own_wells
    powers = all(n == 1 << (n.bit_length() - 1) for n in (n_gx, n_gy))
    if (
        groups == 2
        and depth == 8
        and wells == LANES
        and slots <= LANES // 2
        and slots % 16 == 0
        and width_x % ROWS == 0
        and width_x // ROWS * PACK <= LANES
        and width_y % LANES == 0
        and 2 * (width_y // LANES) + 2 <= depth
        and powers
    ):
        arrays = (
            pressure, source, perm_x, perm_y, line_inverse, robin_below,
            tile_count, perf_owner, perf_well, perf_column, perf_index, well_rate,
        )
        return fused_shards(arrays, (groups, n_gx, n_gy))
    sheet = (width_x, width_y)
    coefs = 1 if groups == 2 else 3
    HBM = pl.BlockSpec(memory_space=pltpu.HBM)
    anywhere = pl.BlockSpec(memory_space=pl.ANY)
    dma = pltpu.SemaphoreType.DMA
    i32 = jnp.int32
    call = pl.pallas_call(
        functools.partial(kernel, (groups, n_gx, n_gy)),
        out_shape=(
            jax.ShapeDtypeStruct(pressure.shape, F32),
            jax.ShapeDtypeStruct((depth, slots), F32),
        ),
        in_specs=[HBM] * 12,
        out_specs=(anywhere, anywhere),
        scratch_shapes=[
            pltpu.VMEM(pressure.shape, F32),
            pltpu.VMEM(pressure.shape, F32),
            pltpu.VMEM(pressure.shape, F32),
            pltpu.VMEM(pressure.shape, F32),
            pltpu.VMEM((depth, depth) + sheet, F32),
            pltpu.VMEM(sheet, F32),
            pltpu.VMEM((1, 1), i32),
            pltpu.VMEM((1, slots), i32),
            pltpu.VMEM((1, slots), i32),
            pltpu.VMEM((1, slots), i32),
            pltpu.VMEM((depth, slots), F32),
            pltpu.VMEM((1, own_wells), F32),
            pltpu.VMEM(sheet, F32),
            pltpu.VMEM(pressure.shape, F32),
            pltpu.VMEM(pressure.shape, F32),
            pltpu.VMEM((depth, slots), F32),
            pltpu.VMEM((depth, width_y), F32),
            pltpu.VMEM((width_x, 128), F32),
            pltpu.VMEM((1, 2 * wells), F32),
            pltpu.VMEM((tiles, 1, 2 * wells), F32),
            pltpu.VMEM((1, wells), F32),
            pltpu.VMEM((tiles, 1, wells), F32),
            pltpu.VMEM((ITERS, 2, 2, depth, width_y), F32),
            pltpu.VMEM((ITERS, 2, 2, depth, width_y), F32),
            pltpu.VMEM((ITERS, 2, width_x, 128), F32),
            pltpu.VMEM((ITERS, 2, width_x, 128), F32),
            pltpu.VMEM((groups, coefs) + sheet, F32),
            pltpu.VMEM((ITERS,) + sheet, F32),
            pltpu.VMEM((ITERS, groups) + sheet, F32),
            pltpu.VMEM((ITERS,) + sheet, F32),
            pltpu.VMEM((ITERS, groups) + sheet, F32),
            pltpu.VMEM(sheet, F32),
            pltpu.VMEM((groups, 1, slots), i32),
            pltpu.VMEM((ITERS, 2, slots), F32),
            pltpu.VMEM((ITERS, groups, 2, slots), F32),
            dma((12,)),
            dma((2,)),
            dma((ITERS, tiles)),
            dma((ITERS, tiles)),
            dma((ITERS, 4)),
            dma((ITERS, 4)),
            dma((groups, coefs)),
            dma((groups, coefs)),
            dma((ITERS, groups)),
            dma((ITERS, groups)),
            dma((ITERS, groups)),
            dma((ITERS, groups)),
            dma((groups,)),
            dma((groups,)),
            dma((ITERS, groups)),
            dma((ITERS, groups)),
        ],
        compiler_params=pltpu.CompilerParams(collective_id=0, has_side_effects=True, vmem_limit_bytes=LIMIT),
        name="window",
    )
    operands = (
        pressure,
        source,
        perm_x,
        perm_y,
        line_inverse[0],
        robin_below[0],
        tile_count,
        perf_owner[:, :, 0],
        perf_well,
        perf_column,
        perf_index[0].T,
        well_rate,
    )
    field, flow = call(
        *[x if x.size == 1 else pltpu.with_memory_space_constraint(x, pltpu.HBM) for x in operands]
    )
    field, flow = pl.pallas_call(
        keep,
        out_shape=(
            jax.ShapeDtypeStruct(field.shape, F32),
            jax.ShapeDtypeStruct(flow.shape, F32),
        ),
        in_specs=[anywhere] * 2,
        out_specs=(HBM, HBM),
        scratch_shapes=[dma((2,))],
        compiler_params=pltpu.CompilerParams(vmem_limit_bytes=1 << 20),
        name="keep",
    )(field, flow)
    return field, flow.T[None]


def solution(mesh):
    placed = (
        P("layer", "gx", "gy"),
        P("layer", "gx", "gy"),
        P("layer", "gx", "gy"),
        P("layer", "gx", "gy"),
        P("layer", None, None, "gx", "gy"),
        P("layer", "gx", "gy"),
        P("layer", ("gx", "gy")),
        P("layer", ("gx", "gy"), None),
        P("layer", ("gx", "gy")),
        P("layer", ("gx", "gy")),
        P("layer", ("gx", "gy"), None),
        P("layer", ("gx", "gy")),
    )
    return jax.shard_map(
        shards,
        mesh=mesh,
        in_specs=placed,
        out_specs=(P("layer", "gx", "gy"), P("layer", ("gx", "gy"), None)),
        check_vma=False,
    )
```
